32 devices in a mesh: grp: 8 (over z, y), ctx: 2 (over x), wsh: 2 (over core).
Axes of the slice: x: 2, y: 2, z: 4, core: 2. Of those that a mesh axis runs over, the one named last changes fastest.
Arguments:
- tokens: bfloat16 [16, 1024, 768], P(('grp', 'wsh'), 'ctx'), may hold values from -6 to 6
- lengths: int32 [16], P(('grp', 'wsh')), may hold values from 256 to 1024, as said below
- query_weight: bfloat16 [768, 768], P('wsh'), may hold values from -0.21875 to 0.21875
- key_weight: bfloat16 [768, 768], P('wsh'), may hold values from -0.21875 to 0.21875
- value_weight: bfloat16 [768, 768], P('wsh'), may hold values from -0.21875 to 0.21875
- output_weight: bfloat16 [768, 768], P('wsh'), may hold values from -3.5 to 3.5
- gate_weight: bfloat16 [768, 2048], P('wsh'), may hold values from -0.21875 to 0.21875
- up_weight: bfloat16 [768, 2048], P('wsh'), may hold values from -0.21875 to 0.21875
- down_weight: bfloat16 [2048, 768], P('wsh'), may hold values from -0.125 to 0.125
- attn_gain: bfloat16 [768], P('wsh'), may hold values from 0.5 to 1.5
- ffn_gain: bfloat16 [768], P('wsh'), may hold values from 0.5 to 1.5
- out_grad: bfloat16 [16, 1024, 768], P(('grp', 'wsh'), 'ctx'), may hold values from -6 to 6
Outputs:
- output: bfloat16 [16, 1024, 768], P(('grp', 'wsh'), 'ctx')
- input_grad: bfloat16 [16, 1024, 768], P(('grp', 'wsh'), 'ctx')
- query_grad: float32 [768, 768], P('wsh')
- key_grad: float32 [768, 768], P('wsh')
- value_grad: float32 [768, 768], P('wsh')
- output_weight_grad: float32 [768, 768], P('wsh')
- gate_grad: float32 [768, 2048], P('wsh')
- up_grad: float32 [768, 2048], P('wsh')
- down_grad: float32 [2048, 768], P('wsh')
- attn_gain_grad: float32 [768], P('wsh')
- ffn_gain_grad: float32 [768], P('wsh')
The draws below stay inside these ranges and needn't reach their ends.
Inputs may be any that keep to these rules, and one draw needn't show every extreme that they name: `lengths`: valid positions of each sequence; in every draw some sequence has exactly 1024 and some other exactly 256.
All inputs are finite; a program needn't handle non-finite values.
Results may differ from the reference program's by a relative error of at most 0.02.
Values may be sent and summed in bfloat16 or wider, within the bound.
No kernel may reach another device: no remote copies, remote signals or barrier semaphores. Data moves between devices by JAX's collectives and lax.ppermute only.
A program may use at most 320 MiB of HBM per device.

```python
import jax
import jax.numpy as jnp
from jax import lax

D = 768
HEADS = 12
HEAD_DIM = 64
FF = 2048
LEN = 1024
SEQS = 16


def draw_lengths(key, part):
    split_keys = jax.random.split(key, 3)
    sampled = jax.random.randint(split_keys[0], (SEQS,), LEN // 4, LEN + 1)
    full_place = jax.random.randint(split_keys[1], (), 0, SEQS)
    short_place = (full_place + 1 + jax.random.randint(split_keys[2], (), 0, SEQS - 1)) % SEQS
    places = jnp.arange(SEQS)
    sampled = jnp.where(places == full_place, LEN, sampled)
    sampled = jnp.where(places == short_place, LEN // 4, sampled)
    return sampled.astype(jnp.int32)


def levels(own_key, shape, pieces, least, top_value):
    def one(axis_at, parts):
        steps = jax.random.uniform(jax.random.fold_in(jax.random.fold_in(own_key, 6), axis_at), (parts,), jnp.float32, least / len(pieces), top_value / len(pieces))
        return jnp.repeat(jnp.exp(steps), shape[axis_at] // parts).reshape((-1,) + (1,) * (len(shape) - axis_at - 1))

    loudness = one(*pieces[0])
    for cut in pieces[1:]:
        loudness = loudness * one(*cut)
    return loudness


def scatter_about(own_key, extent, deviation, limit, cuts=(), held_as=jnp.bfloat16):
    level = levels(own_key, extent, cuts, -0.22, 0.18) if cuts else 1.0
    values = jax.random.normal(own_key, extent, jnp.float32) * deviation * level
    return jnp.minimum(jnp.maximum(values, -limit), limit).astype(held_as)


def setup_inputs(seed: int = 0) -> dict:
    keys = jax.random.split(jax.random.key(seed), 13)
    tokens = scatter_about(keys[0], (SEQS, LEN, D), 1.0, 6.0, ((0, 16), (1, 2)))
    lengths = draw_lengths(jax.random.fold_in(keys[12], 71), 0)
    query_weight = scatter_about(keys[2], (D, D), D ** -0.5, 0.21875, ((0, 2),))
    key_weight = scatter_about(keys[3], (D, D), D ** -0.5, 0.21875, ((0, 2),))
    value_weight = scatter_about(keys[4], (D, D), D ** -0.5, 0.21875, ((0, 2),))
    output_weight = scatter_about(keys[5], (D, D), (max(1, 4 * D // LEN)) ** -0.5, 3.5, ((0, 2),))
    gate_weight = scatter_about(keys[6], (D, FF), D ** -0.5, 0.21875, ((0, 2),))
    up_weight = scatter_about(keys[7], (D, FF), D ** -0.5, 0.21875, ((0, 2),))
    down_weight = scatter_about(keys[8], (FF, D), FF ** -0.5, 0.125, ((0, 2),))
    attn_gain = jnp.clip(1.0 + 0.1 * jax.random.normal(keys[9], (D,), jnp.float32), 0.5, 1.5).astype(jnp.bfloat16)
    ffn_gain = jnp.clip(1.0 + 0.1 * jax.random.normal(keys[10], (D,), jnp.float32), 0.5, 1.5).astype(jnp.bfloat16)
    out_grad = scatter_about(keys[11], (SEQS, LEN, D), 1.0, 6.0, ((0, 16), (1, 2)))
    return {"tokens": tokens, "lengths": lengths, "query_weight": query_weight, "key_weight": key_weight, "value_weight": value_weight, "output_weight": output_weight, "gate_weight": gate_weight, "up_weight": up_weight, "down_weight": down_weight, "attn_gain": attn_gain, "ffn_gain": ffn_gain, "out_grad": out_grad}


@jax.custom_vjp
def low(v):
    return lax.optimization_barrier(v.astype(jnp.bfloat16)).astype(jnp.float32)

@jax.custom_vjp
def low_back(v):
    return v

def low_keep(v):
    return (low(v), None)

def low_pass(kept, grad):
    return (grad,)

def back_keep(v):
    return (v, None)

def back_low(kept, grad):
    return (low(grad),)
low.defvjp(low_keep, low_pass)
low_back.defvjp(back_keep, back_low)
epsilon = 1e-06
floor_score = -1e+30

def rms_norm(values, gain_vec):
    return values * lax.rsqrt(lax.optimization_barrier(jnp.mean(values * values, axis=-1, keepdims=True)) + epsilon) * gain_vec

def matmul(left, right):
    return jnp.dot(left, right, precision=lax.Precision.HIGHEST)

def block_forward(row_input, key_live, query_weight, key_weight, value_weight, output_weight, gate_weight, up_weight, down_weight, attn_gain, ffn_gain):
    normed_attn = low(rms_norm(row_input, attn_gain))
    query_rows = low_back(low(matmul(normed_attn, query_weight)))
    key_rows = low_back(low(matmul(normed_attn, key_weight)))
    value_rows = low_back(low(matmul(normed_attn, value_weight)))
    factor = HEAD_DIM ** (-0.5)
    key_heads = key_rows.reshape(LEN, HEADS, HEAD_DIM)
    value_heads = value_rows.reshape(LEN, HEADS, HEAD_DIM)
    block_rows = min(512, LEN)
    query_blocks = query_rows.reshape(LEN // block_rows, block_rows, HEADS, HEAD_DIM)

    def attend(query_block):
        scores = jnp.einsum('qhd,khd->hqk', query_block, key_heads, precision=lax.Precision.HIGHEST) * factor
        scores = low_back(scores)
        scores = jnp.where(key_live[None, None, :], scores, floor_score)
        row_max = lax.optimization_barrier(jnp.max(scores, axis=-1, keepdims=True))
        log_total = row_max + jnp.log(lax.optimization_barrier(jnp.sum(jnp.exp(scores - row_max), axis=-1, keepdims=True)))
        weights = low(jnp.exp(scores - log_total))
        return jnp.einsum('hqk,khd->qhd', weights, value_heads, precision=lax.Precision.HIGHEST)
    attended = lax.map(jax.checkpoint(attend), query_blocks).reshape(LEN, D)
    attended = low_back(low(attended))
    middle = row_input + low_back(matmul(attended, output_weight))
    normed_ffn = low(rms_norm(middle, ffn_gain))
    gate_rows = low_back(matmul(normed_ffn, gate_weight))
    up_rows = low_back(matmul(normed_ffn, up_weight))
    hidden = low(jax.nn.gelu(gate_rows, approximate=True) * up_rows)
    return middle + low_back(matmul(hidden, down_weight))

def reference(tokens, lengths, query_weight, key_weight, value_weight, output_weight, gate_weight, up_weight, down_weight, attn_gain, ffn_gain, out_grad):
    params = tuple((matrix.astype(jnp.float32) for matrix in (query_weight, key_weight, value_weight, output_weight, gate_weight, up_weight, down_weight, attn_gain, ffn_gain)))
    positions = jnp.arange(LEN, dtype=jnp.int32)

    def per_sequence(totals, inputs):
        row_input, length, cotangent = inputs
        key_live = positions < length

        def forward(row_value, weight_tuple):
            return block_forward(row_value, key_live, *weight_tuple)
        result, pullback = jax.vjp(forward, row_input.astype(jnp.float32), params)
        grad_rows, grad_params = pullback(cotangent.astype(jnp.float32) * key_live[:, None].astype(jnp.float32))
        totals = tuple((running_sum + new_grad for running_sum, new_grad in zip(totals, grad_params)))
        return (totals, (result.astype(jnp.bfloat16), grad_rows.astype(jnp.bfloat16)))
    start_totals = tuple((jnp.zeros(matrix.shape, jnp.float32) for matrix in params))
    totals, (outputs, input_grads) = lax.scan(per_sequence, start_totals, (tokens, lengths, out_grad))
    return (outputs, input_grads, totals[0], totals[1], totals[2], totals[3], totals[4], totals[5], totals[6], totals[7], totals[8])
```

```python
import functools

import jax
import jax.numpy as jnp
from jax import lax
from jax.experimental import pallas as pl
from jax.experimental.pallas import tpu as pltpu
from jax.sharding import PartitionSpec as P

D = 768
HEAD_DIM = 64
PAIR = 2 * HEAD_DIM
EPSILON = 1e-06
DEAD = -1e30
VMEM = 60 << 20

F32 = jnp.float32
BF = jnp.bfloat16
NN = (((1,), (0,)), ((), ()))
NT = (((1,), (1,)), ((), ()))
SMEM = pl.BlockSpec(memory_space=pltpu.SMEM)


def mm(left, right, dims):
    return lax.dot_general(left, right, dims, preferred_element_type=F32)


def whole(shape):
    return pl.BlockSpec(shape, lambda j: (0,) * len(shape))


def call(kernel, grid, in_specs, out_specs, out_shape, flops, moved, name, scratch=()):
    return pl.pallas_call(
        kernel,
        grid=grid,
        in_specs=in_specs,
        out_specs=out_specs,
        out_shape=out_shape,
        scratch_shapes=list(scratch),
        compiler_params=pltpu.CompilerParams(vmem_limit_bytes=VMEM),
        cost_estimate=pl.CostEstimate(flops=flops, bytes_accessed=moved, transcendentals=0),
        name=name,
    )


def shape(dims, dtype):
    return jax.ShapeDtypeStruct(dims, dtype)


def rms_scale(values):
    return lax.rsqrt(jnp.mean(values * values, axis=-1, keepdims=True) + EPSILON)


def stack(core, own, other):
    return jnp.concatenate(
        [jnp.where(core == 0, own, other), jnp.where(core == 0, other, own)], axis=0
    )


def gain_row(core, own, other, index):
    own = own[index : index + 1, :].astype(F32)
    other = other[index : index + 1, :].astype(F32)
    return jnp.concatenate(
        [jnp.where(core == 0, own, other), jnp.where(core == 0, other, own)], axis=1
    )


def put_halves(core, value, own_ref, other_ref):
    half = value.shape[0] // 2
    low, high = value[:half], value[half:]
    own_ref[...] = jnp.where(core == 0, low, high).astype(own_ref.dtype)
    other_ref[...] = jnp.where(core == 0, high, low).astype(other_ref.dtype)


def project_kernel(count, core_ref, x_ref, gain_own, gain_other, *refs):
    core = core_ref[0]
    weights, outs, normed_ref = refs[: 2 * count], refs[2 * count :], refs[2 * count]

    @pl.when(pl.program_id(0) == 0)
    def _():
        x = x_ref[...].astype(F32)
        gain = gain_row(core, gain_own[...], gain_other[...], 0)
        normed_ref[...] = (x * rms_scale(x) * gain).astype(BF)

    normed = normed_ref[...]
    for i in range(count):
        weight = stack(core, weights[2 * i][...], weights[2 * i + 1][...])
        outs[1 + i][...] = mm(normed, weight, NN).astype(BF)


def project(core, x, gains, weights):
    rows, count, cols = x.shape[0], len(weights), 256
    weight_spec = pl.BlockSpec((D // 2, cols), lambda j: (0, j))
    out_spec = pl.BlockSpec((rows, cols), lambda j: (0, j))
    return call(
        functools.partial(project_kernel, count),
        (D // cols,),
        [SMEM, whole((rows, D))] + [whole((2, D // 2))] * 2 + [weight_spec] * (2 * count),
        [whole((rows, D))] + [out_spec] * count,
        [shape((rows, D), BF)] * (1 + count),
        2 * rows * D * D * count,
        2 * D * (rows * (2 + count) + D * count),
        "project",
    )(core, x, *gains, *(part for pair in weights for part in pair))


def split3(value):
    high = value.astype(BF).astype(F32)
    rest = value - high
    mid = rest.astype(BF).astype(F32)
    return high, mid, rest - mid


def key_extra(limits_ref, rows, blocks):
    lane = lax.broadcasted_iota(jnp.int32, (rows, PAIR), 1) % HEAD_DIM
    row = lax.broadcasted_iota(jnp.int32, (rows, PAIR), 0)
    pieces = []
    for block in range(blocks):
        bias = jnp.where(row < limits_ref[block], 0.0, DEAD)
        pieces.append(
            jnp.where(lane < 3, 1.0, jnp.where(lane == 3, bias, 0.0)).astype(BF)
        )
    return jnp.concatenate(pieces, axis=0) if blocks > 1 else pieces[0]


def joined(refs):
    return jnp.concatenate([ref[...] for ref in refs], axis=0) if len(refs) > 1 else refs[0][...]


def place3(lane, base, parts, into):
    for i in (2, 1, 0):
        into = jnp.where(lane == base + i, parts[i], into)
    return into


def attend_kernel(blocks, limits_ref, q_ref, *refs):
    keys, values = joined(refs[:blocks]), joined(refs[blocks : 2 * blocks])
    wide_ref, low_ref, extra_ref = refs[2 * blocks :]
    rows, total = q_ref.shape[0], keys.shape[0]
    queries = q_ref[...] * jnp.asarray(HEAD_DIM**-0.5, BF)
    extra = key_extra(limits_ref, rows, blocks)
    lane = lax.broadcasted_iota(jnp.int32, (rows, PAIR), 1)
    key_lane = lax.broadcasted_iota(jnp.int32, (total, PAIR), 1)
    log_lanes = jnp.where(lane % HEAD_DIM == 3, 1.0, 0.0)
    bias_lane = log_lanes.astype(BF)
    heads = []
    for head in range(2):
        mine = lane // HEAD_DIM == head
        key_mine = key_lane // HEAD_DIM == head
        scores = mm(
            jnp.where(mine, queries, bias_lane), jnp.where(key_mine, keys, extra), NT
        )
        top = jnp.max(scores, axis=-1, keepdims=True)
        weights = jnp.exp(scores - top)
        sums = jnp.sum(weights, axis=-1, keepdims=True)
        heads.append(mm(weights.astype(BF), values, NN) / sums)
        log_lanes = place3(
            lane, HEAD_DIM * (1 - head), split3(-(top + jnp.log(sums))), log_lanes
        )
    attended = jnp.where(lane < HEAD_DIM, heads[0], heads[1])
    wide_ref[...] = attended
    low_ref[...] = attended.astype(BF)
    extra_ref[...] = log_lanes.astype(BF)


def attend(limits, queries, keys, values):
    rows, blocks = queries.shape[0], len(keys)
    spec = pl.BlockSpec((rows, PAIR), lambda j: (0, j))
    return call(
        functools.partial(attend_kernel, blocks),
        (D // PAIR,),
        [SMEM] + [spec] * (1 + 2 * blocks),
        [spec] * 3,
        [shape((rows, D), F32), shape((rows, D), BF), shape((rows, D), BF)],
        16 * rows * rows * blocks * D,
        2 * rows * D * (5 + 2 * blocks),
        "attend",
    )(limits, queries, *keys, *values)


def attend_back_kernel(blocks, core_ref, limits_ref, q_ref, *refs):
    keys, values = joined(refs[:blocks]), joined(refs[blocks : 2 * blocks])
    dmb_ref, wide_ref, low_ref, extra_ref, wo_own, wo_other = refs[2 * blocks : 2 * blocks + 6]
    outs = refs[2 * blocks + 6 :]
    dq_ref, dk_refs, dv_refs = outs[0], outs[1 : 1 + blocks], outs[1 + blocks : 1 + 2 * blocks]
    out_own, out_other = outs[1 + 2 * blocks :]
    step = pl.program_id(0)
    count = pl.num_programs(0) // 2
    rows, total = q_ref.shape[0], keys.shape[0]
    scale = jnp.asarray(HEAD_DIM**-0.5, BF)
    queries = q_ref[...] * scale
    dmb = dmb_ref[...]
    weight = jnp.where(step < count, wo_other[...], wo_own[...])
    grads = mm(dmb, weight, NT).astype(BF)
    out_term = mm(low_ref[...].T, dmb, NN).astype(BF)

    @pl.when(step < count)
    def _():
        out_other[...] = out_term

    @pl.when(step >= count)
    def _():
        out_own[...] = out_term

    log_lanes = extra_ref[...]
    extra = key_extra(limits_ref, rows, blocks)
    lane = lax.broadcasted_iota(jnp.int32, (rows, PAIR), 1)
    key_lane = lax.broadcasted_iota(jnp.int32, (total, PAIR), 1)
    product = grads.astype(F32) * wide_ref[...]
    delta_lanes = jnp.zeros((rows, PAIR), F32)
    for head in range(2):
        mine = lane // HEAD_DIM == head
        delta = -jnp.sum(jnp.where(mine, product, 0.0), axis=-1, keepdims=True)
        delta_lanes = place3(lane, HEAD_DIM * (1 - head), split3(delta), delta_lanes)
    delta_lanes = delta_lanes.astype(BF)
    keys_turned = (keys * scale).T
    none = jnp.zeros((rows, PAIR), BF)
    dk = dv = 0.0
    dqs = []
    for head in range(2):
        mine = lane // HEAD_DIM == head
        key_mine = key_lane // HEAD_DIM == head
        probs = jnp.exp(
            mm(jnp.where(key_mine, keys, extra), jnp.where(mine, queries, log_lanes), NT)
        )
        shifted = mm(
            jnp.where(key_mine, values, extra), jnp.where(mine, grads, delta_lanes), NT
        )
        dscores = (probs * shifted).astype(BF)
        dv = dv + mm(probs.astype(BF), jnp.where(mine, grads, none), NN)
        dk = dk + mm(dscores, jnp.where(mine, queries, none), NN)
        dqs.append(mm(keys_turned[head * HEAD_DIM : (head + 1) * HEAD_DIM], dscores, NN))
    dq_ref[...] = jnp.concatenate(dqs, axis=0).T.astype(BF)
    for block in range(blocks):
        dk_refs[block][...] = dk[block * rows : (block + 1) * rows].astype(BF)
        dv_refs[block][...] = dv[block * rows : (block + 1) * rows].astype(BF)


def attend_back(core, limits, queries, keys, values, dmb, wide, low, extra, out_weight):
    rows, blocks = queries.shape[0], len(keys)
    pairs = D // PAIR
    half = pairs // 2

    def at(j, core_ref):
        return (j + half * (1 - core_ref[0])) % pairs

    spec = pl.BlockSpec((rows, PAIR), lambda j, core_ref, limits_ref: (0, at(j, core_ref)))
    full = pl.BlockSpec((rows, D), lambda j, core_ref, limits_ref: (0, 0))
    other_spec = pl.BlockSpec(
        (PAIR, D), lambda j, core_ref, limits_ref: (jnp.minimum(j, half - 1), 0)
    )
    own_spec = pl.BlockSpec(
        (PAIR, D), lambda j, core_ref, limits_ref: (jnp.maximum(j - half, 0), 0)
    )
    results = pl.pallas_call(
        functools.partial(attend_back_kernel, blocks),
        grid_spec=pltpu.PrefetchScalarGridSpec(
            num_scalar_prefetch=2,
            grid=(pairs,),
            in_specs=[spec] * (1 + 2 * blocks) + [full, spec, spec, spec, own_spec, other_spec],
            out_specs=[spec] * (1 + 2 * blocks) + [own_spec, other_spec],
        ),
        out_shape=[shape((rows, D), BF)] * (1 + 2 * blocks) + [shape((D // 2, D), BF)] * 2,
        compiler_params=pltpu.CompilerParams(vmem_limit_bytes=VMEM),
        cost_estimate=pl.CostEstimate(
            flops=40 * rows * rows * blocks * D,
            bytes_accessed=2 * rows * D * (8 + 4 * blocks),
            transcendentals=0,
        ),
        name="attend_back",
    )(core, limits, queries, *keys, *values, dmb, wide, low, extra, *out_weight)
    return results[0], results[1 : 1 + blocks], results[1 + blocks : 1 + 2 * blocks], results[1 + 2 * blocks :]


CURVE = 0.7978845608028654
CUBIC = 0.044715


def ffn_part(core, step, h2, h2_turned, dyb, weights, grads, acc_out, acc_back):
    gate_own, gate_other, up_own, up_other, down_own, down_other = weights
    dgate_own, dgate_other, dup_own, dup_other, ddown_own, ddown_other = grads
    gate_weight = stack(core, gate_own[...], gate_other[...])
    up_weight = stack(core, up_own[...], up_other[...])
    down_weight = jnp.where(step == core, down_own[...], down_other[...])
    gate = mm(h2, gate_weight, NN)
    up = mm(h2, up_weight, NN)
    dn = mm(dyb, down_weight, NT)
    square = gate * gate
    bent = jnp.tanh(CURVE * gate * (1.0 + CUBIC * square))
    rise = 0.5 * (1.0 + bent)
    bulge = gate * rise
    slope = rise + 0.5 * gate * (1.0 - bent * bent) * (CURVE * (1.0 + 3.0 * CUBIC * square))
    hidden = (bulge * up).astype(BF)
    dgate = (dn * up * slope).astype(BF)
    dup = (dn * bulge).astype(BF)
    ddown = mm(hidden.T, dyb, NN).astype(BF)

    @pl.when(step == core)
    def _():
        ddown_own[...] = ddown

    @pl.when(step != core)
    def _():
        ddown_other[...] = ddown

    put_halves(core, mm(h2_turned, dgate, NN), dgate_own, dgate_other)
    put_halves(core, mm(h2_turned, dup, NN), dup_own, dup_other)
    acc_out[...] += mm(hidden, down_weight, NN)
    acc_back[...] += mm(dgate, gate_weight, NT) + mm(dup, up_weight, NT)


def live_grad(limits_ref, grad_ref):
    rows = grad_ref.shape[0]
    live = lax.broadcasted_iota(jnp.int32, (rows, D), 0) < limits_ref[0]
    return jnp.where(live, grad_ref[...].astype(F32), 0.0)


def ffn_first_kernel(core_ref, limits_ref, x_ref, a_ref, wo_own, wo_other, gain_own, gain_other, grad_ref, *refs):
    core, step = core_ref[0], pl.program_id(0)
    weights, outs = refs[:6], refs[6:]
    m_ref, h2_ref, acc_out, acc_back = outs[:4]
    grads, (turned,) = outs[4:10], outs[10:]

    @pl.when(step == 0)
    def _():
        weight = stack(core, wo_own[...], wo_other[...])
        m = x_ref[...].astype(F32) + mm(a_ref[...], weight, NN)
        gain = gain_row(core, gain_own[...], gain_other[...], 1)
        m_ref[...] = m
        h2 = (m * rms_scale(m) * gain).astype(BF)
        h2_ref[...] = h2
        turned[...] = h2.T
        acc_out[...] = jnp.zeros_like(acc_out)
        acc_back[...] = jnp.zeros_like(acc_back)

    dyb = live_grad(limits_ref, grad_ref).astype(BF)
    ffn_part(core, step, h2_ref[...], turned[...], dyb, weights, grads, acc_out, acc_back)


def ffn_last_kernel(core_ref, limits_ref, m_ref, h2_ref, gain_own, gain_other, grad_ref, out_in, back_in, *refs):
    core, step = core_ref[0], pl.program_id(0)
    weights, outs = refs[:6], refs[6:]
    output_ref, dm_ref, dmb_ref, dgain_ref = outs[:4]
    grads, (turned, acc_out, acc_back) = outs[4:10], outs[10:]

    @pl.when(step == 0)
    def _():
        turned[...] = h2_ref[...].T
        acc_out[...] = out_in[...]
        acc_back[...] = back_in[...]

    dy = live_grad(limits_ref, grad_ref)
    ffn_part(core, step, h2_ref[...], turned[...], dy.astype(BF), weights, grads, acc_out, acc_back)

    @pl.when(step == pl.num_programs(0) - 1)
    def _():
        m = m_ref[...]
        output_ref[...] = (m + acc_out[...]).astype(BF)
        gain = gain_row(core, gain_own[...], gain_other[...], 1)
        scale = rms_scale(m)
        back = acc_back[...]
        dgain_ref[...] = jnp.sum(back * m * scale, axis=0, keepdims=True)
        scaled = back * gain
        dm = dy + scale * scaled - m * (scale * scale * scale) * jnp.mean(
            scaled * m, axis=-1, keepdims=True
        )
        dm_ref[...] = dm
        dmb_ref[...] = dm.astype(BF)


def ffn_specs(part, hidden):
    wide = hidden // 4
    gate_spec = pl.BlockSpec((D // 2, wide), lambda j: (0, part + 2 * j))
    down_spec = pl.BlockSpec((wide, D), lambda j: (part, 0))
    grad_spec = pl.BlockSpec((D // 2, wide), lambda j: (0, j))
    weight_specs = [gate_spec] * 4 + [down_spec] * 2
    grad_specs = [grad_spec] * 4 + [whole((wide, D))] * 2
    grad_shapes = [shape((D // 2, 2 * wide), BF)] * 4 + [shape((wide, D), BF)] * 2
    return weight_specs, grad_specs, grad_shapes


def ffn_first(core, limits, x, attended, out_weight, gains, grad, weights):
    rows, hidden = x.shape[0], weights[0].shape[1]
    weight_specs, grad_specs, grad_shapes = ffn_specs(0, hidden)
    row = whole((rows, D))
    return call(
        ffn_first_kernel,
        (2,),
        [SMEM, SMEM, row, row] + [whole((D // 2, D))] * 2 + [whole((2, D // 2))] * 2 + [row] + weight_specs,
        [row] * 4 + grad_specs,
        [shape((rows, D), F32), shape((rows, D), BF), shape((rows, D), F32), shape((rows, D), F32)] + grad_shapes,
        9 * rows * D * hidden,
        2 * D * (rows * 10 + hidden * 3),
        "ffn_first",
        [pltpu.VMEM((D, rows), BF)],
    )(core, limits, x, attended, *out_weight, *gains, grad, *weights)


def ffn_last(core, limits, m, h2, gains, grad, acc_out, acc_back, weights):
    rows, hidden = h2.shape[0], weights[0].shape[1]
    weight_specs, grad_specs, grad_shapes = ffn_specs(1, hidden)
    row = whole((rows, D))
    return call(
        ffn_last_kernel,
        (2,),
        [SMEM, SMEM, row, row] + [whole((2, D // 2))] * 2 + [row] * 3 + weight_specs,
        [row] * 3 + [whole((1, D))] + grad_specs,
        [shape((rows, D), BF), shape((rows, D), F32), shape((rows, D), BF), shape((1, D), F32)] + grad_shapes,
        9 * rows * D * hidden,
        2 * D * (rows * 10 + hidden * 3),
        "ffn_last",
        [pltpu.VMEM((D, rows), BF), pltpu.VMEM((rows, D), F32), pltpu.VMEM((rows, D), F32)],
    )(core, limits, m, h2, *gains, grad, acc_out, acc_back, *weights)


def project_grads_kernel(blocks, core_ref, dq_ref, *refs):
    core = core_ref[0]
    dks, dvs, normed = refs[:blocks], refs[blocks : 2 * blocks], refs[2 * blocks : 3 * blocks]
    outs, turned = refs[3 * blocks : 3 * blocks + 6], refs[3 * blocks + 6]

    @pl.when(pl.program_id(0) == 0)
    def _():
        for block in range(blocks):
            rows = normed[block].shape[0]
            turned[:, block * rows : (block + 1) * rows] = normed[block][...].T

    rows = dq_ref.shape[0]
    put_halves(core, mm(turned[:, :rows], dq_ref[...], NN), outs[0], outs[1])
    put_halves(core, mm(turned[...], joined(dks), NN), outs[2], outs[3])
    put_halves(core, mm(turned[...], joined(dvs), NN), outs[4], outs[5])


def project_grads(core, dq, dks, dvs, normed):
    rows, blocks, cols = dq.shape[0], len(dks), 256
    spec = pl.BlockSpec((rows, cols), lambda j: (0, j))
    out_spec = pl.BlockSpec((D // 2, cols), lambda j: (0, j))
    return call(
        functools.partial(project_grads_kernel, blocks),
        (D // cols,),
        [SMEM] + [spec] * (1 + 2 * blocks) + [whole((rows, D))] * blocks,
        [out_spec] * 6,
        [shape((D // 2, D), BF)] * 6,
        2 * rows * D * D * (1 + 2 * blocks),
        2 * D * (rows * (1 + 3 * blocks) + D * 3),
        "project_grads",
        [pltpu.VMEM((D, rows * blocks), BF)],
    )(core, dq, *dks, *dvs, *normed)


def project_back_kernel(blocks, core_ref, gain_own, gain_other, dq_ref, *refs):
    core, block = core_ref[0], pl.program_id(0)
    dks, dvs, xs = refs[:blocks], refs[blocks : 2 * blocks], refs[2 * blocks : 3 * blocks]
    weights = refs[3 * blocks : 3 * blocks + 6]
    outs, dgain_ref = refs[3 * blocks + 6 : 4 * blocks + 6], refs[4 * blocks + 6]
    query = stack(core, weights[0][...], weights[1][...])
    key = stack(core, weights[2][...], weights[3][...])
    value = stack(core, weights[4][...], weights[5][...])
    total = jnp.zeros((1, D), F32)
    for block in range(blocks):
        back = mm(dks[block][...], key, NT) + mm(dvs[block][...], value, NT)
        if block == 0:
            back = back + mm(dq_ref[...], query, NT)
        x = xs[block][...].astype(F32)
        total = total + jnp.sum(back * x * rms_scale(x), axis=0, keepdims=True)
        outs[block][...] = back.astype(outs[block].dtype)
    dgain_ref[...] = total


def project_back(core, gains, dq, dks, dvs, xs, weights):
    rows, blocks = dq.shape[0], len(dks)
    row = whole((rows, D))
    return call(
        functools.partial(project_back_kernel, blocks),
        (1,),
        [SMEM] + [whole((2, D // 2))] * 2 + [row] * (1 + 3 * blocks) + [whole((D // 2, D))] * 6,
        [row] * blocks + [whole((1, D))],
        [shape((rows, D), F32)] + [shape((rows, D), BF)] * (blocks - 1) + [shape((1, D), F32)],
        2 * rows * D * D * (1 + 2 * blocks),
        2 * D * (rows * (1 + 4 * blocks) + D * 3),
        "project_back",
    )(core, *gains, dq, *dks, *dvs, *xs, *(part for pair in weights for part in pair))


def input_grad_kernel(core_ref, gain_own, gain_other, x_ref, dm_ref, own_ref, *refs):
    x = x_ref[...].astype(F32)
    scale = rms_scale(x)
    back = own_ref[...]
    for ref in refs[:-1]:
        back = back + ref[...].astype(F32)
    scaled = back * gain_row(core_ref[0], gain_own[...], gain_other[...], 0)
    refs[-1][...] = (
        dm_ref[...]
        + scale * scaled
        - x * (scale * scale * scale) * jnp.mean(scaled * x, axis=-1, keepdims=True)
    ).astype(BF)


def input_grad_of(core, gains, x, dm, own, received):
    rows, cut = x.shape[0], 4
    spec = pl.BlockSpec((rows // cut, D), lambda j: (j, 0))
    return call(
        input_grad_kernel,
        (cut,),
        [SMEM] + [whole((2, D // 2))] * 2 + [spec] * (3 + len(received)),
        spec,
        shape((rows, D), BF),
        rows * D,
        2 * D * rows * 8,
        "input_grad",
    )(core, *gains, x, dm, own, *received)


def swap(value, axis, mask):
    count = lax.axis_size(axis)
    return lax.ppermute(value, axis, [(i, i ^ mask) for i in range(count)])


def bits_of(axis):
    index, out, mask = lax.axis_index(axis), [], 1
    while mask < lax.axis_size(axis):
        out.append(((index // mask) % 2, axis, mask))
        mask *= 2
    return out


def add(left, right):
    return (left.astype(F32) + right.astype(F32)).astype(BF)


def sum_over_chips(arrays):
    ctx, grp = bits_of("ctx"), bits_of("grp")
    cube = [ctx[0], grp[0], grp[1]]
    rest = grp[2:] + ctx[1:]
    orders = [[cube[(i + s) % 3] for i in range(3)] for s in range(len(arrays))]
    current = list(arrays)
    for stage in range(3):
        kept, sent = [], []
        for value, order in zip(current, orders):
            bit, axis, mask = order[stage]
            half = value.shape[0] // 2
            kept.append(lax.dynamic_slice_in_dim(value, bit * half, half, 0))
            sent.append(swap(lax.dynamic_slice_in_dim(value, (1 - bit) * half, half, 0), axis, mask))
        current = [add(k, s) for k, s in zip(kept, sent)]
    for _, axis, mask in rest:
        current = [add(c, swap(c, axis, mask)) for c in current]
    for stage in (2, 1, 0):
        received = [swap(v, o[stage][1], o[stage][2]) for v, o in zip(current, orders)]
        current = [
            jnp.concatenate(
                [jnp.where(o[stage][0] == 0, v, r), jnp.where(o[stage][0] == 0, r, v)], axis=0
            )
            for v, r, o in zip(current, received, orders)
        ]
    return current


def on_device(
    tokens,
    lengths,
    query_weight,
    key_weight,
    value_weight,
    output_weight,
    gate_weight,
    up_weight,
    down_weight,
    attn_gain,
    ffn_gain,
    out_grad,
):
    blocks = lax.axis_size("ctx")
    x, grad = tokens[0], out_grad[0]
    rows = x.shape[0]
    place = lax.axis_index("ctx")
    core = lax.axis_index("wsh").astype(jnp.int32)[None]
    limits = jnp.clip(
        lengths[0] - rows * jnp.stack([place ^ r for r in range(blocks)]).astype(jnp.int32), 0, rows
    )

    def both(own):
        return (own, swap(own, "wsh", 1))

    gains = both(jnp.stack([attn_gain, ffn_gain]))
    xs = [x] + [swap(x, "ctx", r) for r in range(1, blocks)]
    wq, wk, wv, wo = both(query_weight), both(key_weight), both(value_weight), both(output_weight)
    wg, wu, wd = both(gate_weight), both(up_weight), both(down_weight)

    h1, queries, key, value = project(core, x, gains, [wq, wk, wv])
    normed, keys, values = [h1], [key], [value]
    for peer in xs[1:]:
        h1, key, value = project(core, peer, gains, [wk, wv])
        normed.append(h1)
        keys.append(key)
        values.append(value)
    wide, low, extra = attend(limits, queries, keys, values)
    ffn_weights = (*wg, *wu, *wd)
    m, h2, acc_out, acc_back, *grads = ffn_first(
        core, limits, x, low, wo, gains, grad, ffn_weights
    )

    def over_cores(pairs):
        return [add(own, swap(other, "wsh", 1)) for own, other in pairs]

    def pairs_of(values):
        return list(zip(values[0::2], values[1::2]))

    first = sum_over_chips(over_cores(pairs_of(grads)))
    output, dm, dmb, dgain_ffn, *grads = ffn_last(
        core, limits, m, h2, gains, grad, acc_out, acc_back, ffn_weights
    )
    second = sum_over_chips(over_cores(pairs_of(grads)))
    dq, dks, dvs, out_terms = attend_back(
        core, limits, queries, keys, values, dmb, wide, low, extra, wo
    )
    grads = project_grads(core, dq, dks, dvs, normed)
    third = sum_over_chips(over_cores(pairs_of(grads) + [tuple(out_terms)]))
    *backs, dgain_attn = project_back(core, gains, dq, dks, dvs, xs, [wq, wk, wv])
    received = [swap(back, "ctx", r) for r, back in enumerate(backs) if r]
    input_grad = input_grad_of(core, gains, x, dm, backs[0], received)
    dgains = lax.psum(jnp.concatenate([dgain_attn, dgain_ffn], axis=0), ("grp", "ctx", "wsh"))
    dgains = lax.dynamic_slice_in_dim(dgains, core[0] * (D // 2), D // 2, 1)

    def spread(early, late):
        cut = early.shape[1] // 2
        return jnp.concatenate(
            [early[:, :cut], late[:, :cut], early[:, cut:], late[:, cut:]], axis=1
        ).astype(F32)

    return (
        output[None],
        input_grad[None],
        third[0].astype(F32),
        third[1].astype(F32),
        third[2].astype(F32),
        third[3].astype(F32),
        spread(first[0], second[0]),
        spread(first[1], second[1]),
        jnp.concatenate([first[2], second[2]], axis=0).astype(F32),
        dgains[0],
        dgains[1],
    )


def solution(mesh):
    rows, weights, vector = P(("grp", "wsh"), "ctx", None), P("wsh", None), P("wsh")
    in_specs = (rows, P(("grp", "wsh"))) + (weights,) * 7 + (vector,) * 2 + (rows,)
    out_specs = (rows,) * 2 + (weights,) * 7 + (vector,) * 2
    return jax.shard_map(
        on_device, mesh=mesh, in_specs=in_specs, out_specs=out_specs, check_vma=False
    )
```

```python
import functools

import jax
import jax.numpy as jnp
from jax import lax
from jax.experimental import pallas as pl
from jax.experimental.pallas import tpu as pltpu
from jax.sharding import PartitionSpec as P

D = 768
HEAD_DIM = 64
PAIR = 2 * HEAD_DIM
EPSILON = 1e-06
DEAD = -1e30

F32 = jnp.float32
BF = jnp.bfloat16
NN = (((1,), (0,)), ((), ()))
NT = (((1,), (1,)), ((), ()))
SMEM = pl.BlockSpec(memory_space=pltpu.SMEM)
LOCAL = pl.BlockSpec(memory_space=pltpu.VMEM)
FAR = pl.BlockSpec(memory_space=pltpu.HBM)


def mm(left, right, dims):
    return lax.dot_general(left, right, dims, preferred_element_type=F32)


class Load:
    def __init__(self, pieces, dims=None):
        self.pieces = pieces if isinstance(pieces, list) else [(pieces, None, None)]
        first = self.pieces[0][0]
        self.dims, self.dtype = dims or first.shape, first.dtype


class Choice(Load):
    def __init__(self, pair, holder, rows):
        self.pieces = [(pair[0], None, None), (pair[1], None, None)]
        self.dims, self.dtype = (rows.stop - rows.start, pair[0].shape[1]), pair[0].dtype
        self.holder, self.rows = holder, rows


class Store:
    def __init__(self, dims, dtype, columns=None):
        self.shape = shape(dims, dtype)
        self.columns = columns
        self.dims = dims if columns is None else (dims[0], columns.stop - columns.start)


AHEAD = 4
LONG, SHORT = 10**11, 10**10


class Arriving:
    def __init__(self, ref, starts, waits, queue):
        self.ref, self.starts, self.waits, self.queue = ref, starts, waits, queue
        self.shape, self.place = ref.shape, len(queue)
        queue.append(self)

    def begin(self):
        for start in self.starts:
            start()
        self.starts = []

    def ready(self):
        if self.waits:
            for value in self.queue[: self.place + 1 + AHEAD]:
                value.begin()
            for copy in self.waits:
                copy.wait()
            self.waits = []
        return self.ref

    def __getitem__(self, index):
        return self.ready()[index]


class Leaving:
    def __init__(self, ref, target, sem):
        self.ref, self.target, self.sem, self.started = ref, target, sem, False
        self.copy = pltpu.make_async_copy(ref, target, sem)
        self.shape = ref.shape

    def ready(self):
        return self.ref

    def send_lanes(self, here):
        pltpu.make_async_copy(self.ref.at[:, here], self.target.at[:, here], self.sem).start()
        self.started = True

    def __getitem__(self, index):
        return self.ref[index]

    def __setitem__(self, index, value):
        self.ref[index] = value

    def send(self):
        if not self.started:
            self.copy.start()
        self.started = True


def placed(ref, index):
    return ref if index is None else ref.at[index]


def call(body, inputs, outs, vmem, name, scratch=(), aliases=(), near=False):
    arrays, in_specs, loads, copies, plan = [], [], [], 0, []
    for value in inputs:
        if isinstance(value, Load):
            plan.append(len(loads))
            loads.append(value)
            arrays += [pltpu.with_memory_space_constraint(piece[0], pltpu.HBM) for piece in value.pieces]
            in_specs += [FAR] * len(value.pieces)
            copies += len(value.pieces)
        else:
            plan.append(None)
            pinned = near and value.dtype != jnp.int32
            arrays.append(pltpu.with_memory_space_constraint(value, pltpu.VMEM) if pinned else value)
            in_specs.append(SMEM if value.dtype == jnp.int32 else LOCAL)
    count = len(arrays)
    arrays += [pltpu.with_memory_space_constraint(value, pltpu.HBM) for value in aliases]
    in_specs += [FAR] * len(aliases)
    stores = [out for out in outs if isinstance(out, Store)]
    out_shape = [
        pltpu.HBM(out.shape.shape, out.shape.dtype)
        if isinstance(out, Store)
        else pltpu.VMEM(out.shape, out.dtype) if near else out
        for out in outs
    ]
    out_specs = [
        FAR if isinstance(out, Store) else LOCAL for out in outs
    ]
    own_scratch = [pltpu.VMEM(load.dims, load.dtype) for load in loads]
    own_scratch += [pltpu.VMEM(store.dims, store.shape.dtype) for store in stores]
    sems = [pltpu.SemaphoreType.DMA((copies + len(stores),))] if copies + len(stores) else []

    def kernel(*refs):
        ins, results = refs[:count], refs[len(arrays) : len(arrays) + len(outs)]
        rest = list(refs[len(arrays) + len(outs) :])
        homes, sem = rest[: len(own_scratch)], rest[len(own_scratch)] if sems else None
        extra = rest[len(own_scratch) + len(sems) :]
        given, queue, at, number = [], [], 0, 0
        for index in plan:
            if index is None:
                given.append(ins[at])
                at += 1
                continue
            load, home, starts, waits = loads[index], homes[index], [], []
            if isinstance(load, Choice):
                copies_of = [pltpu.make_async_copy(ins[at + i].at[load.rows, :], home, sem.at[number]) for i in (0, 1)]

                def start(copies_of=copies_of, holder=load.holder):
                    for i, copy in enumerate(copies_of):
                        pl.when((given[0][0] == holder) == (i == 0))(copy.start)

                starts, waits = [start], [copies_of[0]]
                at, number = at + 2, number + 2
            else:
                for _, source, target in load.pieces:
                    copy = pltpu.make_async_copy(
                        placed(ins[at], source and source(given[0])),
                        placed(home, target and target(given[0])),
                        sem.at[number],
                    )
                    starts.append(copy.start)
                    waits.append(copy)
                    at, number = at + 1, number + 1
            given.append(Arriving(home, starts, waits, queue))
        for value in queue[: 1 + AHEAD]:
            value.begin()
        leaving, made = [], []
        for out, result in zip(outs, results):
            if isinstance(out, Store):
                home = homes[len(loads) + len(leaving)]
                target = result if out.columns is None else result.at[:, out.columns]
                leaving.append(Leaving(home, target, sem.at[number]))
                made.append(leaving[-1])
                number += 1
            else:
                made.append(result)
        body(*given, *made, *extra)
        for value in queue:
            value.ready()
        for value in leaving:
            value.send()
        for value in leaving:
            value.copy.wait()

    results = [out.shape if isinstance(out, Store) else out for out in outs]
    moved = sum(value.size * value.dtype.itemsize for value in arrays + results)
    return pl.pallas_call(
        kernel,
        in_specs=in_specs,
        out_specs=out_specs,
        out_shape=out_shape,
        scratch_shapes=own_scratch + sems + list(scratch),
        input_output_aliases={count + i: i for i in range(len(aliases))},
        compiler_params=pltpu.CompilerParams(vmem_limit_bytes=vmem << 20),
        cost_estimate=pl.CostEstimate(flops=SHORT if near else LONG, bytes_accessed=moved, transcendentals=0),
        name=name,
    )(*arrays)


def joined_halves(pair, columns=slice(None)):
    half = pair[0].shape[0]
    pieces = []
    for array, mine in zip(pair, (True, False)):

        def into(core_ref, mine=mine):
            start = (core_ref[0] if mine else 1 - core_ref[0]) * half
            return (pl.ds(pl.multiple_of(start, half), half), slice(None))

        pieces.append((array, lambda core_ref: (slice(None), columns), into))
    start, stop, _ = columns.indices(pair[0].shape[1])
    return Load(pieces, (2 * half, stop - start))


def shape(dims, dtype):
    return jax.ShapeDtypeStruct(dims, dtype)


def rms_scale(values):
    return lax.rsqrt(jnp.mean(values * values, axis=-1, keepdims=True) + EPSILON)


def stack(core, own, other):
    return jnp.concatenate(
        [jnp.where(core == 0, own, other), jnp.where(core == 0, other, own)], axis=0
    )


def gain_row(core, own, other, index):
    own = own[index : index + 1, :].astype(F32)
    other = other[index : index + 1, :].astype(F32)
    return jnp.concatenate(
        [jnp.where(core == 0, own, other), jnp.where(core == 0, other, own)], axis=1
    )


def lanes(step, size):
    return pl.ds(pl.multiple_of(step * size, size), size)


def project_kernel(count, core_ref, gain_own, gain_other, x_ref, *refs):
    weights, outs = refs[:count], refs[count:]
    gain = gain_row(core_ref[0], gain_own[...], gain_other[...], 0)
    x = x_ref[...].astype(F32)
    outs[0][...] = (x * rms_scale(x) * gain).astype(BF)
    outs[0].send()
    normed = outs[0][...]
    for i in range(count):
        outs[1 + i][...] = mm(normed, weights[i][...], NN).astype(BF)
        outs[1 + i].send()


def project(core, x, gains, weights):
    count = len(weights)
    return call(
        functools.partial(project_kernel, count),
        [core, *gains, Load(x)] + [joined_halves(pair) for pair in weights],
        [Store(x.shape, BF) for _ in range(1 + count)],
        14 if x.shape[0] <= 512 else 48,
        "project",
    )


def split3(value):
    high = value.astype(BF).astype(F32)
    rest = value - high
    mid = rest.astype(BF).astype(F32)
    return high, mid, rest - mid


def key_extra(limit, rows):
    lane = lax.broadcasted_iota(jnp.int32, (rows, PAIR), 1) % HEAD_DIM
    row = lax.broadcasted_iota(jnp.int32, (rows, PAIR), 0)
    bias = jnp.where(row < limit, 0.0, DEAD)
    return jnp.where(lane < 3, 1.0, jnp.where(lane == 3, bias, 0.0)).astype(BF)


def block_of(step, rows):
    return pl.ds(pl.multiple_of(step * rows, rows), rows)


def place3(lane, base, parts, into):
    for i in (2, 1, 0):
        into = jnp.where(lane == base + i, parts[i], into)
    return into


def attend_block(limit, queries, bias_lane, keys, values, lane, earlier):
    rows = queries.shape[0]
    extra = key_extra(limit, rows)
    ones = jnp.ones((rows, PAIR), BF)
    results = []
    for head in range(2):
        mine = lane // HEAD_DIM == head
        scores = mm(jnp.where(mine, queries, bias_lane), jnp.where(mine, keys, extra), NT)
        top = jnp.max(scores, axis=-1, keepdims=True)
        if earlier is not None:
            top = jnp.maximum(top, earlier[head][1])
        weights = jnp.exp(scores - top).astype(BF)
        total = mm(weights, jnp.where(mine, values, ones), NN)
        if earlier is not None:
            total = total + earlier[head][0] * jnp.exp(earlier[head][1] - top)
        results.append((total, top))
    return results


def scaled_queries(q_ref, here):
    queries = q_ref[:, here] * jnp.asarray(HEAD_DIM**-0.5, BF)
    lane = lax.broadcasted_iota(jnp.int32, queries.shape, 1)
    return queries, jnp.where(lane % HEAD_DIM == 3, 1.0, 0.0).astype(BF), lane


def attend_own_kernel(limits_ref, q_ref, k_ref, v_ref, first_ref, second_ref, top_ref):
    top_ref[...] = jnp.zeros_like(top_ref.ref)
    for ref in (q_ref, k_ref, v_ref):
        ref.ready()

    @pl.loop(0, D // PAIR)
    def _(pair):
        here = lanes(pair, PAIR)
        queries, bias_lane, lane = scaled_queries(q_ref, here)
        heads = attend_block(limits_ref[0], queries, bias_lane, k_ref[:, here], v_ref[:, here], lane, None)
        first_ref[:, here], second_ref[:, here] = heads[0][0], heads[1][0]
        first_ref.send_lanes(here)
        second_ref.send_lanes(here)
        tops = top_ref[...]
        for head in range(2):
            tops = jnp.where(lane == 2 * pair + head, heads[head][1], tops)
        top_ref[...] = tops


def attend_own(limits, queries, keys, values):
    rows = queries.shape[0]
    return call(
        attend_own_kernel,
        [limits, Load(queries), Load(keys), Load(values)],
        [Store((rows, D), F32), Store((rows, D), F32), Store((rows, PAIR), F32)],
        16,
        "attend_own",
    )


def own_rows_kernel(core_ref, limits_ref, gain_own, gain_other, x_ref, wq, wk, wv, h1, q, k, v, *partial):
    project_kernel(3, core_ref, gain_own, gain_other, x_ref, wq, wk, wv, h1, q, k, v)
    attend_own_kernel(limits_ref, q, k, v, *partial)


def own_rows(core, limits, x, gains, weights):
    rows = x.shape[0]
    results = call(
        own_rows_kernel,
        [core, limits, *gains, Load(x)] + [joined_halves(pair) for pair in weights],
        [Store((rows, D), BF) for _ in range(4)]
        + [Store((rows, D), F32), Store((rows, D), F32), Store((rows, PAIR), F32)],
        22,
        "own_rows",
    )
    return results[:4], results[4:]


def attend_rest_kernel(limits_ref, q_ref, k_ref, v_ref, first_ref, second_ref, top_ref, wide_ref, low_ref, extra_ref):
    for ref in (q_ref, k_ref, v_ref, first_ref, second_ref, top_ref):
        ref.ready()
    rows = q_ref.shape[0]
    blocks = k_ref.shape[0] // rows

    @pl.loop(0, D // PAIR)
    def _(pair):
        here = lanes(pair, PAIR)
        queries, bias_lane, lane = scaled_queries(q_ref, here)
        tops = top_ref[...]
        heads = [
            (ref[:, here], jnp.sum(jnp.where(lane == 2 * pair + i, tops, 0.0), axis=-1, keepdims=True))
            for i, ref in enumerate((first_ref, second_ref))
        ]

        def more(block, heads):
            place = block_of(block, rows)
            return attend_block(
                limits_ref[1 + block], queries, bias_lane, k_ref[place, here], v_ref[place, here], lane, heads
            )

        heads = more(0, heads) if blocks == 1 else lax.fori_loop(0, blocks, more, heads)
        log_lanes = jnp.where(lane % HEAD_DIM == 3, 1.0, 0.0)
        outs = []
        for head, (total, top) in enumerate(heads):
            outs.append(total / pltpu.roll(total, HEAD_DIM, 1))
            log_lanes = place3(
                lane, HEAD_DIM * (1 - head), split3(-(top + jnp.log(total))), log_lanes
            )
        attended = jnp.where(lane < HEAD_DIM, outs[0], outs[1])
        wide_ref[:, here] = attended
        low_ref[:, here] = attended.astype(BF)
        extra_ref[:, here] = log_lanes.astype(BF)
        for ref in (wide_ref, low_ref, extra_ref):
            ref.send_lanes(here)


def attend_rest(limits, queries, keys, values, partial):
    rows = queries.shape[0]
    return call(
        attend_rest_kernel,
        [limits, Load(queries), Load(keys), Load(values)] + [Load(value) for value in partial],
        [Store((rows, D), F32), Store((rows, D), BF), Store((rows, D), BF)],
        18 if keys.shape[0] == rows else 40,
        "attend_rest",
    )


def attend_back_kernel(count, limits_ref, q_ref, dmb_ref, wo_ref, low_ref, wide_ref, extra_ref, *refs):
    inputs, outs = refs[:4], refs[4:]
    dq_ref, grad_refs, out_ref = outs[0], outs[1:5], outs[5]
    rows = q_ref.shape[0]
    scale = jnp.asarray(HEAD_DIM**-0.5, BF)
    lane = lax.broadcasted_iota(jnp.int32, (rows, PAIR), 1)
    none = jnp.zeros((rows, PAIR), BF)
    for ref in (q_ref, dmb_ref, low_ref, wide_ref, extra_ref, *inputs):
        ref.ready()

    @pl.loop(0, count)
    def _(pair):
        here = lanes(pair, PAIR)
        queries = q_ref[:, here] * scale
        dmb = dmb_ref[...]
        grads = mm(dmb, wo_ref[here, :], NT).astype(BF)
        out_ref[here, :] = mm(low_ref[:, here].T, dmb, NN).astype(BF)
        log_lanes = extra_ref[:, here]
        product = grads.astype(F32) * wide_ref[:, here]
        delta_lanes = jnp.zeros((rows, PAIR), F32)
        for head in range(2):
            mine = lane // HEAD_DIM == head
            delta = -jnp.sum(jnp.where(mine, product, 0.0), axis=-1, keepdims=True)
            delta_lanes = place3(lane, HEAD_DIM * (1 - head), split3(delta), delta_lanes)
        delta_lanes = delta_lanes.astype(BF)

        def over(limit, k_ref, v_ref, dk_ref, dv_ref, place):
            keys, values = k_ref[place, here], v_ref[place, here]
            extra = key_extra(limit, rows)
            keys_turned = (keys * scale).T
            dk = dv = 0.0
            dqs = []
            for head in range(2):
                mine = lane // HEAD_DIM == head
                probs = jnp.exp(
                    mm(jnp.where(mine, keys, extra), jnp.where(mine, queries, log_lanes), NT)
                )
                shifted = mm(
                    jnp.where(mine, values, extra), jnp.where(mine, grads, delta_lanes), NT
                )
                dscores = (probs * shifted).astype(BF)
                dv = dv + mm(probs.astype(BF), jnp.where(mine, grads, none), NN)
                dk = dk + mm(dscores, jnp.where(mine, queries, none), NN)
                dqs.append(mm(keys_turned[head * HEAD_DIM : (head + 1) * HEAD_DIM], dscores, NN))
            dk_ref[place, here] = dk.astype(BF)
            dv_ref[place, here] = dv.astype(BF)
            return jnp.concatenate(dqs, axis=0)

        k_own, k_rest, v_own, v_rest = inputs
        dk_own, dk_rest, dv_own, dv_rest = grad_refs
        dq = over(limits_ref[0], k_own, v_own, dk_own, dv_own, slice(None))
        blocks = k_rest.shape[0] // rows

        def more(block, dq):
            return dq + over(limits_ref[1 + block], k_rest, v_rest, dk_rest, dv_rest, block_of(block, rows))

        dq = more(0, dq) if blocks == 1 else lax.fori_loop(0, blocks, more, dq)
        dq_ref[:, here] = dq.T.astype(BF)
        for ref in (dq_ref, *grad_refs):
            ref.send_lanes(here)


def attend_back_inputs(queries, keys, values, dmb, wide, low, extra, out_weight, first, count):
    columns = slice(first * PAIR, (first + count) * PAIR)
    half = D // PAIR // 2

    def part(value):
        dims = (value.shape[0], columns.stop - columns.start)
        return Load([(value, lambda core_ref: (slice(None), columns), None)], dims)

    rows_of = [
        Choice(out_weight, pair // half, slice(pair % half * PAIR, (pair % half + 1) * PAIR))
        for pair in range(first, first + count)
    ]
    loads = [part(queries), Load(dmb)] + rows_of + [part(low), part(wide), part(extra)]
    return loads + [part(value) for value in (keys[0], values[0], keys[1], values[1])], columns


def attend_back_body(count, core_ref, limits_ref, refs, turned_wo):
    q_ref, dmb_ref, wo_refs, rest = refs[0], refs[1], refs[2 : 2 + count], refs[2 + count :]
    for i, ref in enumerate(wo_refs):
        turned_wo[i * PAIR : (i + 1) * PAIR, :] = ref[...]
    low_ref, wide_ref, extra_ref, k_own, v_own, k_rest, v_rest = rest[:7]
    attend_back_kernel(
        count, limits_ref, q_ref, dmb_ref, turned_wo, low_ref, wide_ref, extra_ref, k_own, k_rest, v_own, v_rest, *rest[7:]
    )


def attend_back(core, limits, queries, keys, values, dmb, wide, low, extra, out_weight, first, count, earlier):
    rows, rest = queries.shape[0], keys[1].shape[0]
    loads, columns = attend_back_inputs(queries, keys, values, dmb, wide, low, extra, out_weight, first, count)

    def body(core_ref, limits_ref, *refs):
        attend_back_body(count, core_ref, limits_ref, refs[:-1], refs[-1])

    return call(
        body,
        [core, limits] + loads,
        [Store((size, D), BF, columns) for size in (rows, rows, rest, rows, rest)]
        + [Store((columns.stop - columns.start, D), BF)],
        20 if rest == rows else 48,
        "attend_back",
        [pltpu.VMEM((count * PAIR, D), BF)],
        aliases=earlier,
    )


CURVE = 0.7978845608028654
CUBIC = 0.044715


def ffn_part(core, step, h2_ref, turned, dyb, dyb_turned, weights, own_ref, other_ref):
    wide, half = own_ref.shape[1] // 2, D // 2
    here = slice(step * wide, (step + 1) * wide)
    gate_weight, up_weight, down_weight = weights
    gate = mm(h2_ref[...], gate_weight[...], NN)
    up = mm(h2_ref[...], up_weight[...], NN)
    dn = mm(dyb[...], down_weight[...], NT)
    square = gate * gate
    bent = jnp.tanh(CURVE * gate * (1.0 + CUBIC * square))
    rise = 0.5 * (1.0 + bent)
    bulge = gate * rise
    slope = rise + 0.5 * gate * (1.0 - bent * bent) * (CURVE * (1.0 + 3.0 * CUBIC * square))
    hidden = (bulge * up).astype(BF)
    dgate = (dn * up * slope).astype(BF)
    dup = (dn * bulge).astype(BF)
    ddown = mm(dyb_turned[...], hidden, NN).astype(BF)

    @pl.when(step == core)
    def _():
        own_ref[2 * half :, :wide] = ddown[:half]
        own_ref[2 * half :, wide:] = ddown[half:]

    @pl.when(step != core)
    def _():
        other_ref[2 * half :, :wide] = ddown[:half]
        other_ref[2 * half :, wide:] = ddown[half:]

    dgate_term = mm(turned[...], dgate, NN).astype(BF)
    dup_term = mm(turned[...], dup, NN).astype(BF)
    for i, term in ((0, dgate_term), (1, dup_term)):
        place = slice(i * half, (i + 1) * half)
        own_ref[place, here] = jnp.where(core == 0, term[:half], term[half:])
        other_ref[place, here] = jnp.where(core == 0, term[half:], term[:half])
    back = mm(dgate, gate_weight[...], NT) + mm(dup, up_weight[...], NT)
    return mm(hidden, down_weight[...], NN), back


def live_grad(limits_ref, grad_ref):
    rows = grad_ref.shape[0]
    live = lax.broadcasted_iota(jnp.int32, (rows, D), 0) < limits_ref[0]
    return jnp.where(live, grad_ref[...].astype(F32), 0.0)


def ffn_first_kernel(core_ref, limits_ref, gain_own, gain_other, a_ref, wo_ref, x_ref, grad_ref, *refs):
    core = core_ref[0]
    weights, outs = refs[:6], refs[6:]
    m_ref, h2_ref, turned, dyb, dyb_turned, acc_out, acc_back, own_ref, other_ref = outs
    m = mm(a_ref[...], wo_ref[...], NN) + x_ref[...].astype(F32)
    gain = gain_row(core, gain_own[...], gain_other[...], 1)
    m_ref[...] = m
    m_ref.send()
    h2 = (m * rms_scale(m) * gain).astype(BF)
    h2_ref[...] = h2
    h2_ref.send()
    turned[...] = h2.T
    turned.send()
    low = live_grad(limits_ref, grad_ref).astype(BF)
    dyb[...] = low
    dyb.send()
    dyb_turned[...] = low.T
    dyb_turned.send()
    out, back = ffn_part(core, 0, h2_ref, turned, dyb, dyb_turned, weights[:3], own_ref, other_ref)
    acc_out[...], acc_back[...] = out, back
    out, back = ffn_part(core, 1, h2_ref, turned, dyb, dyb_turned, weights[3:], own_ref, other_ref)
    acc_out[...] += out
    acc_back[...] += back


def ffn_last_kernel(core_ref, limits_ref, gain_own, gain_other, h2_ref, *refs):
    core = core_ref[0]
    dyb, dyb_turned, turned, out_in, back_in, m_ref, grad_ref = refs[2], refs[4], refs[5], *refs[9:13]
    weights = (refs[0], refs[1], refs[3], *refs[6:9])
    output_ref, dm_ref, dmb_ref, own_ref, other_ref, acc_out, acc_back = refs[13:]
    out, back = ffn_part(core, 0, h2_ref, turned, dyb, dyb_turned, weights[:3], own_ref, other_ref)
    acc_out[...] = out_in[...] + out
    acc_back[...] = back_in[...] + back
    out, back = ffn_part(core, 1, h2_ref, turned, dyb, dyb_turned, weights[3:], own_ref, other_ref)
    m = m_ref[...]
    gain = gain_row(core, gain_own[...], gain_other[...], 1)
    scale = rms_scale(m)
    scaled = (acc_back[...] + back) * gain
    dm = live_grad(limits_ref, grad_ref) + scale * scaled - m * (scale * scale * scale) * jnp.mean(
        scaled * m, axis=-1, keepdims=True
    )
    dmb_ref[...] = dm.astype(BF)
    dmb_ref.send()
    dm_ref[...] = dm
    dm_ref.send()
    output_ref[...] = (m + acc_out[...] + out).astype(BF)


def middle_kernel(core_ref, limits_ref, gain_own, gain_other, x_rest, wk, wv, q, first, second, top, wo, x, grad, *refs):
    weights, outs = refs[:6], refs[6:]
    h1_rest, k_rest, v_rest, wide, low, extra = outs[:6]
    project_kernel(2, core_ref, gain_own, gain_other, x_rest, wk, wv, h1_rest, k_rest, v_rest)
    attend_rest_kernel(limits_ref, q, k_rest, v_rest, first, second, top, wide, low, extra)
    ffn_first_kernel(core_ref, limits_ref, gain_own, gain_other, low, wo, x, grad, *weights, *outs[6:])


def middle(core, limits, gains, x, x_rest, key_value, queries, partial, out_weight, grad, weights):
    rows, hidden = x.shape[0], weights[0][0].shape[1]
    low, turned, full = ((rows, D), BF), ((D, rows), BF), ((rows, D), F32)
    outs = [low, low, low, full, low, low, full, low, turned, low, turned, full, full]
    results = call(
        middle_kernel,
        [core, limits, *gains, Load(x_rest)]
        + [joined_halves(pair) for pair in key_value]
        + [Load(queries)]
        + [Load(value) for value in partial]
        + [joined_halves(out_weight), Load(x), Load(grad)]
        + ffn_weights_of(weights, 0),
        [Store(*dims) for dims in outs] + grad_shapes(hidden),
        46,
        "middle",
    )
    return results[:3], results[3:6], results[6:13], results[13], results[14]


def ffn_weights_of(weights, part):
    gate, up, down = weights
    wide = gate[0].shape[1] // 4
    rows = slice(part * wide, (part + 1) * wide)
    loads = []
    for step in range(2):
        columns = slice((part + 2 * step) * wide, (part + 2 * step + 1) * wide)
        loads += [joined_halves(pair, columns) for pair in (gate, up)]
        loads.append(Choice(down, step, rows))
    return loads


def grad_shapes(hidden):
    return [Store((3 * D // 2, hidden // 2), BF) for _ in range(2)]


def ffn_first(core, limits, x, attended, out_weight, gains, grad, weights):
    rows, hidden = x.shape[0], weights[0][0].shape[1]
    low, turned, full = ((rows, D), BF), ((D, rows), BF), ((rows, D), F32)
    return call(
        ffn_first_kernel,
        [core, limits, *gains, Load(attended), joined_halves(out_weight), Load(x), Load(grad)]
        + ffn_weights_of(weights, 0),
        [Store(*dims) for dims in (full, low, turned, low, turned, full, full)] + grad_shapes(hidden),
        34,
        "ffn_first",
    )


def ffn_last(core, limits, kept, gains, grad, weights):
    m, h2, turned, dyb, dyb_turned, acc_out, acc_back = kept
    rows, hidden = grad.shape[0], weights[0][0].shape[1]
    low, full = ((rows, D), BF), ((rows, D), F32)
    parts = ffn_weights_of(weights, 1)
    loads = [*parts[:2], Load(dyb), parts[2], Load(dyb_turned), Load(turned), *parts[3:]]
    loads += [Load(value) for value in (acc_out, acc_back, m, grad)]
    return call(
        ffn_last_kernel,
        [core, limits, *gains, Load(h2)] + loads,
        [Store(*low), Store(*full), Store(*low)] + grad_shapes(hidden),
        34,
        "ffn_last",
        [pltpu.VMEM((rows, D), F32)] * 2,
    )


def project_grads_kernel(core_ref, own_normed, dq_ref, rest_normed, dk_own, dk_rest, dv_own, dv_rest, *refs):
    core = core_ref[0]
    out_terms, (own_ref, other_ref) = refs[:-2], refs[-2:]
    half = D // 2

    def put(i, term):
        own_ref[i * half : (i + 1) * half, :] = jnp.where(core == 0, term[:half], term[half:])
        other_ref[i * half : (i + 1) * half, :] = jnp.where(core == 0, term[half:], term[:half])

    turned = own_normed[...].T
    put(0, mm(turned, dq_ref[...], NN).astype(BF))
    turned_rest = rest_normed[...].T
    put(1, (mm(turned, dk_own[...], NN) + mm(turned_rest, dk_rest[...], NN)).astype(BF))
    put(2, (mm(turned, dv_own[...], NN) + mm(turned_rest, dv_rest[...], NN)).astype(BF))
    put(3, jnp.concatenate([term[...] for term in out_terms], axis=0))


def project_grads(core, normed, dq, dks, dvs, out_terms):
    total = dks[0].shape[0] + dks[1].shape[0]
    arrays = (normed[0], dq, normed[1], *dks, *dvs, *out_terms)
    return call(
        project_grads_kernel,
        [core] + [Load(value) for value in arrays],
        [Store((2 * D, D), BF) for _ in range(2)],
        18 if total <= 1024 else 54,
        "project_grads",
    )


def last_piece(core, limits, queries, keys, values, dmb, wide, low, extra, out_weight, first, count, earlier, out_terms, normed):
    rows, rest = queries.shape[0], keys[1].shape[0]
    loads, columns = attend_back_inputs(queries, keys, values, dmb, wide, low, extra, out_weight, first, count)
    done = slice(0, columns.start)
    inputs = len(loads)

    def before(value):
        return Load([(value, lambda core_ref: (slice(None), done), None)], (value.shape[0], done.stop))

    more = [Load(normed[0]), before(earlier[0]), Load(normed[1])]
    more += [before(value) for value in earlier[1:]] + [Load(term) for term in out_terms]

    def body(core_ref, limits_ref, *refs):
        ins, given, outs, wo, out_term = refs[:inputs], refs[inputs : inputs + len(more)], refs[-9:-4], refs[-2], refs[-1]
        own_ref, other_ref = refs[-4:-2]
        attend_back_body(count, core_ref, limits_ref, (*ins, *outs, out_term), wo)

        def both_parts(left, right):
            return jnp.concatenate([left[...], right[...]], axis=1)

        merged = [both_parts(left, right) for left, right in zip((given[1], *given[3:7]), outs)]
        project_grads_kernel(
            core_ref, given[0], merged[0], given[2], *merged[1:], *given[7:], out_term, own_ref, other_ref
        )

    width = columns.stop - columns.start
    return call(
        body,
        [core, limits] + loads + more,
        [Store((size, width), BF) for size in (rows, rows, rest, rows, rest)] + [Store((2 * D, D), BF) for _ in range(2)],
        36,
        "last_piece",
        [pltpu.VMEM((count * PAIR, D), BF)] * 2,
    )


def project_back_kernel(core_ref, dk_rest, key, dv_rest, value, dq_ref, query, dk_own, dv_own, rest_ref, own_ref):
    rows = dq_ref.shape[0]
    for ref in (dk_rest, key, dv_rest, value):
        ref.ready()

    def rest(block, _):
        place = block_of(block, rows)
        back = mm(dk_rest[place, :], key[...], NT) + mm(dv_rest[place, :], value[...], NT)
        rest_ref[place, :] = back.astype(BF)
        return _

    blocks = dk_rest.shape[0] // rows
    rest(0, 0) if blocks == 1 else lax.fori_loop(0, blocks, rest, 0)
    rest_ref.send()
    own_ref[...] = (
        mm(dq_ref[...], query[...], NT) + mm(dk_own[...], key[...], NT) + mm(dv_own[...], value[...], NT)
    )


def project_back(core, dq, dks, dvs, weights):
    query, key, value = (joined_halves(pair) for pair in weights)
    total = dks[0][0].shape[0] + dks[1][0].shape[0]

    def side_by_side(parts):
        pieces, start = [], 0
        for i, part in enumerate(parts):
            width = D - start if i == len(parts) - 1 else D - parts[-1].shape[1]
            columns = slice(start, start + width)
            take = None if part.shape[1] == width else (lambda core_ref, columns=columns: (slice(None), columns))
            pieces.append((part, take, lambda core_ref, columns=columns: (slice(None), columns)))
            start += width
        return Load(pieces, (parts[0].shape[0], D))

    dq_load, (dk_own, dk_rest), (dv_own, dv_rest) = side_by_side(dq), map(side_by_side, dks), map(side_by_side, dvs)
    return call(
        project_back_kernel,
        [core, dk_rest, key, dv_rest, value, dq_load, query, dk_own, dv_own],
        [Store((total - dq[0].shape[0], D), BF), Store((dq[0].shape[0], D), F32)],
        20 if total <= 1024 else 40,
        "project_back",
    )


def input_grad_kernel(core_ref, gain_own, gain_other, x_ref, dm_ref, own_ref, *refs):
    x = x_ref[...].astype(F32)
    scale = rms_scale(x)
    back = own_ref[...]
    for ref in refs[:-1]:
        back = back + ref[...].astype(F32)
    scaled = back * gain_row(core_ref[0], gain_own[...], gain_other[...], 0)
    refs[-1][...] = (
        dm_ref[...]
        + scale * scaled
        - x * (scale * scale * scale) * jnp.mean(scaled * x, axis=-1, keepdims=True)
    ).astype(BF)


def input_grad_of(core, gains, x, dm, own, received):
    return call(
        input_grad_kernel,
        [core, *gains] + [Load(value) for value in (x, dm, own, *received)],
        [Store(x.shape, BF)],
        14 if len(received) == 1 else 24,
        "input_grad",
    )[0]


def swap(value, axis, mask):
    count = lax.axis_size(axis)
    return lax.ppermute(value, axis, [(i, i ^ mask) for i in range(count)])


def tie(values, *earlier):
    return lax.optimization_barrier((values, earlier))[0]


def fold_kernel(count, bits_ref, *refs):
    outs = refs[2 * count :]
    for i in range(count):
        own, got = refs[2 * i], refs[2 * i + 1]
        half = own.shape[0] // 2
        for j, bit in ((0, bits_ref[i]), (1, 1 - bits_ref[i])):
            here = pl.ds(pl.multiple_of(bit * half, 16), half)
            outs[2 * i + j][...] = (own[here, :].astype(F32) + got[here, :].astype(F32)).astype(BF)


def paired(owns, gots):
    return [part for pair in zip(owns, gots) for part in pair]


def fold(bits, owns, gots):
    outs = [shape((own.shape[0] // 2, own.shape[1]), BF) for own in owns for _ in range(2)]
    results = call(
        functools.partial(fold_kernel, len(owns)),
        [bits] + paired(owns, gots),
        outs,
        3,
        "fold",
        near=True,
    )
    return results[0::2], results[1::2]


def fold_far(bits, own, got):
    rows, cols = own.shape
    half, parts = rows // 2, 3
    size = half // parts
    inputs = []
    for i in range(2 * parts):
        for value in (own, got):

            def here(bits_ref, i=i):
                bit = bits_ref[0] if i < parts else 1 - bits_ref[0]
                return (pl.ds(pl.multiple_of(bit * half + i % parts * size, 16), size), slice(None))

            inputs.append(Load([(value, here, None)], (size, cols)))

    def body(bits_ref, *refs):
        ins, (sent, kept) = refs[:-2], refs[-2:]
        for i in range(2 * parts):
            out = kept if i < parts else sent
            place = slice(i % parts * size, (i % parts + 1) * size)
            out[place, :] = (ins[2 * i][...].astype(F32) + ins[2 * i + 1][...].astype(F32)).astype(BF)

    sent, kept = call(
        body, [bits] + inputs, [shape((half, cols), BF)] * 2, 14, "fold_far", near=True
    )
    return [kept], [sent]


def add_kernel(count, *refs):
    for i in range(count):
        refs[2 * count + i][...] = (
            refs[2 * i][...].astype(F32) + refs[2 * i + 1][...].astype(F32)
        ).astype(BF)


def add(owns, gots):
    return call(
        functools.partial(add_kernel, len(owns)),
        paired(owns, gots),
        [shape(own.shape, BF) for own in owns],
        3,
        "add",
        near=True,
    )


def merge_kernel(count, bits_ref, *refs):
    for i in range(count):
        refs[2 * count + i][...] = stack(bits_ref[i], refs[2 * i][...], refs[2 * i + 1][...])


def merge(bits, owns, gots):
    return call(
        functools.partial(merge_kernel, len(owns)),
        [bits] + paired(owns, gots),
        [shape((2 * own.shape[0], own.shape[1]), BF) for own in owns],
        3,
        "merge",
        near=True,
    )


class Chain:
    def __init__(self, orders, owns, others):
        sizes = [lax.axis_size(axis) for axis in ("grp", "ctx", "wsh")]
        total = sizes[0] * sizes[1] * sizes[2]
        near = [2, 2 * sizes[1], 4 * sizes[1]]
        self.far, mask = [], 2
        while mask < total:
            if mask not in near:
                self.far.append(mask)
            mask *= 2
        here = (lax.axis_index("grp") * sizes[1] + lax.axis_index("ctx")) * 2 + lax.axis_index("wsh")
        self.total, self.near, self.orders = total, near, orders
        self.bits = []
        for stage in range(3):
            row = []
            for order in orders:
                one, two = near[order[0][stage]], near[order[1][stage]]
                mask = jnp.where(lax.axis_index("wsh") == 0, one, two)
                row.append((here // mask) % 2)
            self.bits.append(jnp.stack(row).astype(jnp.int32))
        self.count = 0
        self.kept = list(owns)
        self.got = [self.send(value, (1, 1)) for value in others]

    def send(self, value, masks):
        pairs = [(i, i ^ masks[i % 2]) for i in range(self.total)]
        return lax.ppermute(value, ("grp", "ctx", "wsh"), pairs)

    def send_near(self, values, stage):
        return [
            self.send(value, (self.near[order[0][stage]], self.near[order[1][stage]]))
            for value, order in zip(values, self.orders)
        ]

    def stages(self):
        return 3 + 1 + len(self.far) + 2

    def step(self, *earlier):
        stage, far = self.count, len(self.far)
        self.count += 1
        kept, got = tie((self.kept, self.got), *earlier)
        if stage < 3:
            far_away = stage == 0 and len(kept) == 1 and kept[0].shape[0] % 96 == 0
            self.kept, sent = fold_far(self.bits[0], kept[0], got[0]) if far_away else fold(self.bits[stage], kept, got)
            self.got = self.send_near(sent, stage)
            return sent
        if stage <= 3 + far:
            self.kept = add(kept, got)
            if stage < 3 + far:
                mask = self.far[stage - 3]
                self.got = [self.send(value, (mask, mask)) for value in self.kept]
            else:
                self.got = self.send_near(self.kept, 2)
            return self.kept
        back = 2 - (stage - 4 - far)
        self.kept = merge(self.bits[back], kept, got)
        self.got = self.send_near(self.kept, back - 1)
        return self.kept


def over_gain(total, gain):
    return jnp.sum(total, axis=1, keepdims=True) / gain


def ffn_finish_kernel(bits_ref, gain_ref, gate_ref, up_ref, *refs):
    dgate_ref, dup_ref, ddown_ref, dgain_ref = refs[4:]
    early = stack(bits_ref[0], refs[0][...], refs[1][...])
    late = stack(bits_ref[1], refs[2][...], refs[3][...])
    half, wide = D // 2, early.shape[1] // 2
    total = jnp.zeros((half, wide), F32)
    for i, (weight, out) in enumerate(((gate_ref, dgate_ref), (up_ref, dup_ref))):
        for part, value in ((0, early), (1, late)):
            for j in range(2):
                piece = value[i * half : (i + 1) * half, j * wide : (j + 1) * wide].astype(F32)
                place = slice((part + 2 * j) * wide, (part + 2 * j + 1) * wide)
                out[:, place] = piece
                total = total + piece * weight[:, place].astype(F32)
        out.send()
    dgain_ref[...] = over_gain(total, gain_ref[...])
    for part, value in ((0, early), (1, late)):
        for j in range(2):
            piece = value[2 * half :, j * wide : (j + 1) * wide]
            ddown_ref[part * wide : (part + 1) * wide, j * half : (j + 1) * half] = piece.T.astype(F32)


def ffn_finish(bits, gain, gate, up, early, late):
    hidden, half = gate.shape[1], D // 2
    outs = [(half, hidden), (half, hidden), (hidden // 2, D), (half, 1)]
    arrays = (gate, up, early.kept[0], early.got[0], late.kept[0], late.got[0])
    return call(
        ffn_finish_kernel,
        [bits, gain] + [Load(value) for value in arrays],
        [Store(dims, F32) for dims in outs[:3]] + [shape(outs[3], F32)],
        30,
        "ffn_finish",
    )


def attention_finish_kernel(bits_ref, gain_ref, *refs):
    streams = len(refs) // 2 - 4
    weights, outs = refs[:3], refs[3 + 2 * streams :]
    value = jnp.concatenate(
        [stack(bits_ref[i], refs[3 + 2 * i][...], refs[4 + 2 * i][...]) for i in range(streams)], axis=0
    )
    half = D // 2
    total = jnp.zeros((half, D), F32)
    for i in range(4):
        piece = value[i * half : (i + 1) * half].astype(F32)
        outs[i][...] = piece
        outs[i].send()
        if i < 3:
            total = total + piece * weights[i][...].astype(F32)
    outs[4][...] = over_gain(total, gain_ref[...])


def attention_finish(bits, gain, weights, chain):
    half = D // 2
    return call(
        attention_finish_kernel,
        [bits, gain] + [Load(value) for value in (*weights, *paired(chain.kept, chain.got))],
        [Store((half, D), F32)] * 4 + [shape((half, 1), F32)],
        20,
        "attention_finish",
    )


def on_device(
    tokens,
    lengths,
    query_weight,
    key_weight,
    value_weight,
    output_weight,
    gate_weight,
    up_weight,
    down_weight,
    attn_gain,
    ffn_gain,
    out_grad,
):
    blocks = lax.axis_size("ctx")
    x, grad = tokens[0], out_grad[0]
    rows = x.shape[0]
    place = lax.axis_index("ctx")
    core = lax.axis_index("wsh").astype(jnp.int32)[None]
    limits = jnp.clip(
        lengths[0] - rows * jnp.stack([place ^ r for r in range(blocks)]).astype(jnp.int32), 0, rows
    )

    def both(own):
        return (own, swap(own, "wsh", 1))

    wq, wk, wv = both(query_weight), both(key_weight), both(value_weight)
    gains = both(jnp.stack([attn_gain, ffn_gain]))
    others = [swap(x, "ctx", r) for r in range(1, blocks)]
    x_rest = others[0] if blocks == 2 else jnp.concatenate(others, axis=0)
    if blocks == 2:
        (h1, queries, key, value), partial = own_rows(core, limits, x, gains, [wq, wk, wv])
    else:
        h1, queries, key, value = project(core, x, gains, [wq, wk, wv])
        partial = attend_own(limits, queries, key, value)
    wo, wg, wu, wd = (
        both(tie(weight, wv[1])) for weight in (output_weight, gate_weight, up_weight, down_weight)
    )
    ffn_weights = (wg, wu, wd)
    if blocks == 2:
        rest, (wide, low, extra), kept, own, other = middle(
            core, limits, gains, x, x_rest, [wk, wv], queries, partial, wo, grad, ffn_weights
        )
    else:
        rest = project(core, x_rest, gains, [wk, wv])
        wide, low, extra = attend_rest(limits, queries, *rest[1:], partial)
        *kept, own, other = ffn_first(core, limits, x, low, wo, gains, grad, ffn_weights)
    normed, keys, values = (h1, rest[0]), (key, rest[1]), (value, rest[2])
    first = Chain([((0, 1, 2), (1, 0, 2))], [own], [other])
    output, dm, dmb, own, other = ffn_last(core, limits, kept, gains, grad, ffn_weights)
    second = Chain([((2, 1, 0), (0, 2, 1))], [own], [other])
    token = first.step(dmb)
    arrays = (core, limits, queries, keys, values)
    *most, out_term = attend_back(*arrays, tie(dmb, token), wide, low, extra, wo, 0, 4, ())
    token = first.step(out_term)
    token = second.step(token)
    arrays += (tie(dmb, token), wide, low, extra, wo, 4, 2)
    if blocks == 2:
        *final, own, other = last_piece(*arrays, most, [out_term], normed)
        grads = list(zip(most, final))
    else:
        *most, last_term = attend_back(*arrays, most)
        own, other = project_grads(core, normed, most[0], most[1:3], most[3:5], [out_term, last_term])
        grads = [(value,) for value in most]
    dq, dks, dvs = grads[0], grads[1:3], grads[3:5]
    third = Chain([((0, 1, 2), (1, 2, 0))], [own], [other])
    token = first.step(own)
    token = second.step(token)
    back_rest, back_own = project_back(core, tie(dq, token), dks, dvs, [wq, wk, wv])
    received = [
        swap(back_rest[(r - 1) * rows : r * rows] if blocks > 2 else back_rest, "ctx", r)
        for r in range(1, blocks)
    ]
    token = third.step(back_own)
    token = first.step(token)
    token = second.step(token)
    token = third.step(token)
    input_grad = input_grad_of(core, gains, x, dm, tie(back_own, token), received)
    token = input_grad
    waiting = [first, third, second]
    while any(chain.count < chain.stages() for chain in waiting):
        for chain in waiting:
            if chain.count < chain.stages():
                token = chain.step(token)
    bits = jnp.concatenate([first.bits[0], second.bits[0]])
    dgate, dup, ddown, dgain_ffn = ffn_finish(
        bits, ffn_gain.astype(F32)[:, None], gate_weight, up_weight, first, second
    )
    dquery, dkey, dvalue, dout, dgain_attn = attention_finish(
        third.bits[0], attn_gain.astype(F32)[:, None], [query_weight, key_weight, value_weight], third
    )
    return (
        output[None],
        input_grad[None],
        dquery,
        dkey,
        dvalue,
        dout,
        dgate,
        dup,
        ddown,
        dgain_attn[:, 0],
        dgain_ffn[:, 0],
    )


def solution(mesh):
    rows, weights, vector = P(("grp", "wsh"), "ctx", None), P("wsh", None), P("wsh")
    in_specs = (rows, P(("grp", "wsh"))) + (weights,) * 7 + (vector,) * 2 + (rows,)
    out_specs = (rows,) * 2 + (weights,) * 7 + (vector,) * 2
    return jax.shard_map(
        on_device, mesh=mesh, in_specs=in_specs, out_specs=out_specs, check_vma=False
    )
```

```python
import functools

import jax
import jax.numpy as jnp
from jax import lax
from jax.experimental import pallas as pl
from jax.experimental.pallas import tpu as pltpu
from jax.sharding import PartitionSpec as P

D = 768
HEAD_DIM = 64
PAIR = 2 * HEAD_DIM
EPSILON = 1e-06
DEAD = -1e30

F32 = jnp.float32
BF = jnp.bfloat16
NN = (((1,), (0,)), ((), ()))
NT = (((1,), (1,)), ((), ()))
SMEM = pl.BlockSpec(memory_space=pltpu.SMEM)
LOCAL = pl.BlockSpec(memory_space=pltpu.VMEM)
FAR = pl.BlockSpec(memory_space=pltpu.HBM)
ANYWHERE = pl.BlockSpec(memory_space=pl.ANY)


def mm(left, right, dims):
    return lax.dot_general(left, right, dims, preferred_element_type=F32)


class Load:
    def __init__(self, pieces, dims=None, arrived=()):
        self.pieces = pieces if isinstance(pieces, list) else [(pieces, None, None)]
        self.arrived = arrived
        first = self.pieces[0][0]
        self.dims, self.dtype = dims or first.shape, first.dtype


class Choice(Load):
    def __init__(self, pair, holder, rows):
        self.pieces = [(pair[0], None, None), (pair[1], None, None)]
        self.dims, self.dtype = (rows.stop - rows.start, pair[0].shape[1]), pair[0].dtype
        self.arrived = (1,)
        self.holder, self.rows = holder, rows


class Store:
    def __init__(self, dims, dtype, columns=None):
        self.shape = shape(dims, dtype)
        self.columns = columns
        self.dims = dims if columns is None else (dims[0], columns.stop - columns.start)


AHEAD = 4
LONG, SHORT = 10**11, 10**10


class Spread(Store):
    def __init__(self, dims, dtype, parts):
        self.shape, self.parts = shape(dims, dtype), parts


class Arriving:
    def __init__(self, ref, starts, waits, queue):
        self.ref, self.starts, self.waits, self.queue = ref, starts, waits, queue
        self.shape, self.place = ref.shape, len(queue)
        queue.append(self)

    def begin(self):
        for start in self.starts:
            start()
        self.starts = []

    def ready(self):
        if self.waits:
            for value in self.queue[: self.place + 1 + AHEAD]:
                value.begin()
            for copy in self.waits:
                copy.wait()
            self.waits = []
        return self.ref

    def __getitem__(self, index):
        return self.ready()[index]


class Leaving:
    def __init__(self, ref, target, sem):
        self.ref, self.target, self.sem, self.started = ref, target, sem, False
        self.copy = pltpu.make_async_copy(ref, target, sem)
        self.shape = ref.shape

    def ready(self):
        return self.ref

    def send_lanes(self, here):
        pltpu.make_async_copy(self.ref.at[:, here], self.target.at[:, here], self.sem).start()
        self.started = True

    def __getitem__(self, index):
        return self.ref[index]

    def __setitem__(self, index, value):
        self.ref[index] = value

    def send(self):
        if not self.started:
            self.copy.start()
        self.started = True


def placed(ref, index):
    return ref if index is None else ref.at[index]


def call(body, inputs, outs, vmem, name, scratch=(), aliases=(), near=False):
    arrays, in_specs, loads, copies, plan = [], [], [], 0, []
    for value in inputs:
        if isinstance(value, Load):
            plan.append(len(loads))
            loads.append(value)
            for i, piece in enumerate(value.pieces):
                arrived = i in value.arrived
                arrays.append(piece[0] if arrived else pltpu.with_memory_space_constraint(piece[0], pltpu.HBM))
                in_specs.append(ANYWHERE if arrived else FAR)
            copies += len(value.pieces)
        else:
            plan.append(None)
            pinned = near and value.dtype != jnp.int32
            arrays.append(pltpu.with_memory_space_constraint(value, pltpu.VMEM) if pinned else value)
            in_specs.append(SMEM if value.dtype == jnp.int32 else LOCAL)
    count = len(arrays)
    arrays += [pltpu.with_memory_space_constraint(value, pltpu.HBM) for value in aliases]
    in_specs += [FAR] * len(aliases)
    stores = [out for out in outs if isinstance(out, Store)]
    out_shape = [
        pltpu.HBM(out.shape.shape, out.shape.dtype)
        if isinstance(out, Store)
        else pltpu.VMEM(out.shape, out.dtype) if near else out
        for out in outs
    ]
    out_specs = [
        FAR if isinstance(out, Store) else LOCAL for out in outs
    ]
    own_scratch = [pltpu.VMEM(load.dims, load.dtype) for load in loads]
    homes_of = [
        [dims for dims, _ in store.parts] if isinstance(store, Spread) else [store.dims] for store in stores
    ]
    own_scratch += [pltpu.VMEM(dims, store.shape.dtype) for store, group in zip(stores, homes_of) for dims in group]
    copies += sum(len(group) for group in homes_of)
    sems = [pltpu.SemaphoreType.DMA((copies,))] if copies else []

    def kernel(*refs):
        ins, results = refs[:count], refs[len(arrays) : len(arrays) + len(outs)]
        rest = list(refs[len(arrays) + len(outs) :])
        homes, sem = rest[: len(own_scratch)], rest[len(own_scratch)] if sems else None
        extra = rest[len(own_scratch) + len(sems) :]
        given, queue, at, number = [], [], 0, 0
        for index in plan:
            if index is None:
                given.append(ins[at])
                at += 1
                continue
            load, home, starts, waits = loads[index], homes[index], [], []
            if isinstance(load, Choice):
                copies_of = [pltpu.make_async_copy(ins[at + i].at[load.rows, :], home, sem.at[number]) for i in (0, 1)]

                def start(copies_of=copies_of, holder=load.holder):
                    for i, copy in enumerate(copies_of):
                        pl.when((given[0][0] == holder) == (i == 0))(copy.start)

                starts, waits = [start], [copies_of[0]]
                at, number = at + 2, number + 2
            else:
                for _, source, target in load.pieces:
                    copy = pltpu.make_async_copy(
                        placed(ins[at], source and source(given[0])),
                        placed(home, target and target(given[0])),
                        sem.at[number],
                    )
                    starts.append(copy.start)
                    waits.append(copy)
                    at, number = at + 1, number + 1
            given.append(Arriving(home, starts, waits, queue))
        for value in queue[: 1 + AHEAD]:
            value.begin()
        leaving, made = [], []
        for out, result in zip(outs, results):
            if isinstance(out, Spread):
                group = []
                for _, place in out.parts:
                    home = homes[len(loads) + len(leaving)]
                    leaving.append(Leaving(home, result.at[place], sem.at[number]))
                    group.append(leaving[-1])
                    number += 1
                made.append(group)
            elif isinstance(out, Store):
                home = homes[len(loads) + len(leaving)]
                target = result if out.columns is None else result.at[:, out.columns]
                leaving.append(Leaving(home, target, sem.at[number]))
                made.append(leaving[-1])
                number += 1
            else:
                made.append(result)
        body(*given, *made, *extra)
        for value in queue:
            value.ready()
        for value in leaving:
            value.send()
        for value in leaving:
            value.copy.wait()

    results = [out.shape if isinstance(out, Store) else out for out in outs]
    moved = sum(value.size * value.dtype.itemsize for value in arrays + results)
    return pl.pallas_call(
        kernel,
        in_specs=in_specs,
        out_specs=out_specs,
        out_shape=out_shape,
        scratch_shapes=own_scratch + sems + list(scratch),
        input_output_aliases={count + i: i for i in range(len(aliases))},
        compiler_params=pltpu.CompilerParams(vmem_limit_bytes=vmem << 20),
        cost_estimate=pl.CostEstimate(flops=SHORT if near else LONG, bytes_accessed=moved, transcendentals=0),
        name=name,
    )(*arrays)


def joined_halves(pair, columns=slice(None)):
    half = pair[0].shape[0]
    pieces = []
    for array, mine in zip(pair, (True, False)):

        def into(core_ref, mine=mine):
            start = (core_ref[0] if mine else 1 - core_ref[0]) * half
            return (pl.ds(pl.multiple_of(start, half), half), slice(None))

        pieces.append((array, lambda core_ref: (slice(None), columns), into))
    start, stop, _ = columns.indices(pair[0].shape[1])
    return Load(pieces, (2 * half, stop - start), arrived=(1,))


def shape(dims, dtype):
    return jax.ShapeDtypeStruct(dims, dtype)


def rms_scale(values):
    return lax.rsqrt(jnp.mean(values * values, axis=-1, keepdims=True) + EPSILON)


def stack(core, own, other):
    return jnp.concatenate(
        [jnp.where(core == 0, own, other), jnp.where(core == 0, other, own)], axis=0
    )


def gain_row(core, own, other, index):
    own = own[index : index + 1, :].astype(F32)
    other = other[index : index + 1, :].astype(F32)
    return jnp.concatenate(
        [jnp.where(core == 0, own, other), jnp.where(core == 0, other, own)], axis=1
    )


def lanes(step, size):
    return pl.ds(pl.multiple_of(step * size, size), size)


def project_kernel(count, core_ref, gain_own, gain_other, x_ref, *refs):
    weights, outs = refs[:count], refs[count:]
    gain = gain_row(core_ref[0], gain_own[...], gain_other[...], 0)
    x = x_ref[...].astype(F32)
    outs[0][...] = (x * rms_scale(x) * gain).astype(BF)
    outs[0].send()
    normed = outs[0][...]
    for i in range(count):
        outs[1 + i][...] = mm(normed, weights[i][...], NN).astype(BF)
        outs[1 + i].send()


def project(core, x, gains, weights):
    count = len(weights)
    return call(
        functools.partial(project_kernel, count),
        [core, *gains, Load(x)] + [joined_halves(pair) for pair in weights],
        [Store(x.shape, BF) for _ in range(1 + count)],
        14 if x.shape[0] <= 512 else 48,
        "project",
    )


def split3(value):
    high = value.astype(BF).astype(F32)
    rest = value - high
    mid = rest.astype(BF).astype(F32)
    return high, mid, rest - mid


def key_extra(limit, rows):
    lane = lax.broadcasted_iota(jnp.int32, (rows, PAIR), 1) % HEAD_DIM
    row = lax.broadcasted_iota(jnp.int32, (rows, PAIR), 0)
    bias = jnp.where(row < limit, 0.0, DEAD)
    return jnp.where(lane < 3, 1.0, jnp.where(lane == 3, bias, 0.0)).astype(BF)


def block_of(step, rows):
    return pl.ds(pl.multiple_of(step * rows, rows), rows)


def place3(lane, base, parts, into):
    for i in (2, 1, 0):
        into = jnp.where(lane == base + i, parts[i], into)
    return into


def attend_block(limit, queries, bias_lane, keys, values, lane, earlier):
    rows = queries.shape[0]
    extra = key_extra(limit, rows)
    ones = jnp.ones((rows, PAIR), BF)
    results = []
    for head in range(2):
        mine = lane // HEAD_DIM == head
        scores = mm(jnp.where(mine, queries, bias_lane), jnp.where(mine, keys, extra), NT)
        top = jnp.max(scores, axis=-1, keepdims=True)
        if earlier is not None:
            top = jnp.maximum(top, earlier[head][1])
        weights = jnp.exp(scores - top).astype(BF)
        total = mm(weights, jnp.where(mine, values, ones), NN)
        if earlier is not None:
            total = total + earlier[head][0] * jnp.exp(earlier[head][1] - top)
        results.append((total, top))
    return results


def scaled_queries(q_ref, here):
    queries = q_ref[:, here] * jnp.asarray(HEAD_DIM**-0.5, BF)
    lane = lax.broadcasted_iota(jnp.int32, queries.shape, 1)
    return queries, jnp.where(lane % HEAD_DIM == 3, 1.0, 0.0).astype(BF), lane


def attend_own_kernel(limits_ref, q_ref, k_ref, v_ref, first_ref, second_ref, top_ref):
    top_ref[...] = jnp.zeros_like(top_ref.ref)
    for ref in (q_ref, k_ref, v_ref):
        ref.ready()

    @pl.loop(0, D // PAIR)
    def _(pair):
        here = lanes(pair, PAIR)
        queries, bias_lane, lane = scaled_queries(q_ref, here)
        heads = attend_block(limits_ref[0], queries, bias_lane, k_ref[:, here], v_ref[:, here], lane, None)
        first_ref[:, here], second_ref[:, here] = heads[0][0], heads[1][0]
        first_ref.send_lanes(here)
        second_ref.send_lanes(here)
        tops = top_ref[...]
        for head in range(2):
            tops = jnp.where(lane == 2 * pair + head, heads[head][1], tops)
        top_ref[...] = tops


def attend_own(limits, queries, keys, values):
    rows = queries.shape[0]
    return call(
        attend_own_kernel,
        [limits, Load(queries), Load(keys), Load(values)],
        [Store((rows, D), F32), Store((rows, D), F32), Store((rows, PAIR), F32)],
        16,
        "attend_own",
    )


def own_rows_kernel(core_ref, limits_ref, gain_own, gain_other, x_ref, wq, wk, wv, h1, q, k, v, *partial):
    project_kernel(3, core_ref, gain_own, gain_other, x_ref, wq, wk, wv, h1, q, k, v)
    attend_own_kernel(limits_ref, q, k, v, *partial)


def own_rows(core, limits, x, gains, weights):
    rows = x.shape[0]
    results = call(
        own_rows_kernel,
        [core, limits, *gains, Load(x)] + [joined_halves(pair) for pair in weights],
        [Store((rows, D), BF) for _ in range(4)]
        + [Store((rows, D), F32), Store((rows, D), F32), Store((rows, PAIR), F32)],
        22,
        "own_rows",
    )
    return results[:4], results[4:]


def attend_rest_kernel(limits_ref, q_ref, k_ref, v_ref, first_ref, second_ref, top_ref, wide_ref, low_ref, extra_ref):
    for ref in (q_ref, k_ref, v_ref, first_ref, second_ref, top_ref):
        ref.ready()
    rows = q_ref.shape[0]
    blocks = k_ref.shape[0] // rows

    @pl.loop(0, D // PAIR)
    def _(pair):
        here = lanes(pair, PAIR)
        queries, bias_lane, lane = scaled_queries(q_ref, here)
        tops = top_ref[...]
        heads = [
            (ref[:, here], jnp.sum(jnp.where(lane == 2 * pair + i, tops, 0.0), axis=-1, keepdims=True))
            for i, ref in enumerate((first_ref, second_ref))
        ]

        def more(block, heads):
            place = block_of(block, rows)
            return attend_block(
                limits_ref[1 + block], queries, bias_lane, k_ref[place, here], v_ref[place, here], lane, heads
            )

        heads = more(0, heads) if blocks == 1 else lax.fori_loop(0, blocks, more, heads)
        log_lanes = jnp.where(lane % HEAD_DIM == 3, 1.0, 0.0)
        outs = []
        for head, (total, top) in enumerate(heads):
            outs.append(total / pltpu.roll(total, HEAD_DIM, 1))
            log_lanes = place3(
                lane, HEAD_DIM * (1 - head), split3(-(top + jnp.log(total))), log_lanes
            )
        attended = jnp.where(lane < HEAD_DIM, outs[0], outs[1])
        wide_ref[:, here] = attended
        low_ref[:, here] = attended.astype(BF)
        extra_ref[:, here] = log_lanes.astype(BF)
        for ref in (wide_ref, low_ref, extra_ref):
            ref.send_lanes(here)


def attend_rest(limits, queries, keys, values, partial):
    rows = queries.shape[0]
    return call(
        attend_rest_kernel,
        [limits, Load(queries), Load(keys), Load(values)] + [Load(value) for value in partial],
        [Store((rows, D), F32), Store((rows, D), BF), Store((rows, D), BF)],
        18 if keys.shape[0] == rows else 40,
        "attend_rest",
    )


def attend_back_kernel(count, limits_ref, q_ref, dmb_ref, wo_ref, low_ref, wide_ref, extra_ref, *refs):
    inputs, outs = refs[:4], refs[4:]
    dq_ref, grad_refs, out_ref = outs[0], outs[1:5], outs[5]
    rows = q_ref.shape[0]
    scale = jnp.asarray(HEAD_DIM**-0.5, BF)
    lane = lax.broadcasted_iota(jnp.int32, (rows, PAIR), 1)
    none = jnp.zeros((rows, PAIR), BF)
    for ref in (q_ref, dmb_ref, low_ref, wide_ref, extra_ref, *inputs):
        ref.ready()

    @pl.loop(0, count)
    def _(pair):
        here = lanes(pair, PAIR)
        queries = q_ref[:, here] * scale
        dmb = dmb_ref[...]
        grads = mm(dmb, wo_ref[here, :], NT).astype(BF)
        out_ref[here, :] = mm(low_ref[:, here].T, dmb, NN).astype(BF)
        log_lanes = extra_ref[:, here]
        product = grads.astype(F32) * wide_ref[:, here]
        delta_lanes = jnp.zeros((rows, PAIR), F32)
        for head in range(2):
            mine = lane // HEAD_DIM == head
            delta = -jnp.sum(jnp.where(mine, product, 0.0), axis=-1, keepdims=True)
            delta_lanes = place3(lane, HEAD_DIM * (1 - head), split3(delta), delta_lanes)
        delta_lanes = delta_lanes.astype(BF)

        def over(limit, k_ref, v_ref, dk_ref, dv_ref, place):
            keys, values = k_ref[place, here], v_ref[place, here]
            extra = key_extra(limit, rows)
            keys_turned = (keys * scale).T
            dk = dv = 0.0
            dqs = []
            for head in range(2):
                mine = lane // HEAD_DIM == head
                probs = jnp.exp(
                    mm(jnp.where(mine, keys, extra), jnp.where(mine, queries, log_lanes), NT)
                )
                shifted = mm(
                    jnp.where(mine, values, extra), jnp.where(mine, grads, delta_lanes), NT
                )
                dscores = (probs * shifted).astype(BF)
                dv = dv + mm(probs.astype(BF), jnp.where(mine, grads, none), NN)
                dk = dk + mm(dscores, jnp.where(mine, queries, none), NN)
                dqs.append(mm(keys_turned[head * HEAD_DIM : (head + 1) * HEAD_DIM], dscores, NN))
            dk_ref[place, here] = dk.astype(BF)
            dv_ref[place, here] = dv.astype(BF)
            return jnp.concatenate(dqs, axis=0)

        k_own, k_rest, v_own, v_rest = inputs
        dk_own, dk_rest, dv_own, dv_rest = grad_refs
        dq = over(limits_ref[0], k_own, v_own, dk_own, dv_own, slice(None))
        blocks = k_rest.shape[0] // rows

        def more(block, dq):
            return dq + over(limits_ref[1 + block], k_rest, v_rest, dk_rest, dv_rest, block_of(block, rows))

        dq = more(0, dq) if blocks == 1 else lax.fori_loop(0, blocks, more, dq)
        dq_ref[:, here] = dq.T.astype(BF)
        for ref in (dq_ref, *grad_refs):
            ref.send_lanes(here)


def attend_back_inputs(queries, keys, values, dmb, wide, low, extra, out_weight, first, count):
    columns = slice(first * PAIR, (first + count) * PAIR)
    half = D // PAIR // 2

    def part(value):
        dims = (value.shape[0], columns.stop - columns.start)
        return Load([(value, lambda core_ref: (slice(None), columns), None)], dims)

    rows_of = [
        Choice(out_weight, pair // half, slice(pair % half * PAIR, (pair % half + 1) * PAIR))
        for pair in range(first, first + count)
    ]
    loads = [part(queries), Load(dmb)] + rows_of + [part(low), part(wide), part(extra)]
    return loads + [part(value) for value in (keys[0], values[0], keys[1], values[1])], columns


def attend_back_body(count, core_ref, limits_ref, refs, turned_wo):
    q_ref, dmb_ref, wo_refs, rest = refs[0], refs[1], refs[2 : 2 + count], refs[2 + count :]
    for i, ref in enumerate(wo_refs):
        turned_wo[i * PAIR : (i + 1) * PAIR, :] = ref[...]
    low_ref, wide_ref, extra_ref, k_own, v_own, k_rest, v_rest = rest[:7]
    attend_back_kernel(
        count, limits_ref, q_ref, dmb_ref, turned_wo, low_ref, wide_ref, extra_ref, k_own, k_rest, v_own, v_rest, *rest[7:]
    )


def attend_back(core, limits, queries, keys, values, dmb, wide, low, extra, out_weight, first, count, earlier):
    rows, rest = queries.shape[0], keys[1].shape[0]
    loads, columns = attend_back_inputs(queries, keys, values, dmb, wide, low, extra, out_weight, first, count)

    def body(core_ref, limits_ref, *refs):
        attend_back_body(count, core_ref, limits_ref, refs[:-1], refs[-1])

    return call(
        body,
        [core, limits] + loads,
        [Store((size, D), BF, columns) for size in (rows, rows, rest, rows, rest)]
        + [Store((columns.stop - columns.start, D), BF)],
        20 if rest == rows else 48,
        "attend_back",
        [pltpu.VMEM((count * PAIR, D), BF)],
        aliases=earlier,
    )


CURVE = 0.7978845608028654
CUBIC = 0.044715


def ffn_part(part, core, step, h2_ref, turned, dyb, dyb_turned, weights, own_ref, other_ref, acc_out, acc_back):
    wide, half = own_ref.shape[1] // 2, D // 2
    here, there = lanes(step, wide), lanes(part + 2 * step, wide)
    gate_ref, up_ref, down_ref = weights
    rows = block_of(part + 2 * step, wide)
    gate = mm(h2_ref[...], gate_ref[:, there], NN)
    up = mm(h2_ref[...], up_ref[:, there], NN)
    dn = mm(dyb[...], down_ref[rows, :], NT)
    square = gate * gate
    bent = jnp.tanh(CURVE * gate * (1.0 + CUBIC * square))
    rise = 0.5 * (1.0 + bent)
    bulge = gate * rise
    slope = rise + 0.5 * gate * (1.0 - bent * bent) * (CURVE * (1.0 + 3.0 * CUBIC * square))
    hidden = (bulge * up).astype(BF)
    dgate = (dn * up * slope).astype(BF)
    dup = (dn * bulge).astype(BF)
    ddown = mm(dyb_turned[...], hidden, NN).astype(BF)

    @pl.when(step == core)
    def _():
        own_ref[2 * half :, :wide] = ddown[:half]
        own_ref[2 * half :, wide:] = ddown[half:]

    @pl.when(step != core)
    def _():
        other_ref[2 * half :, :wide] = ddown[:half]
        other_ref[2 * half :, wide:] = ddown[half:]

    dgate_term = mm(turned[...], dgate, NN).astype(BF)
    dup_term = mm(turned[...], dup, NN).astype(BF)
    for i, term in ((0, dgate_term), (1, dup_term)):
        place = slice(i * half, (i + 1) * half)
        own_ref[place, here] = jnp.where(core == 0, term[:half], term[half:])
        other_ref[place, here] = jnp.where(core == 0, term[half:], term[:half])
    acc_back[...] += mm(dgate, gate_ref[:, there], NT) + mm(dup, up_ref[:, there], NT)
    acc_out[...] += mm(hidden, down_ref[rows, :], NN)


def live_grad(limits_ref, grad_ref):
    rows = grad_ref.shape[0]
    live = lax.broadcasted_iota(jnp.int32, (rows, D), 0) < limits_ref[0]
    return jnp.where(live, grad_ref[...].astype(F32), 0.0)


def ffn_body(core_ref, limits_ref, gain_own, gain_other, a_ref, wo_ref, x_ref, grad_ref, weights, outs, scratch, m_ref, acc_out):
    core = core_ref[0]
    output_ref, dm_ref, dmb_ref, *grads = outs
    h2_ref, turned, dyb, dyb_turned = scratch
    acc_back = dm_ref.ref
    m = mm(a_ref[...], wo_ref[...], NN) + x_ref[...].astype(F32)
    gain = gain_row(core, gain_own[...], gain_other[...], 1)
    m_ref[...] = m
    h2 = (m * rms_scale(m) * gain).astype(BF)
    h2_ref[...] = h2
    turned[...] = h2.T
    low = live_grad(limits_ref, grad_ref).astype(BF)
    dyb[...] = low
    dyb_turned[...] = low.T
    acc_out[...] = jnp.zeros_like(acc_out)
    acc_back[...] = jnp.zeros_like(acc_back)
    for ref in weights:
        ref.ready()
    for part in range(2):

        @pl.loop(0, 2)
        def _(step):
            ffn_part(
                part, core, step, h2_ref, turned, dyb, dyb_turned, weights, *grads[2 * part : 2 * part + 2], acc_out, acc_back
            )

        grads[2 * part + 1].send()
        grads[2 * part].send()
    m = m_ref[...]
    scale = rms_scale(m)
    scaled = acc_back[...] * gain
    dm = dyb[...].astype(F32) + scale * scaled - m * (scale * scale * scale) * jnp.mean(
        scaled * m, axis=-1, keepdims=True
    )
    dmb_ref[...] = dm.astype(BF)
    dmb_ref.send()
    dm_ref[...] = dm
    dm_ref.send()
    output_ref[...] = (m + acc_out[...]).astype(BF)


def ffn_results(rows, hidden):
    outs = [Store((rows, D), BF), Store((rows, D), F32), Store((rows, D), BF)]
    scratch = [pltpu.VMEM((rows, D), BF), pltpu.VMEM((D, rows), BF), pltpu.VMEM((rows, D), BF), pltpu.VMEM((D, rows), BF)]
    return outs + [Store((3 * D // 2, hidden // 2), BF) for _ in range(4)], scratch


def feed_forward(core, limits, x, attended, out_weight, gains, grad, weights):
    rows, hidden = x.shape[0], weights[0][0].shape[1]
    outs, scratch = ffn_results(rows, hidden)

    def body(core_ref, limits_ref, gain_own, gain_other, a, wo, x, grad, *refs):
        ffn_body(core_ref, limits_ref, gain_own, gain_other, a, wo, x, grad, refs[:3], refs[3:10], refs[10:14], *refs[14:])

    return call(
        body,
        [core, limits, *gains, Load(attended), joined_halves(out_weight), Load(x), Load(grad)]
        + [joined_halves(pair) for pair in weights],
        outs,
        52,
        "feed_forward",
        scratch + [pltpu.VMEM((rows, D), F32)] * 2,
    )


def middle_kernel(core_ref, limits_ref, gain_own, gain_other, x_rest, wk, wv, q, first, second, top, wo, x, grad, *refs):
    weights, outs = refs[:3], refs[3:]
    h1_rest, k_rest, v_rest, wide, low, extra = outs[:6]
    project_kernel(2, core_ref, gain_own, gain_other, x_rest, wk, wv, h1_rest, k_rest, v_rest)
    attend_rest_kernel(limits_ref, q, k_rest, v_rest, first, second, top, wide, low, extra)
    ffn_body(
        core_ref, limits_ref, gain_own, gain_other, low, wo, x, grad, weights, outs[6:13], outs[13:], first.ref, second.ref
    )


def middle(core, limits, gains, x, x_rest, key_value, queries, partial, out_weight, grad, weights):
    rows, hidden = x.shape[0], weights[0][0].shape[1]
    low, full = ((rows, D), BF), ((rows, D), F32)
    ffn_outs, scratch = ffn_results(rows, hidden)
    results = call(
        middle_kernel,
        [core, limits, *gains, x_rest]
        + [joined_halves(pair) for pair in key_value]
        + [Load(queries)]
        + [Load(value) for value in partial]
        + [joined_halves(out_weight), Load(x), Load(grad)]
        + [joined_halves(pair) for pair in weights],
        [Store(*dims) for dims in (low, low, low, full, low, low)] + ffn_outs,
        60,
        "middle",
        scratch,
    )
    return results[:3], results[3:6], results[6:]


def project_grads_kernel(core_ref, own_normed, dq_ref, rest_normed, dk_own, dk_rest, dv_own, dv_rest, *refs):
    core = core_ref[0]
    out_terms, (own_ref, other_ref) = refs[:-2], refs[-2:]
    half = D // 2

    def put(i, term):
        own_ref[i * half : (i + 1) * half, :] = jnp.where(core == 0, term[:half], term[half:])
        other_ref[i * half : (i + 1) * half, :] = jnp.where(core == 0, term[half:], term[:half])

    turned = own_normed[...].T
    put(0, mm(turned, dq_ref[...], NN).astype(BF))
    turned_rest = rest_normed[...].T
    put(1, (mm(turned, dk_own[...], NN) + mm(turned_rest, dk_rest[...], NN)).astype(BF))
    put(2, (mm(turned, dv_own[...], NN) + mm(turned_rest, dv_rest[...], NN)).astype(BF))
    put(3, jnp.concatenate([term[...] for term in out_terms], axis=0))


def project_grads(core, normed, dq, dks, dvs, out_terms):
    total = dks[0].shape[0] + dks[1].shape[0]
    arrays = (normed[0], dq, normed[1], *dks, *dvs, *out_terms)
    return call(
        project_grads_kernel,
        [core] + [Load(value) for value in arrays],
        [Store((2 * D, D), BF) for _ in range(2)],
        18 if total <= 1024 else 54,
        "project_grads",
    )


def last_piece(core, limits, queries, keys, values, dmb, wide, low, extra, out_weight, first, count, earlier, out_terms, normed):
    rows, rest = queries.shape[0], keys[1].shape[0]
    loads, columns = attend_back_inputs(queries, keys, values, dmb, wide, low, extra, out_weight, first, count)
    done = slice(0, columns.start)
    inputs = len(loads)

    def before(value):
        return Load([(value, lambda core_ref: (slice(None), done), None)], (value.shape[0], done.stop))

    more = [Load(normed[0]), before(earlier[0]), Load(normed[1])]
    more += [before(value) for value in earlier[1:]] + [Load(term) for term in out_terms]

    def body(core_ref, limits_ref, *refs):
        ins, given, outs, wo, out_term = refs[:inputs], refs[inputs : inputs + len(more)], refs[-9:-4], refs[-2], refs[-1]
        own_ref, other_ref = refs[-4:-2]
        attend_back_body(count, core_ref, limits_ref, (*ins, *outs, out_term), wo)

        def both_parts(left, right):
            return jnp.concatenate([left[...], right[...]], axis=1)

        merged = [both_parts(left, right) for left, right in zip((given[1], *given[3:7]), outs)]
        project_grads_kernel(
            core_ref, given[0], merged[0], given[2], *merged[1:], *given[7:], out_term, own_ref, other_ref
        )

    width = columns.stop - columns.start
    return call(
        body,
        [core, limits] + loads + more,
        [Store((size, width), BF) for size in (rows, rows, rest, rows, rest)] + [Store((2 * D, D), BF) for _ in range(2)],
        36,
        "last_piece",
        [pltpu.VMEM((count * PAIR, D), BF)] * 2,
    )


def project_back_kernel(core_ref, dk_rest, key, dv_rest, value, dq_ref, query, dk_own, dv_own, rest_ref, own_ref):
    rows = dq_ref.shape[0]
    for ref in (dk_rest, key, dv_rest, value):
        ref.ready()

    def rest(block, _):
        place = block_of(block, rows)
        back = mm(dk_rest[place, :], key[...], NT) + mm(dv_rest[place, :], value[...], NT)
        rest_ref[place, :] = back.astype(BF)
        return _

    blocks = dk_rest.shape[0] // rows
    rest(0, 0) if blocks == 1 else lax.fori_loop(0, blocks, rest, 0)
    rest_ref.send()
    own_ref[...] = (
        mm(dq_ref[...], query[...], NT) + mm(dk_own[...], key[...], NT) + mm(dv_own[...], value[...], NT)
    )


def project_back(core, dq, dks, dvs, weights):
    query, key, value = (joined_halves(pair) for pair in weights)
    total = dks[0][0].shape[0] + dks[1][0].shape[0]

    def side_by_side(parts):
        pieces, start = [], 0
        for i, part in enumerate(parts):
            width = D - start if i == len(parts) - 1 else D - parts[-1].shape[1]
            columns = slice(start, start + width)
            take = None if part.shape[1] == width else (lambda core_ref, columns=columns: (slice(None), columns))
            pieces.append((part, take, lambda core_ref, columns=columns: (slice(None), columns)))
            start += width
        return Load(pieces, (parts[0].shape[0], D))

    dq_load, (dk_own, dk_rest), (dv_own, dv_rest) = side_by_side(dq), map(side_by_side, dks), map(side_by_side, dvs)
    return call(
        project_back_kernel,
        [core, dk_rest, key, dv_rest, value, dq_load, query, dk_own, dv_own],
        [Store((total - dq[0].shape[0], D), BF), Store((dq[0].shape[0], D), F32)],
        20 if total <= 1024 else 40,
        "project_back",
    )


def input_grad_kernel(core_ref, gain_own, gain_other, x_ref, dm_ref, own_ref, *refs):
    x = x_ref[...].astype(F32)
    scale = rms_scale(x)
    back = own_ref[...]
    for ref in refs[:-1]:
        back = back + ref[...].astype(F32)
    scaled = back * gain_row(core_ref[0], gain_own[...], gain_other[...], 0)
    refs[-1][...] = (
        dm_ref[...]
        + scale * scaled
        - x * (scale * scale * scale) * jnp.mean(scaled * x, axis=-1, keepdims=True)
    ).astype(BF)


def input_grad_of(core, gains, x, dm, own, received):
    return call(
        input_grad_kernel,
        [core, *gains] + [Load(value) for value in (x, dm, own, *received)],
        [Store(x.shape, BF)],
        14 if len(received) == 1 else 24,
        "input_grad",
    )[0]


def swap(value, axis, mask):
    count = lax.axis_size(axis)
    return lax.ppermute(value, axis, [(i, i ^ mask) for i in range(count)])


def tie(values, *earlier):
    return lax.optimization_barrier((values, earlier))[0]


def fold_kernel(count, bits_ref, *refs):
    outs = refs[2 * count :]
    for i in range(count):
        own, got = refs[2 * i], refs[2 * i + 1]
        half = own.shape[0] // 2
        for j, bit in ((0, bits_ref[i]), (1, 1 - bits_ref[i])):
            here = pl.ds(pl.multiple_of(bit * half, 16), half)
            outs[2 * i + j][...] = (own[here, :].astype(F32) + got[here, :].astype(F32)).astype(BF)


def paired(owns, gots):
    return [part for pair in zip(owns, gots) for part in pair]


def fold(bits, owns, gots):
    outs = [shape((own.shape[0] // 2, own.shape[1]), BF) for own in owns for _ in range(2)]
    results = call(
        functools.partial(fold_kernel, len(owns)),
        [bits] + paired(owns, gots),
        outs,
        3,
        "fold",
        near=True,
    )
    return results[0::2], results[1::2]


def fold_far(bits, own, got):
    rows, cols = own.shape
    half, parts = rows // 2, 3
    size = half // parts
    inputs = []
    for i in range(2 * parts):
        for value in (own, got):

            def here(bits_ref, i=i):
                bit = bits_ref[0] if i < parts else 1 - bits_ref[0]
                return (pl.ds(pl.multiple_of(bit * half + i % parts * size, 16), size), slice(None))

            inputs.append(Load([(value, here, None)], (size, cols), arrived=(0,) if value is got else ()))

    def body(bits_ref, *refs):
        ins, (sent, kept) = refs[:-2], refs[-2:]
        for i in range(2 * parts):
            out = kept if i < parts else sent
            place = slice(i % parts * size, (i % parts + 1) * size)
            out[place, :] = (ins[2 * i][...].astype(F32) + ins[2 * i + 1][...].astype(F32)).astype(BF)

    sent, kept = call(
        body, [bits] + inputs, [shape((half, cols), BF)] * 2, 14, "fold_far", near=True
    )
    return [kept], [sent]


def add_kernel(count, *refs):
    for i in range(count):
        refs[2 * count + i][...] = (
            refs[2 * i][...].astype(F32) + refs[2 * i + 1][...].astype(F32)
        ).astype(BF)


def add(owns, gots):
    return call(
        functools.partial(add_kernel, len(owns)),
        paired(owns, gots),
        [shape(own.shape, BF) for own in owns],
        3,
        "add",
        near=True,
    )


def merge_kernel(count, bits_ref, *refs):
    for i in range(count):
        refs[2 * count + i][...] = stack(bits_ref[i], refs[2 * i][...], refs[2 * i + 1][...])


def merge(bits, owns, gots):
    return call(
        functools.partial(merge_kernel, len(owns)),
        [bits] + paired(owns, gots),
        [shape((2 * own.shape[0], own.shape[1]), BF) for own in owns],
        3,
        "merge",
        near=True,
    )


class Chain:
    def __init__(self, orders, owns, others):
        sizes = [lax.axis_size(axis) for axis in ("grp", "ctx", "wsh")]
        total = sizes[0] * sizes[1] * sizes[2]
        near = [2, 2 * sizes[1], 4 * sizes[1]]
        self.far, mask = [], 2
        while mask < total:
            if mask not in near:
                self.far.append(mask)
            mask *= 2
        here = (lax.axis_index("grp") * sizes[1] + lax.axis_index("ctx")) * 2 + lax.axis_index("wsh")
        self.total, self.near, self.orders = total, near, orders
        self.bits = []
        for stage in range(3):
            row = []
            for order in orders:
                one, two = near[order[0][stage]], near[order[1][stage]]
                mask = jnp.where(lax.axis_index("wsh") == 0, one, two)
                row.append((here // mask) % 2)
            self.bits.append(jnp.stack(row).astype(jnp.int32))
        self.count = 0
        self.kept = list(owns)
        self.got = [self.send(value, (1, 1)) for value in others]

    def send(self, value, masks):
        pairs = [(i, i ^ masks[i % 2]) for i in range(self.total)]
        return lax.ppermute(value, ("grp", "ctx", "wsh"), pairs)

    def send_near(self, values, stage):
        return [
            self.send(value, (self.near[order[0][stage]], self.near[order[1][stage]]))
            for value, order in zip(values, self.orders)
        ]

    def stages(self):
        return 3 + 1 + len(self.far) + 2

    def step(self, *earlier):
        stage, far = self.count, len(self.far)
        self.count += 1
        kept, got = tie((self.kept, self.got), *earlier)
        if stage < 3:
            far_away = stage == 0 and len(kept) == 1 and kept[0].shape[0] % 96 == 0
            self.kept, sent = fold_far(self.bits[0], kept[0], got[0]) if far_away else fold(self.bits[stage], kept, got)
            self.got = self.send_near(sent, stage)
            return sent
        if stage <= 3 + far:
            self.kept = add(kept, got)
            if stage < 3 + far:
                mask = self.far[stage - 3]
                self.got = [self.send(value, (mask, mask)) for value in self.kept]
            else:
                self.got = self.send_near(self.kept, 2)
            return self.kept
        back = 2 - (stage - 4 - far)
        self.kept = merge(self.bits[back], kept, got)
        self.got = self.send_near(self.kept, back - 1)
        return self.kept


def over_gain(total, gain):
    column = jnp.broadcast_to(jnp.sum(total, axis=1, keepdims=True), (total.shape[0], PAIR))
    return column.T[:1, :] / gain.astype(F32)


def ffn_finish(bits, gain, gate, up, part, chain, earlier, before):
    half, hidden = gate.shape
    wide = hidden // 4
    columns = [slice((part + 2 * j) * wide, (part + 2 * j + 1) * wide) for j in range(2)]

    def of(value):
        pieces = [
            (value, lambda bits_ref, c=c: (slice(None), c), lambda bits_ref, j=j: (slice(None), slice(j * wide, (j + 1) * wide)))
            for j, c in enumerate(columns)
        ]
        return Load(pieces, (half, 2 * wide))

    def body(bits_ref, gain_ref, kept, got, gate_ref, up_ref, *refs):
        dgate, dup, (ddown,), gain_out = refs[-4:]
        value = stack(bits_ref[0], kept[...], got[...])
        total = refs[0][...] if before else jnp.zeros((half, PAIR), F32)
        for i, (weight, outs) in enumerate(((gate_ref, dgate), (up_ref, dup))):
            term = value[i * half : (i + 1) * half].astype(F32)
            for j in range(2):
                outs[j][...] = term[:, j * wide : (j + 1) * wide]
                outs[j].send()
            product = term * weight[...].astype(F32)
            total = total + sum(product[:, k : k + PAIR] for k in range(0, 2 * wide, PAIR))
        for j in range(2):
            piece = value[2 * half :, j * wide : (j + 1) * wide]
            ddown[:, j * half : (j + 1) * half] = piece.T.astype(F32)
        gain_out[...] = over_gain(total, gain_ref[...]) if before else total

    kept, got = tie((chain.kept[0], chain.got[0]), earlier)
    wide_parts = [((half, wide), (slice(None), c)) for c in columns]
    down_part = [((wide, D), (slice(part * wide, (part + 1) * wide), slice(None)))]
    return call(
        body,
        [bits, gain, Load(kept), Load(got), of(gate), of(up)] + list(before[3:]),
        [Spread((half, hidden), F32, wide_parts) for _ in range(2)]
        + [Spread((2 * wide, D), F32, down_part), shape((1, half) if before else (half, PAIR), F32)],
        24,
        "ffn_finish",
        aliases=before[:3],
    )


def attention_finish_kernel(bits_ref, gain_ref, *refs):
    streams = len(refs) // 2 - 4
    weights, outs = refs[:3], refs[3 + 2 * streams :]
    value = jnp.concatenate(
        [stack(bits_ref[i], refs[3 + 2 * i][...], refs[4 + 2 * i][...]) for i in range(streams)], axis=0
    )
    half = D // 2
    total = jnp.zeros((half, PAIR), F32)
    for i in range(4):
        piece = value[i * half : (i + 1) * half].astype(F32)
        outs[i][...] = piece
        outs[i].send()
        if i < 3:
            product = piece * weights[i][...].astype(F32)
            total = total + sum(product[:, k : k + PAIR] for k in range(0, D, PAIR))
    outs[4][...] = over_gain(total, gain_ref[...])


def attention_finish(bits, gain, weights, chain):
    half = D // 2
    return call(
        attention_finish_kernel,
        [bits, gain] + [Load(value) for value in (*weights, *paired(chain.kept, chain.got))],
        [Store((half, D), F32)] * 4 + [shape((1, half), F32)],
        20,
        "attention_finish",
    )


ORDER = (3, 1, 2, 1, 3, 2, "send", 1, 3, 3, 2, 1, 2, 3, 1, 3, 2, "input", 3, "early", "late")
AXES = (((0, 1, 2), (1, 0, 2)), ((2, 1, 0), (0, 2, 1)), ((0, 1, 2), (1, 2, 0)))
EARLY = 1


def on_device(
    tokens,
    lengths,
    query_weight,
    key_weight,
    value_weight,
    output_weight,
    gate_weight,
    up_weight,
    down_weight,
    attn_gain,
    ffn_gain,
    out_grad,
):
    blocks = lax.axis_size("ctx")
    x, grad = tokens[0], out_grad[0]
    rows = x.shape[0]
    place = lax.axis_index("ctx")
    core = lax.axis_index("wsh").astype(jnp.int32)[None]
    limits = jnp.clip(
        lengths[0] - rows * jnp.stack([place ^ r for r in range(blocks)]).astype(jnp.int32), 0, rows
    )

    def both(own):
        return (own, swap(own, "wsh", 1))

    wq, wk, wv = both(query_weight), both(key_weight), both(value_weight)
    gains = both(jnp.stack([attn_gain, ffn_gain]))
    others = [swap(x, "ctx", r) for r in range(1, blocks)]
    x_rest = others[0] if blocks == 2 else jnp.concatenate(others, axis=0)
    if blocks == 2:
        (h1, queries, key, value), partial = own_rows(core, limits, x, gains, [wq, wk, wv])
    else:
        h1, queries, key, value = project(core, x, gains, [wq, wk, wv])
        partial = attend_own(limits, queries, key, value)
    wo, wg, wu, wd = (
        both(tie(weight, wv[1])) for weight in (output_weight, gate_weight, up_weight, down_weight)
    )
    ffn_weights = (wg, wu, wd)
    if blocks == 2:
        rest, (wide, low, extra), results = middle(
            core, limits, gains, x, x_rest, [wk, wv], queries, partial, wo, grad, ffn_weights
        )
    else:
        rest = project(core, x_rest, gains, [wk, wv])
        wide, low, extra = attend_rest(limits, queries, *rest[1:], partial)
        results = feed_forward(core, limits, x, low, wo, gains, grad, ffn_weights)
    output, dm, dmb, *sums = results
    normed, keys, values = (h1, rest[0]), (key, rest[1]), (value, rest[2])
    first = Chain([AXES[0]], sums[:1], sums[1:2])
    second = Chain([AXES[1]], sums[2:3], sums[3:4])
    arrays = (core, limits, queries, keys, values)
    *most, out_term = attend_back(*arrays, dmb, wide, low, extra, wo, 0, EARLY, ())
    token = second.step(first.step(out_term))
    out_terms = [out_term]
    arrays += (tie(dmb, token), wide, low, extra, wo, EARLY, D // PAIR - EARLY)
    if blocks == 2:
        *final, own, other = last_piece(*arrays, most, out_terms, normed)
        grads = list(zip(most, final))
    else:
        *most, last_term = attend_back(*arrays, most)
        own, other = project_grads(core, normed, most[0], most[1:3], most[3:5], [*out_terms, last_term])
        grads = [(value,) for value in most]
    dq, dks, dvs = grads[0], grads[1:3], grads[3:5]
    third = Chain([AXES[2]], [own], [other])
    token = first.step(own)
    token = second.step(token)
    back_rest, back_own = project_back(core, tie(dq, token), dks, dvs, [wq, wk, wv])
    token, received, chains, hidden = back_own, [], (first, second, third), ()
    for name in ORDER:
        if name == "send":
            sent = tie(back_rest, token)
            received = [
                swap(sent[(r - 1) * rows : r * rows] if blocks > 2 else sent, "ctx", r)
                for r in range(1, blocks)
            ]
        elif name == "input":
            token = input_grad = input_grad_of(core, gains, x, dm, tie(back_own, token), received)
        elif name in ("early", "late"):
            part = int(name == "late")
            chain = (first, second)[part]
            hidden = ffn_finish(
                chain.bits[0], ffn_gain[None], gate_weight, up_weight, part, chain, token, hidden
            )
            token = hidden[3]
        else:
            chain = chains[name - 1]
            for _ in range(1 + (len(chain.far) - 1) * (chain.count == 4)):
                token = chain.step(token)
    dquery, dkey, dvalue, dout, dgain_attn = attention_finish(
        third.bits[0], attn_gain[None], [query_weight, key_weight, value_weight], third
    )
    return (
        output[None],
        input_grad[None],
        dquery,
        dkey,
        dvalue,
        dout,
        *hidden[:3],
        dgain_attn[0],
        hidden[3][0],
    )


def solution(mesh):
    rows, weights, vector = P(("grp", "wsh"), "ctx", None), P("wsh", None), P("wsh")
    in_specs = (rows, P(("grp", "wsh"))) + (weights,) * 7 + (vector,) * 2 + (rows,)
    out_specs = (rows,) * 2 + (weights,) * 7 + (vector,) * 2
    return jax.shard_map(
        on_device, mesh=mesh, in_specs=in_specs, out_specs=out_specs, check_vma=False
    )
```

```python
import functools

import jax
import jax.numpy as jnp
from jax import lax
from jax.experimental import pallas as pl
from jax.experimental.pallas import tpu as pltpu
from jax.sharding import PartitionSpec as P

D = 768
HEAD_DIM = 64
PAIR = 2 * HEAD_DIM
EPSILON = 1e-06
DEAD = -1e30

F32 = jnp.float32
BF = jnp.bfloat16
NN = (((1,), (0,)), ((), ()))
NT = (((1,), (1,)), ((), ()))
SMEM = pl.BlockSpec(memory_space=pltpu.SMEM)
LOCAL = pl.BlockSpec(memory_space=pltpu.VMEM)
FAR = pl.BlockSpec(memory_space=pltpu.HBM)
ANYWHERE = pl.BlockSpec(memory_space=pl.ANY)


def mm(left, right, dims):
    return lax.dot_general(left, right, dims, preferred_element_type=F32)


class Load:
    def __init__(self, pieces, dims=None, arrived=()):
        self.pieces = pieces if isinstance(pieces, list) else [(pieces, None, None)]
        self.arrived = arrived
        first = self.pieces[0][0]
        self.dims, self.dtype = dims or first.shape, first.dtype


class Choice(Load):
    def __init__(self, pair, holder, rows):
        self.pieces = [(pair[0], None, None), (pair[1], None, None)]
        self.dims, self.dtype = (rows.stop - rows.start, pair[0].shape[1]), pair[0].dtype
        self.arrived = (1,)
        self.holder, self.rows = holder, rows


class Store:
    def __init__(self, dims, dtype, columns=None):
        self.shape = shape(dims, dtype)
        self.columns = columns
        self.dims = dims if columns is None else (dims[0], columns.stop - columns.start)


AHEAD = 4
LONG, SHORT = 10**11, 2 * 10**10


class Spread(Store):
    def __init__(self, dims, dtype, parts):
        self.shape, self.parts = shape(dims, dtype), parts


class Arriving:
    def __init__(self, ref, starts, waits, queue):
        self.ref, self.starts, self.waits, self.queue = ref, starts, waits, queue
        self.shape, self.place = ref.shape, len(queue)
        queue.append(self)

    def begin(self):
        for start in self.starts:
            start()
        self.starts = []

    def ready(self):
        if self.waits:
            for value in self.queue[: self.place + 1 + AHEAD]:
                value.begin()
            for copy in self.waits:
                copy.wait()
            self.waits = []
        return self.ref

    def __getitem__(self, index):
        return self.ready()[index]


class Leaving:
    def __init__(self, ref, target, sem):
        self.ref, self.target, self.sem, self.started = ref, target, sem, False
        self.copy = pltpu.make_async_copy(ref, target, sem)
        self.shape = ref.shape

    def ready(self):
        return self.ref

    def send_lanes(self, here):
        pltpu.make_async_copy(self.ref.at[:, here], self.target.at[:, here], self.sem).start()
        self.started = True

    def __getitem__(self, index):
        return self.ref[index]

    def __setitem__(self, index, value):
        self.ref[index] = value

    def send(self):
        if not self.started:
            self.copy.start()
        self.started = True


def placed(ref, index):
    return ref if index is None else ref.at[index]


def call(body, inputs, outs, vmem, name, scratch=(), aliases=(), near=False):
    arrays, in_specs, loads, copies, plan = [], [], [], 0, []
    for value in inputs:
        if isinstance(value, Load):
            plan.append(len(loads))
            loads.append(value)
            for i, piece in enumerate(value.pieces):
                arrived = i in value.arrived
                arrays.append(piece[0] if arrived else pltpu.with_memory_space_constraint(piece[0], pltpu.HBM))
                in_specs.append(ANYWHERE if arrived else FAR)
            copies += len(value.pieces)
        else:
            plan.append(None)
            pinned = near and value.dtype != jnp.int32
            arrays.append(pltpu.with_memory_space_constraint(value, pltpu.VMEM) if pinned else value)
            in_specs.append(SMEM if value.dtype == jnp.int32 else LOCAL)
    count = len(arrays)
    arrays += [pltpu.with_memory_space_constraint(value, pltpu.HBM) for value in aliases]
    in_specs += [FAR] * len(aliases)
    stores = [out for out in outs if isinstance(out, Store)]
    out_shape = [
        pltpu.HBM(out.shape.shape, out.shape.dtype)
        if isinstance(out, Store)
        else pltpu.VMEM(out.shape, out.dtype) if near else out
        for out in outs
    ]
    out_specs = [
        FAR if isinstance(out, Store) else LOCAL for out in outs
    ]
    own_scratch = [pltpu.VMEM(load.dims, load.dtype) for load in loads]
    homes_of = [
        [dims for dims, _ in store.parts] if isinstance(store, Spread) else [store.dims] for store in stores
    ]
    own_scratch += [pltpu.VMEM(dims, store.shape.dtype) for store, group in zip(stores, homes_of) for dims in group]
    copies += sum(len(group) for group in homes_of)
    sems = [pltpu.SemaphoreType.DMA((copies,))] if copies else []

    def kernel(*refs):
        ins, results = refs[:count], refs[len(arrays) : len(arrays) + len(outs)]
        rest = list(refs[len(arrays) + len(outs) :])
        homes, sem = rest[: len(own_scratch)], rest[len(own_scratch)] if sems else None
        extra = rest[len(own_scratch) + len(sems) :]
        given, queue, at, number = [], [], 0, 0
        for index in plan:
            if index is None:
                given.append(ins[at])
                at += 1
                continue
            load, home, starts, waits = loads[index], homes[index], [], []
            if isinstance(load, Choice):
                copies_of = [pltpu.make_async_copy(ins[at + i].at[load.rows, :], home, sem.at[number]) for i in (0, 1)]

                def start(copies_of=copies_of, holder=load.holder):
                    for i, copy in enumerate(copies_of):
                        pl.when((given[0][0] == holder) == (i == 0))(copy.start)

                starts, waits = [start], [copies_of[0]]
                at, number = at + 2, number + 2
            else:
                for _, source, target in load.pieces:
                    copy = pltpu.make_async_copy(
                        placed(ins[at], source and source(given[0])),
                        placed(home, target and target(given[0])),
                        sem.at[number],
                    )
                    starts.append(copy.start)
                    waits.append(copy)
                    at, number = at + 1, number + 1
            given.append(Arriving(home, starts, waits, queue))
        for value in queue[: 1 + AHEAD]:
            value.begin()
        leaving, made = [], []
        for out, result in zip(outs, results):
            if isinstance(out, Spread):
                group = []
                for _, place in out.parts:
                    home = homes[len(loads) + len(leaving)]
                    leaving.append(Leaving(home, result.at[place], sem.at[number]))
                    group.append(leaving[-1])
                    number += 1
                made.append(group)
            elif isinstance(out, Store):
                home = homes[len(loads) + len(leaving)]
                target = result if out.columns is None else result.at[:, out.columns]
                leaving.append(Leaving(home, target, sem.at[number]))
                made.append(leaving[-1])
                number += 1
            else:
                made.append(result)
        body(*given, *made, *extra)
        for value in queue:
            value.ready()
        for value in leaving:
            value.send()
        for value in leaving:
            value.copy.wait()

    results = [out.shape if isinstance(out, Store) else out for out in outs]
    moved = sum(value.size * value.dtype.itemsize for value in arrays + results)
    return pl.pallas_call(
        kernel,
        in_specs=in_specs,
        out_specs=out_specs,
        out_shape=out_shape,
        scratch_shapes=own_scratch + sems + list(scratch),
        input_output_aliases={count + i: i for i in range(len(aliases))},
        compiler_params=pltpu.CompilerParams(vmem_limit_bytes=vmem << 20),
        cost_estimate=pl.CostEstimate(flops=SHORT if near else LONG, bytes_accessed=moved, transcendentals=0),
        name=name,
    )(*arrays)


def joined_halves(pair, columns=slice(None)):
    half = pair[0].shape[0]
    pieces = []
    for array, mine in zip(pair, (True, False)):

        def into(core_ref, mine=mine):
            start = (core_ref[0] if mine else 1 - core_ref[0]) * half
            return (pl.ds(pl.multiple_of(start, half), half), slice(None))

        pieces.append((array, lambda core_ref: (slice(None), columns), into))
    start, stop, _ = columns.indices(pair[0].shape[1])
    return Load(pieces, (2 * half, stop - start), arrived=(1,))


def shape(dims, dtype):
    return jax.ShapeDtypeStruct(dims, dtype)


def rms_scale(values):
    return lax.rsqrt(jnp.mean(values * values, axis=-1, keepdims=True) + EPSILON)


def stack(core, own, other):
    return jnp.concatenate(
        [jnp.where(core == 0, own, other), jnp.where(core == 0, other, own)], axis=0
    )


def gain_row(core, own, other, index):
    own = own[index : index + 1, :].astype(F32)
    other = other[index : index + 1, :].astype(F32)
    return jnp.concatenate(
        [jnp.where(core == 0, own, other), jnp.where(core == 0, other, own)], axis=1
    )


def lanes(step, size):
    return pl.ds(pl.multiple_of(step * size, size), size)


def project_kernel(count, core_ref, gain_own, gain_other, x_ref, *refs):
    weights, outs = refs[:count], refs[count:]
    gain = gain_row(core_ref[0], gain_own[...], gain_other[...], 0)
    x = x_ref[...].astype(F32)
    outs[0][...] = (x * rms_scale(x) * gain).astype(BF)
    outs[0].send()
    normed = outs[0][...]
    for i in range(count):
        outs[1 + i][...] = mm(normed, weights[i][...], NN).astype(BF)
        outs[1 + i].send()


def project(core, x, gains, weights):
    count = len(weights)
    return call(
        functools.partial(project_kernel, count),
        [core, *gains, Load(x)] + [joined_halves(pair) for pair in weights],
        [Store(x.shape, BF) for _ in range(1 + count)],
        14 if x.shape[0] <= 512 else 48,
        "project",
    )


def split3(value):
    high = value.astype(BF).astype(F32)
    rest = value - high
    mid = rest.astype(BF).astype(F32)
    return high, mid, rest - mid


def key_extra(limit, rows):
    lane = lax.broadcasted_iota(jnp.int32, (rows, PAIR), 1) % HEAD_DIM
    row = lax.broadcasted_iota(jnp.int32, (rows, PAIR), 0)
    bias = jnp.where(row < limit, 0.0, DEAD)
    return jnp.where(lane < 3, 1.0, jnp.where(lane == 3, bias, 0.0)).astype(BF)


def block_of(step, rows):
    return pl.ds(pl.multiple_of(step * rows, rows), rows)


def place3(lane, base, parts, into):
    for i in (2, 1, 0):
        into = jnp.where(lane == base + i, parts[i], into)
    return into


def attend_block(limit, queries, bias_lane, keys, values, lane, earlier):
    rows = queries.shape[0]
    extra = key_extra(limit, rows)
    ones = jnp.ones((rows, PAIR), BF)
    results = []
    for head in range(2):
        mine = lane // HEAD_DIM == head
        scores = mm(jnp.where(mine, queries, bias_lane), jnp.where(mine, keys, extra), NT)
        top = jnp.max(scores, axis=-1, keepdims=True)
        if earlier is not None:
            top = jnp.maximum(top, earlier[head][1])
        weights = jnp.exp(scores - top).astype(BF)
        total = mm(weights, jnp.where(mine, values, ones), NN)
        if earlier is not None:
            total = total + earlier[head][0] * jnp.exp(earlier[head][1] - top)
        results.append((total, top))
    return results


def scaled_queries(q_ref, here):
    queries = q_ref[:, here] * jnp.asarray(HEAD_DIM**-0.5, BF)
    lane = lax.broadcasted_iota(jnp.int32, queries.shape, 1)
    return queries, jnp.where(lane % HEAD_DIM == 3, 1.0, 0.0).astype(BF), lane


def attend_own_kernel(limits_ref, q_ref, k_ref, v_ref, first_ref, second_ref, top_ref):
    top_ref[...] = jnp.zeros_like(top_ref.ref)
    for ref in (q_ref, k_ref, v_ref):
        ref.ready()

    @pl.loop(0, D // PAIR, unroll=2)
    def _(pair):
        here = lanes(pair, PAIR)
        queries, bias_lane, lane = scaled_queries(q_ref, here)
        heads = attend_block(limits_ref[0], queries, bias_lane, k_ref[:, here], v_ref[:, here], lane, None)
        first_ref[:, here], second_ref[:, here] = heads[0][0], heads[1][0]
        first_ref.send_lanes(here)
        second_ref.send_lanes(here)
        tops = top_ref[...]
        for head in range(2):
            tops = jnp.where(lane == 2 * pair + head, heads[head][1], tops)
        top_ref[...] = tops


def attend_own(limits, queries, keys, values):
    rows = queries.shape[0]
    return call(
        attend_own_kernel,
        [limits, Load(queries), Load(keys), Load(values)],
        [Store((rows, D), F32), Store((rows, D), F32), Store((rows, PAIR), F32)],
        16,
        "attend_own",
    )


def own_rows_kernel(core_ref, limits_ref, gain_own, gain_other, x_ref, wq, wk, wv, h1, q, k, v, *partial):
    project_kernel(3, core_ref, gain_own, gain_other, x_ref, wq, wk, wv, h1, q, k, v)
    attend_own_kernel(limits_ref, q, k, v, *partial)


def own_rows(core, limits, x, gains, weights):
    rows = x.shape[0]
    results = call(
        own_rows_kernel,
        [core, limits, *gains, Load(x)] + [joined_halves(pair) for pair in weights],
        [Store((rows, D), BF) for _ in range(4)]
        + [Store((rows, D), F32), Store((rows, D), F32), Store((rows, PAIR), F32)],
        22,
        "own_rows",
    )
    return results[:4], results[4:]


def attend_rest_kernel(limits_ref, q_ref, k_ref, v_ref, first_ref, second_ref, top_ref, wide_ref, low_ref, extra_ref):
    for ref in (q_ref, k_ref, v_ref, first_ref, second_ref, top_ref):
        ref.ready()
    rows = q_ref.shape[0]
    blocks = k_ref.shape[0] // rows

    @pl.loop(0, D // PAIR, unroll=2)
    def _(pair):
        here = lanes(pair, PAIR)
        queries, bias_lane, lane = scaled_queries(q_ref, here)
        tops = top_ref[...]
        heads = [
            (ref[:, here], jnp.sum(jnp.where(lane == 2 * pair + i, tops, 0.0), axis=-1, keepdims=True))
            for i, ref in enumerate((first_ref, second_ref))
        ]

        def more(block, heads):
            place = block_of(block, rows)
            return attend_block(
                limits_ref[1 + block], queries, bias_lane, k_ref[place, here], v_ref[place, here], lane, heads
            )

        heads = more(0, heads) if blocks == 1 else lax.fori_loop(0, blocks, more, heads)
        log_lanes = jnp.where(lane % HEAD_DIM == 3, 1.0, 0.0)
        outs = []
        for head, (total, top) in enumerate(heads):
            outs.append(total / pltpu.roll(total, HEAD_DIM, 1))
            log_lanes = place3(
                lane, HEAD_DIM * (1 - head), split3(-(top + jnp.log(total))), log_lanes
            )
        attended = jnp.where(lane < HEAD_DIM, outs[0], outs[1])
        wide_ref[:, here] = attended
        low_ref[:, here] = attended.astype(BF)
        extra_ref[:, here] = log_lanes.astype(BF)
        for ref in (wide_ref, low_ref, extra_ref):
            ref.send_lanes(here)


def attend_rest(limits, queries, keys, values, partial):
    rows = queries.shape[0]
    return call(
        attend_rest_kernel,
        [limits, Load(queries), Load(keys), Load(values)] + [Load(value) for value in partial],
        [Store((rows, D), F32), Store((rows, D), BF), Store((rows, D), BF)],
        18 if keys.shape[0] == rows else 40,
        "attend_rest",
    )


def attend_back_kernel(count, limits_ref, q_ref, dmb_ref, wo_ref, low_ref, wide_ref, extra_ref, *refs):
    inputs, outs = refs[:4], refs[4:]
    dq_ref, grad_refs, out_ref = outs[0], outs[1:5], outs[5]
    rows = q_ref.shape[0]
    scale = jnp.asarray(HEAD_DIM**-0.5, BF)
    lane = lax.broadcasted_iota(jnp.int32, (rows, PAIR), 1)
    none = jnp.zeros((rows, PAIR), BF)
    for ref in (q_ref, dmb_ref, low_ref, wide_ref, extra_ref, *inputs):
        ref.ready()

    @pl.loop(0, count)
    def _(pair):
        here = lanes(pair, PAIR)
        queries = q_ref[:, here] * scale
        dmb = dmb_ref[...]
        grads = mm(dmb, wo_ref[here, :], NT).astype(BF)
        out_ref[here, :] = mm(low_ref[:, here].T, dmb, NN).astype(BF)
        log_lanes = extra_ref[:, here]
        product = grads.astype(F32) * wide_ref[:, here]
        delta_lanes = jnp.zeros((rows, PAIR), F32)
        for head in range(2):
            mine = lane // HEAD_DIM == head
            delta = -jnp.sum(jnp.where(mine, product, 0.0), axis=-1, keepdims=True)
            delta_lanes = place3(lane, HEAD_DIM * (1 - head), split3(delta), delta_lanes)
        delta_lanes = delta_lanes.astype(BF)

        def over(limit, k_ref, v_ref, dk_ref, dv_ref, place):
            keys, values = k_ref[place, here], v_ref[place, here]
            extra = key_extra(limit, rows)
            keys_turned = (keys * scale).T
            dk = dv = 0.0
            dqs = []
            for head in range(2):
                mine = lane // HEAD_DIM == head
                probs = jnp.exp(
                    mm(jnp.where(mine, keys, extra), jnp.where(mine, queries, log_lanes), NT)
                )
                shifted = mm(
                    jnp.where(mine, values, extra), jnp.where(mine, grads, delta_lanes), NT
                )
                dscores = (probs * shifted).astype(BF)
                dv = dv + mm(probs.astype(BF), jnp.where(mine, grads, none), NN)
                dk = dk + mm(dscores, jnp.where(mine, queries, none), NN)
                dqs.append(mm(keys_turned[head * HEAD_DIM : (head + 1) * HEAD_DIM], dscores, NN))
            dk_ref[place, here] = dk.astype(BF)
            dv_ref[place, here] = dv.astype(BF)
            return jnp.concatenate(dqs, axis=0)

        k_own, k_rest, v_own, v_rest = inputs
        dk_own, dk_rest, dv_own, dv_rest = grad_refs
        dq = over(limits_ref[0], k_own, v_own, dk_own, dv_own, slice(None))
        blocks = k_rest.shape[0] // rows

        def more(block, dq):
            return dq + over(limits_ref[1 + block], k_rest, v_rest, dk_rest, dv_rest, block_of(block, rows))

        dq = more(0, dq) if blocks == 1 else lax.fori_loop(0, blocks, more, dq)
        dq_ref[:, here] = dq.T.astype(BF)
        for ref in (dq_ref, *grad_refs):
            ref.send_lanes(here)


def attend_back_inputs(queries, keys, values, dmb, wide, low, extra, out_weight, first, count):
    columns = slice(first * PAIR, (first + count) * PAIR)
    half = D // PAIR // 2

    def part(value):
        dims = (value.shape[0], columns.stop - columns.start)
        return Load([(value, lambda core_ref: (slice(None), columns), None)], dims)

    rows_of = [
        Choice(out_weight, pair // half, slice(pair % half * PAIR, (pair % half + 1) * PAIR))
        for pair in range(first, first + count)
    ]
    loads = [part(queries), Load(dmb)] + rows_of + [part(low), part(wide), part(extra)]
    return loads + [part(value) for value in (keys[0], values[0], keys[1], values[1])], columns


def attend_back_body(count, core_ref, limits_ref, refs, turned_wo):
    q_ref, dmb_ref, wo_refs, rest = refs[0], refs[1], refs[2 : 2 + count], refs[2 + count :]
    for i, ref in enumerate(wo_refs):
        turned_wo[i * PAIR : (i + 1) * PAIR, :] = ref[...]
    low_ref, wide_ref, extra_ref, k_own, v_own, k_rest, v_rest = rest[:7]
    attend_back_kernel(
        count, limits_ref, q_ref, dmb_ref, turned_wo, low_ref, wide_ref, extra_ref, k_own, k_rest, v_own, v_rest, *rest[7:]
    )


def attend_back(core, limits, queries, keys, values, dmb, wide, low, extra, out_weight, first, count, earlier):
    rows, rest = queries.shape[0], keys[1].shape[0]
    loads, columns = attend_back_inputs(queries, keys, values, dmb, wide, low, extra, out_weight, first, count)

    def body(core_ref, limits_ref, *refs):
        attend_back_body(count, core_ref, limits_ref, refs[:-1], refs[-1])

    return call(
        body,
        [core, limits] + loads,
        [Store((size, D), BF, columns) for size in (rows, rows, rest, rows, rest)]
        + [Store((columns.stop - columns.start, D), BF)],
        20 if rest == rows else 48,
        "attend_back",
        [pltpu.VMEM((count * PAIR, D), BF)],
        aliases=earlier,
    )


CURVE = 0.7978845608028654
CUBIC = 0.044715


def ffn_part(part, core, step, h2_ref, turned, dyb, dyb_turned, weights, own_ref, other_ref, acc_out, acc_back):
    wide, half = own_ref.shape[1] // 2, D // 2
    here, there = lanes(step, wide), lanes(part + 2 * step, wide)
    gate_ref, up_ref, down_ref = weights
    rows = block_of(part + 2 * step, wide)
    gate = mm(h2_ref[...], gate_ref[:, there], NN)
    up = mm(h2_ref[...], up_ref[:, there], NN)
    dn = mm(dyb[...], down_ref[rows, :], NT)
    square = gate * gate
    bent = jnp.tanh(CURVE * gate * (1.0 + CUBIC * square))
    rise = 0.5 * (1.0 + bent)
    bulge = gate * rise
    slope = rise + 0.5 * gate * (1.0 - bent * bent) * (CURVE * (1.0 + 3.0 * CUBIC * square))
    hidden = (bulge * up).astype(BF)
    dgate = (dn * up * slope).astype(BF)
    dup = (dn * bulge).astype(BF)
    ddown = mm(dyb_turned[...], hidden, NN).astype(BF)

    @pl.when(step == core)
    def _():
        own_ref[2 * half :, :wide] = ddown[:half]
        own_ref[2 * half :, wide:] = ddown[half:]

    @pl.when(step != core)
    def _():
        other_ref[2 * half :, :wide] = ddown[:half]
        other_ref[2 * half :, wide:] = ddown[half:]

    dgate_term = mm(turned[...], dgate, NN).astype(BF)
    dup_term = mm(turned[...], dup, NN).astype(BF)
    for i, term in ((0, dgate_term), (1, dup_term)):
        place = slice(i * half, (i + 1) * half)
        own_ref[place, here] = jnp.where(core == 0, term[:half], term[half:])
        other_ref[place, here] = jnp.where(core == 0, term[half:], term[:half])
    acc_back[...] += mm(dgate, gate_ref[:, there], NT) + mm(dup, up_ref[:, there], NT)
    acc_out[...] += mm(hidden, down_ref[rows, :], NN)


def live_grad(limits_ref, grad_ref):
    rows = grad_ref.shape[0]
    live = lax.broadcasted_iota(jnp.int32, (rows, D), 0) < limits_ref[0]
    return jnp.where(live, grad_ref[...].astype(F32), 0.0)


def ffn_body(core_ref, limits_ref, gain_own, gain_other, a_ref, wo_ref, x_ref, grad_ref, weights, outs, scratch, m_ref, acc_out):
    core = core_ref[0]
    output_ref, dm_ref, dmb_ref, *grads = outs
    h2_ref, turned, dyb, dyb_turned = scratch
    acc_back = dm_ref.ref
    m = mm(a_ref[...], wo_ref[...], NN) + x_ref[...].astype(F32)
    gain = gain_row(core, gain_own[...], gain_other[...], 1)
    m_ref[...] = m
    h2 = (m * rms_scale(m) * gain).astype(BF)
    h2_ref[...] = h2
    turned[...] = h2.T
    low = live_grad(limits_ref, grad_ref).astype(BF)
    dyb[...] = low
    dyb_turned[...] = low.T
    acc_out[...] = jnp.zeros_like(acc_out)
    acc_back[...] = jnp.zeros_like(acc_back)
    for ref in weights:
        ref.ready()
    for part in range(2):

        @pl.loop(0, 2)
        def _(step):
            ffn_part(
                part, core, step, h2_ref, turned, dyb, dyb_turned, weights, *grads[2 * part : 2 * part + 2], acc_out, acc_back
            )

        grads[2 * part + 1].send()
        grads[2 * part].send()
    m = m_ref[...]
    scale = rms_scale(m)
    scaled = acc_back[...] * gain
    dm = dyb[...].astype(F32) + scale * scaled - m * (scale * scale * scale) * jnp.mean(
        scaled * m, axis=-1, keepdims=True
    )
    dmb_ref[...] = dm.astype(BF)
    dmb_ref.send()
    dm_ref[...] = dm
    dm_ref.send()
    output_ref[...] = (m + acc_out[...]).astype(BF)


def ffn_results(rows, hidden):
    outs = [Store((rows, D), BF), Store((rows, D), F32), Store((rows, D), BF)]
    scratch = [pltpu.VMEM((rows, D), BF), pltpu.VMEM((D, rows), BF), pltpu.VMEM((rows, D), BF), pltpu.VMEM((D, rows), BF)]
    return outs + [Store((3 * D // 2, hidden // 2), BF) for _ in range(4)], scratch


def feed_forward(core, limits, x, attended, out_weight, gains, grad, weights):
    rows, hidden = x.shape[0], weights[0][0].shape[1]
    outs, scratch = ffn_results(rows, hidden)

    def body(core_ref, limits_ref, gain_own, gain_other, a, wo, x, grad, *refs):
        ffn_body(core_ref, limits_ref, gain_own, gain_other, a, wo, x, grad, refs[:3], refs[3:10], refs[10:14], *refs[14:])

    return call(
        body,
        [core, limits, *gains, Load(attended), joined_halves(out_weight), Load(x), Load(grad)]
        + [joined_halves(pair) for pair in weights],
        outs,
        52,
        "feed_forward",
        scratch + [pltpu.VMEM((rows, D), F32)] * 2,
    )


def middle_kernel(core_ref, limits_ref, gain_own, gain_other, x_rest, wk, wv, q, first, second, top, wo, x, grad, *refs):
    weights, outs = refs[:3], refs[3:]
    h1_rest, k_rest, v_rest, wide, low, extra = outs[:6]
    project_kernel(2, core_ref, gain_own, gain_other, x_rest, wk, wv, h1_rest, k_rest, v_rest)
    for ref in (q, first, second, top, wo, x, grad, *weights):
        ref.begin()
    attend_rest_kernel(limits_ref, q, k_rest, v_rest, first, second, top, wide, low, extra)
    ffn_body(
        core_ref, limits_ref, gain_own, gain_other, low, wo, x, grad, weights, outs[6:13], outs[13:], first.ref, second.ref
    )


def middle(core, limits, gains, x, x_rest, key_value, queries, partial, out_weight, grad, weights):
    rows, hidden = x.shape[0], weights[0][0].shape[1]
    low, full = ((rows, D), BF), ((rows, D), F32)
    ffn_outs, scratch = ffn_results(rows, hidden)
    results = call(
        middle_kernel,
        [core, limits, *gains, x_rest]
        + [joined_halves(pair) for pair in key_value]
        + [Load(queries)]
        + [Load(value) for value in partial]
        + [joined_halves(out_weight), Load(x), Load(grad)]
        + [joined_halves(pair) for pair in weights],
        [Store(*dims) for dims in (low, low, low, full, low, low)] + ffn_outs,
        49,
        "middle",
        scratch,
    )
    return results[:3], results[3:6], results[6:]


def project_grads_kernel(core_ref, own_normed, dq_ref, rest_normed, dk_own, dk_rest, dv_own, dv_rest, *refs):
    core = core_ref[0]
    out_terms, (own_ref, other_ref) = refs[:-2], refs[-2:]
    half = D // 2

    def put(i, term):
        own_ref[i * half : (i + 1) * half, :] = jnp.where(core == 0, term[:half], term[half:])
        other_ref[i * half : (i + 1) * half, :] = jnp.where(core == 0, term[half:], term[:half])

    turned = own_normed[...].T
    put(0, mm(turned, dq_ref[...], NN).astype(BF))
    turned_rest = rest_normed[...].T
    put(1, (mm(turned, dk_own[...], NN) + mm(turned_rest, dk_rest[...], NN)).astype(BF))
    put(2, (mm(turned, dv_own[...], NN) + mm(turned_rest, dv_rest[...], NN)).astype(BF))
    put(3, jnp.concatenate([term[...] for term in out_terms], axis=0))


def project_grads(core, normed, dq, dks, dvs, out_terms):
    total = dks[0].shape[0] + dks[1].shape[0]
    arrays = (normed[0], dq, normed[1], *dks, *dvs, *out_terms)
    return call(
        project_grads_kernel,
        [core] + [Load(value) for value in arrays],
        [Store((2 * D, D), BF) for _ in range(2)],
        18 if total <= 1024 else 54,
        "project_grads",
    )


def last_piece(core, limits, queries, keys, values, dmb, wide, low, extra, out_weight, first, count, earlier, out_terms, normed):
    rows, rest = queries.shape[0], keys[1].shape[0]
    loads, columns = attend_back_inputs(queries, keys, values, dmb, wide, low, extra, out_weight, first, count)
    done = slice(0, columns.start)
    inputs = len(loads)

    def before(value):
        return Load([(value, lambda core_ref: (slice(None), done), None)], (value.shape[0], done.stop))

    more = [Load(normed[0]), before(earlier[0]), Load(normed[1])]
    more += [before(value) for value in earlier[1:]] + [Load(term) for term in out_terms]

    def body(core_ref, limits_ref, *refs):
        ins, given, outs, wo, out_term = refs[:inputs], refs[inputs : inputs + len(more)], refs[-9:-4], refs[-2], refs[-1]
        own_ref, other_ref = refs[-4:-2]
        attend_back_body(count, core_ref, limits_ref, (*ins, *outs, out_term), wo)

        def both_parts(left, right):
            return jnp.concatenate([left[...], right[...]], axis=1)

        merged = [both_parts(left, right) for left, right in zip((given[1], *given[3:7]), outs)]
        project_grads_kernel(
            core_ref, given[0], merged[0], given[2], *merged[1:], *given[7:], out_term, own_ref, other_ref
        )

    width = columns.stop - columns.start
    return call(
        body,
        [core, limits] + loads + more,
        [Store((size, width), BF) for size in (rows, rows, rest, rows, rest)] + [Store((2 * D, D), BF) for _ in range(2)],
        36,
        "last_piece",
        [pltpu.VMEM((count * PAIR, D), BF)] * 2,
    )


def project_back_kernel(core_ref, dk_rest, key, dv_rest, value, dq_ref, query, dk_own, dv_own, rest_ref, own_ref):
    rows = dq_ref.shape[0]
    for ref in (dk_rest, key, dv_rest, value):
        ref.ready()

    def rest(block, _):
        place = block_of(block, rows)
        back = mm(dk_rest[place, :], key[...], NT) + mm(dv_rest[place, :], value[...], NT)
        rest_ref[place, :] = back.astype(BF)
        return _

    blocks = dk_rest.shape[0] // rows
    rest(0, 0) if blocks == 1 else lax.fori_loop(0, blocks, rest, 0)
    rest_ref.send()
    own_ref[...] = (
        mm(dq_ref[...], query[...], NT) + mm(dk_own[...], key[...], NT) + mm(dv_own[...], value[...], NT)
    )


def project_back(core, dq, dks, dvs, weights):
    query, key, value = (joined_halves(pair) for pair in weights)
    total = dks[0][0].shape[0] + dks[1][0].shape[0]

    def side_by_side(parts):
        pieces, start = [], 0
        for i, part in enumerate(parts):
            width = D - start if i == len(parts) - 1 else D - parts[-1].shape[1]
            columns = slice(start, start + width)
            take = None if part.shape[1] == width else (lambda core_ref, columns=columns: (slice(None), columns))
            pieces.append((part, take, lambda core_ref, columns=columns: (slice(None), columns)))
            start += width
        return Load(pieces, (parts[0].shape[0], D))

    dq_load, (dk_own, dk_rest), (dv_own, dv_rest) = side_by_side(dq), map(side_by_side, dks), map(side_by_side, dvs)
    return call(
        project_back_kernel,
        [core, dk_rest, key, dv_rest, value, dq_load, query, dk_own, dv_own],
        [Store((total - dq[0].shape[0], D), BF), Store((dq[0].shape[0], D), F32)],
        20 if total <= 1024 else 40,
        "project_back",
    )


def input_grad_kernel(core_ref, gain_own, gain_other, x_ref, dm_ref, own_ref, *refs):
    x = x_ref[...].astype(F32)
    scale = rms_scale(x)
    back = own_ref[...]
    for ref in refs[:-1]:
        back = back + ref[...].astype(F32)
    scaled = back * gain_row(core_ref[0], gain_own[...], gain_other[...], 0)
    refs[-1][...] = (
        dm_ref[...]
        + scale * scaled
        - x * (scale * scale * scale) * jnp.mean(scaled * x, axis=-1, keepdims=True)
    ).astype(BF)


def input_grad_of(core, gains, x, dm, own, received):
    return call(
        input_grad_kernel,
        [core, *gains] + [Load(value) for value in (x, dm, own)] + [Load(value, arrived=(0,)) for value in received],
        [Store(x.shape, BF)],
        14 if len(received) == 1 else 24,
        "input_grad",
    )[0]


def swap(value, axis, mask):
    count = lax.axis_size(axis)
    return lax.ppermute(value, axis, [(i, i ^ mask) for i in range(count)])


def tie(values, *earlier):
    return lax.optimization_barrier((values, earlier))[0]


def fold_kernel(count, bits_ref, *refs):
    outs = refs[2 * count :]
    for i in range(count):
        own, got = refs[2 * i], refs[2 * i + 1]
        half = own.shape[0] // 2
        for j, bit in ((0, bits_ref[i]), (1, 1 - bits_ref[i])):
            here = pl.ds(pl.multiple_of(bit * half, 16), half)
            outs[2 * i + j][...] = (own[here, :].astype(F32) + got[here, :].astype(F32)).astype(BF)


def paired(owns, gots):
    return [part for pair in zip(owns, gots) for part in pair]


def fold(bits, owns, gots):
    outs = [shape((own.shape[0] // 2, own.shape[1]), BF) for own in owns for _ in range(2)]
    results = call(
        functools.partial(fold_kernel, len(owns)),
        [bits] + paired(owns, gots),
        outs,
        3,
        "fold",
        near=True,
    )
    return results[0::2], results[1::2]


def fold_far(bits, own, got):
    rows, cols = own.shape
    half, parts = rows // 2, 3
    size = half // parts
    inputs = []
    for i in range(2 * parts):
        for value in (own, got):

            def here(bits_ref, i=i):
                bit = bits_ref[0] if i < parts else 1 - bits_ref[0]
                return (pl.ds(pl.multiple_of(bit * half + i % parts * size, 16), size), slice(None))

            inputs.append(Load([(value, here, None)], (size, cols), arrived=(0,) if value is got else ()))

    def body(bits_ref, *refs):
        ins, (sent, kept) = refs[:-2], refs[-2:]
        for i in range(2 * parts):
            out = kept if i < parts else sent
            place = slice(i % parts * size, (i % parts + 1) * size)
            out[place, :] = (ins[2 * i][...].astype(F32) + ins[2 * i + 1][...].astype(F32)).astype(BF)

    sent, kept = call(
        body, [bits] + inputs, [shape((half, cols), BF)] * 2, 14, "fold_far"
    )
    return [kept], [sent]


def add_kernel(count, *refs):
    for i in range(count):
        refs[2 * count + i][...] = (
            refs[2 * i][...].astype(F32) + refs[2 * i + 1][...].astype(F32)
        ).astype(BF)


def add(owns, gots):
    return call(
        functools.partial(add_kernel, len(owns)),
        paired(owns, gots),
        [shape(own.shape, BF) for own in owns],
        3,
        "add",
        near=True,
    )


def merge_kernel(count, bits_ref, *refs):
    for i in range(count):
        refs[2 * count + i][...] = stack(bits_ref[i], refs[2 * i][...], refs[2 * i + 1][...])


def merge(bits, owns, gots):
    return call(
        functools.partial(merge_kernel, len(owns)),
        [bits] + paired(owns, gots),
        [shape((2 * own.shape[0], own.shape[1]), BF) for own in owns],
        3,
        "merge",
        near=True,
    )


class Chain:
    def __init__(self, orders, owns, others):
        sizes = [lax.axis_size(axis) for axis in ("grp", "ctx", "wsh")]
        total = sizes[0] * sizes[1] * sizes[2]
        near = [2, 2 * sizes[1], 4 * sizes[1]]
        self.far, mask = [], 2
        while mask < total:
            if mask not in near:
                self.far.append(mask)
            mask *= 2
        here = (lax.axis_index("grp") * sizes[1] + lax.axis_index("ctx")) * 2 + lax.axis_index("wsh")
        self.total, self.near, self.orders = total, near, orders
        self.bits = []
        for stage in range(3):
            row = []
            for order in orders:
                one, two = near[order[0][stage]], near[order[1][stage]]
                mask = jnp.where(lax.axis_index("wsh") == 0, one, two)
                row.append((here // mask) % 2)
            self.bits.append(jnp.stack(row).astype(jnp.int32))
        self.count = 0
        self.kept = list(owns)
        self.got = [self.send(value, (1, 1)) for value in others]

    def send(self, value, masks):
        pairs = [(i, i ^ masks[i % 2]) for i in range(self.total)]
        return lax.ppermute(value, ("grp", "ctx", "wsh"), pairs)

    def send_near(self, values, stage):
        return [
            self.send(value, (self.near[order[0][stage]], self.near[order[1][stage]]))
            for value, order in zip(values, self.orders)
        ]

    def stages(self):
        return 3 + 1 + len(self.far) + 2

    def step(self, *earlier):
        stage, far = self.count, len(self.far)
        self.count += 1
        kept, got = tie((self.kept, self.got), *earlier)
        if stage < 3:
            far_away = stage == 0 and len(kept) == 1 and kept[0].shape[0] % 96 == 0
            self.kept, sent = fold_far(self.bits[0], kept[0], got[0]) if far_away else fold(self.bits[stage], kept, got)
            self.got = self.send_near(sent, stage)
            return sent
        if stage <= 3 + far:
            self.kept = add(kept, got)
            if stage < 3 + far:
                mask = self.far[stage - 3]
                self.got = [self.send(value, (mask, mask)) for value in self.kept]
            else:
                self.got = self.send_near(self.kept, 2)
            return self.kept
        back = 2 - (stage - 4 - far)
        self.kept = merge(self.bits[back], kept, got)
        self.got = self.send_near(self.kept, back - 1)
        return self.kept


def over_gain(total, gain):
    column = jnp.broadcast_to(jnp.sum(total, axis=1, keepdims=True), (total.shape[0], PAIR))
    return column.T[:1, :] / gain.astype(F32)


def ffn_finish(bits, gain, gate, up, part, chain, earlier, before):
    half, hidden = gate.shape
    wide = hidden // 4
    columns = [slice((part + 2 * j) * wide, (part + 2 * j + 1) * wide) for j in range(2)]

    def of(value):
        pieces = [
            (value, lambda bits_ref, c=c: (slice(None), c), lambda bits_ref, j=j: (slice(None), slice(j * wide, (j + 1) * wide)))
            for j, c in enumerate(columns)
        ]
        return Load(pieces, (half, 2 * wide))

    def body(bits_ref, gain_ref, kept, got, gate_ref, up_ref, *refs):
        dgate, dup, (ddown,), gain_out = refs[-4:]
        value = stack(bits_ref[0], kept[...], got[...])
        total = refs[0][...] if before else jnp.zeros((half, PAIR), F32)
        for i, (weight, outs) in enumerate(((gate_ref, dgate), (up_ref, dup))):
            term = value[i * half : (i + 1) * half].astype(F32)
            for j in range(2):
                outs[j][...] = term[:, j * wide : (j + 1) * wide]
                outs[j].send()
            product = term * weight[...].astype(F32)
            total = total + sum(product[:, k : k + PAIR] for k in range(0, 2 * wide, PAIR))
        for j in range(2):
            piece = value[2 * half :, j * wide : (j + 1) * wide]
            ddown[:, j * half : (j + 1) * half] = piece.T.astype(F32)
        gain_out[...] = over_gain(total, gain_ref[...]) if before else total

    kept, got = tie((chain.kept[0], chain.got[0]), earlier)
    wide_parts = [((half, wide), (slice(None), c)) for c in columns]
    down_part = [((wide, D), (slice(part * wide, (part + 1) * wide), slice(None)))]
    return call(
        body,
        [bits, gain, Load(kept, arrived=(0,)), Load(got, arrived=(0,)), of(gate), of(up)] + list(before[3:]),
        [Spread((half, hidden), F32, wide_parts) for _ in range(2)]
        + [Spread((2 * wide, D), F32, down_part), shape((1, half) if before else (half, PAIR), F32)],
        24,
        "ffn_finish",
        aliases=before[:3],
    )


def attention_finish_kernel(bits_ref, gain_ref, *refs):
    streams = len(refs) // 2 - 4
    weights, outs = refs[:3], refs[3 + 2 * streams :]
    value = jnp.concatenate(
        [stack(bits_ref[i], refs[3 + 2 * i][...], refs[4 + 2 * i][...]) for i in range(streams)], axis=0
    )
    half = D // 2
    total = jnp.zeros((half, PAIR), F32)
    for i in range(4):
        piece = value[i * half : (i + 1) * half].astype(F32)
        outs[i][...] = piece
        outs[i].send()
        if i < 3:
            product = piece * weights[i][...].astype(F32)
            total = total + sum(product[:, k : k + PAIR] for k in range(0, D, PAIR))
    outs[4][...] = over_gain(total, gain_ref[...])


def attention_finish(bits, gain, weights, chain):
    half = D // 2
    return call(
        attention_finish_kernel,
        [bits, gain]
        + [Load(value) for value in weights]
        + [Load(value, arrived=(0,)) for value in paired(chain.kept, chain.got)],
        [Store((half, D), F32)] * 4 + [shape((1, half), F32)],
        20,
        "attention_finish",
    )


ORDER = (1, 2, 3, "back", 1, 2, 1, 3, 2, "send", 1, 3, 2, 1, 3, 2, 1, 3, 2, 3, "input", "early", 3, "late")
AXES = (((0, 1, 2), (1, 0, 2)), ((2, 1, 0), (0, 2, 1)), ((0, 1, 2), (1, 2, 0)))
EARLY = ((1, (1, 2)),)


def on_device(
    tokens,
    lengths,
    query_weight,
    key_weight,
    value_weight,
    output_weight,
    gate_weight,
    up_weight,
    down_weight,
    attn_gain,
    ffn_gain,
    out_grad,
):
    blocks = lax.axis_size("ctx")
    x, grad = tokens[0], out_grad[0]
    rows = x.shape[0]
    place = lax.axis_index("ctx")
    core = lax.axis_index("wsh").astype(jnp.int32)[None]
    limits = jnp.clip(
        lengths[0] - rows * jnp.stack([place ^ r for r in range(blocks)]).astype(jnp.int32), 0, rows
    )

    def both(own):
        return (own, swap(own, "wsh", 1))

    wq, wk, wv = both(query_weight), both(key_weight), both(value_weight)
    gains = both(jnp.stack([attn_gain, ffn_gain]))
    others = [swap(x, "ctx", r) for r in range(1, blocks)]
    x_rest = others[0] if blocks == 2 else jnp.concatenate(others, axis=0)
    if blocks == 2:
        (h1, queries, key, value), partial = own_rows(core, limits, x, gains, [wq, wk, wv])
    else:
        h1, queries, key, value = project(core, x, gains, [wq, wk, wv])
        partial = attend_own(limits, queries, key, value)
    wo, wg, wu, wd = (
        both(tie(weight, wv[1])) for weight in (output_weight, gate_weight, up_weight, down_weight)
    )
    ffn_weights = (wg, wu, wd)
    if blocks == 2:
        rest, (wide, low, extra), results = middle(
            core, limits, gains, x, x_rest, [wk, wv], queries, partial, wo, grad, ffn_weights
        )
    else:
        rest = project(core, x_rest, gains, [wk, wv])
        wide, low, extra = attend_rest(limits, queries, *rest[1:], partial)
        results = feed_forward(core, limits, x, low, wo, gains, grad, ffn_weights)
    output, dm, dmb, *sums = results
    normed, keys, values = (h1, rest[0]), (key, rest[1]), (value, rest[2])
    first = Chain([AXES[0]], sums[:1], sums[1:2])
    second = Chain([AXES[1]], sums[2:3], sums[3:4])
    arrays = (core, limits, queries, keys, values)
    most, out_terms, token, first_pair = (), [], None, 0
    for count, steps in EARLY:
        ready = dmb if token is None else tie(dmb, token)
        *most, out_term = attend_back(*arrays, ready, wide, low, extra, wo, first_pair, count, most)
        out_terms.append(out_term)
        first_pair, token = first_pair + count, out_term
        for name in steps:
            token = (first, second)[name - 1].step(token)
    arrays += (tie(dmb, token), wide, low, extra, wo, first_pair, D // PAIR - first_pair)
    if blocks == 2:
        *final, own, other = last_piece(*arrays, most, out_terms, normed)
        grads = list(zip(most, final))
    else:
        *most, last_term = attend_back(*arrays, most)
        own, other = project_grads(core, normed, most[0], most[1:3], most[3:5], [*out_terms, last_term])
        grads = [(value,) for value in most]
    dq, dks, dvs = grads[0], grads[1:3], grads[3:5]
    third = Chain([AXES[2]], [own], [other])
    token = own
    received, chains, hidden = [], (first, second, third), ()
    for name in ORDER:
        if name == "back":
            back_rest, back_own = project_back(core, tie(dq, token), dks, dvs, [wq, wk, wv])
            token = back_own
        elif name == "send":
            sent = tie(back_rest, token)
            received = [
                swap(sent[(r - 1) * rows : r * rows] if blocks > 2 else sent, "ctx", r)
                for r in range(1, blocks)
            ]
        elif name == "input":
            token = input_grad = input_grad_of(core, gains, x, dm, tie(back_own, token), received)
        elif name in ("early", "late"):
            part = int(name == "late")
            chain = (first, second)[part]
            hidden = ffn_finish(
                chain.bits[0], ffn_gain[None], gate_weight, up_weight, part, chain, token, hidden
            )
            token = hidden[3]
        else:
            chain = chains[name - 1]
            for _ in range(1 + (len(chain.far) - 1) * (chain.count == 4)):
                token = chain.step(token)
    dquery, dkey, dvalue, dout, dgain_attn = attention_finish(
        third.bits[0], attn_gain[None], [query_weight, key_weight, value_weight], third
    )
    return (
        output[None],
        input_grad[None],
        dquery,
        dkey,
        dvalue,
        dout,
        *hidden[:3],
        dgain_attn.reshape(D // 2),
        hidden[3].reshape(D // 2),
    )


def solution(mesh):
    rows, weights, vector = P(("grp", "wsh"), "ctx", None), P("wsh", None), P("wsh")
    in_specs = (rows, P(("grp", "wsh"))) + (weights,) * 7 + (vector,) * 2 + (rows,)
    out_specs = (rows,) * 2 + (weights,) * 7 + (vector,) * 2
    return jax.shard_map(
        on_device, mesh=mesh, in_specs=in_specs, out_specs=out_specs, check_vma=False
    )
```

```python
import functools

import jax
import jax.numpy as jnp
from jax import lax
from jax.experimental import pallas as pl
from jax.experimental.pallas import tpu as pltpu
from jax.sharding import PartitionSpec as P

D = 768
HEAD_DIM = 64
PAIR = 2 * HEAD_DIM
EPSILON = 1e-06
DEAD = -1e30

F32 = jnp.float32
BF = jnp.bfloat16
NN = (((1,), (0,)), ((), ()))
NT = (((1,), (1,)), ((), ()))
SMEM = pl.BlockSpec(memory_space=pltpu.SMEM)
LOCAL = pl.BlockSpec(memory_space=pltpu.VMEM)
FAR = pl.BlockSpec(memory_space=pltpu.HBM)
ANYWHERE = pl.BlockSpec(memory_space=pl.ANY)


def mm(left, right, dims):
    return lax.dot_general(left, right, dims, preferred_element_type=F32)


class Load:
    def __init__(self, pieces, dims=None, arrived=()):
        self.pieces = pieces if isinstance(pieces, list) else [(pieces, None, None)]
        self.arrived = arrived
        first = self.pieces[0][0]
        self.dims, self.dtype = dims or first.shape, first.dtype


class Choice(Load):
    def __init__(self, pair, holder, rows):
        self.pieces = [(pair[0], None, None), (pair[1], None, None)]
        self.dims, self.dtype = (rows.stop - rows.start, pair[0].shape[1]), pair[0].dtype
        self.arrived = (1,)
        self.holder, self.rows = holder, rows


class Store:
    def __init__(self, dims, dtype, columns=None):
        self.shape = shape(dims, dtype)
        self.columns = columns
        self.dims = dims if columns is None else (dims[0], columns.stop - columns.start)


AHEAD = 7
LONG, SHORT = 10**11, 2 * 10**10


class Spread(Store):
    def __init__(self, dims, dtype, parts):
        self.shape, self.parts = shape(dims, dtype), parts


class Arriving:
    def __init__(self, ref, starts, waits, queue):
        self.ref, self.starts, self.waits, self.queue = ref, starts, waits, queue
        self.shape, self.place = ref.shape, len(queue)
        queue.append(self)

    def begin(self):
        for start in self.starts:
            start()
        self.starts = []

    def ready(self):
        if self.waits:
            for value in self.queue[: self.place + 1 + AHEAD]:
                value.begin()
            for copy in self.waits:
                copy.wait()
            self.waits = []
        return self.ref

    def __getitem__(self, index):
        return self.ready()[index]


class Leaving:
    def __init__(self, ref, target, sem):
        self.ref, self.target, self.sem, self.started = ref, target, sem, False
        self.copy = pltpu.make_async_copy(ref, target, sem)
        self.shape = ref.shape

    def ready(self):
        return self.ref

    def send_lanes(self, here):
        pltpu.make_async_copy(self.ref.at[:, here], self.target.at[:, here], self.sem).start()
        self.started = True

    def __getitem__(self, index):
        return self.ref[index]

    def __setitem__(self, index, value):
        self.ref[index] = value

    def send(self):
        if not self.started:
            self.copy.start()
        self.started = True


def placed(ref, index):
    return ref if index is None else ref.at[index]


def call(body, inputs, outs, vmem, name, scratch=(), aliases=(), near=False):
    arrays, in_specs, loads, copies, plan = [], [], [], 0, []
    for value in inputs:
        if isinstance(value, Load):
            plan.append(len(loads))
            loads.append(value)
            for i, piece in enumerate(value.pieces):
                arrived = i in value.arrived
                arrays.append(piece[0] if arrived else pltpu.with_memory_space_constraint(piece[0], pltpu.HBM))
                in_specs.append(ANYWHERE if arrived else FAR)
            copies += len(value.pieces)
        else:
            plan.append(None)
            pinned = near and value.dtype != jnp.int32
            arrays.append(pltpu.with_memory_space_constraint(value, pltpu.VMEM) if pinned else value)
            in_specs.append(SMEM if value.dtype == jnp.int32 else LOCAL)
    count = len(arrays)
    arrays += [pltpu.with_memory_space_constraint(value, pltpu.HBM) for value in aliases]
    in_specs += [FAR] * len(aliases)
    stores = [out for out in outs if isinstance(out, Store)]
    out_shape = [
        pltpu.HBM(out.shape.shape, out.shape.dtype)
        if isinstance(out, Store)
        else pltpu.VMEM(out.shape, out.dtype) if near else out
        for out in outs
    ]
    out_specs = [
        FAR if isinstance(out, Store) else LOCAL for out in outs
    ]
    own_scratch = [pltpu.VMEM(load.dims, load.dtype) for load in loads]
    homes_of = [
        [dims for dims, _ in store.parts] if isinstance(store, Spread) else [store.dims] for store in stores
    ]
    own_scratch += [pltpu.VMEM(dims, store.shape.dtype) for store, group in zip(stores, homes_of) for dims in group]
    copies += sum(len(group) for group in homes_of)
    sems = [pltpu.SemaphoreType.DMA((copies,))] if copies else []

    def kernel(*refs):
        ins, results = refs[:count], refs[len(arrays) : len(arrays) + len(outs)]
        rest = list(refs[len(arrays) + len(outs) :])
        homes, sem = rest[: len(own_scratch)], rest[len(own_scratch)] if sems else None
        extra = rest[len(own_scratch) + len(sems) :]
        given, queue, at, number = [], [], 0, 0
        for index in plan:
            if index is None:
                given.append(ins[at])
                at += 1
                continue
            load, home, starts, waits = loads[index], homes[index], [], []
            if isinstance(load, Choice):
                copies_of = [pltpu.make_async_copy(ins[at + i].at[load.rows, :], home, sem.at[number]) for i in (0, 1)]

                def start(copies_of=copies_of, holder=load.holder):
                    for i, copy in enumerate(copies_of):
                        pl.when((given[0][0] == holder) == (i == 0))(copy.start)

                starts, waits = [start], [copies_of[0]]
                at, number = at + 2, number + 2
            else:
                for _, source, target in load.pieces:
                    copy = pltpu.make_async_copy(
                        placed(ins[at], source and source(given[0])),
                        placed(home, target and target(given[0])),
                        sem.at[number],
                    )
                    starts.append(copy.start)
                    waits.append(copy)
                    at, number = at + 1, number + 1
            given.append(Arriving(home, starts, waits, queue))
        for value in queue[: 1 + AHEAD]:
            value.begin()
        leaving, made = [], []
        for out, result in zip(outs, results):
            if isinstance(out, Spread):
                group = []
                for _, place in out.parts:
                    home = homes[len(loads) + len(leaving)]
                    leaving.append(Leaving(home, result.at[place], sem.at[number]))
                    group.append(leaving[-1])
                    number += 1
                made.append(group)
            elif isinstance(out, Store):
                home = homes[len(loads) + len(leaving)]
                target = result if out.columns is None else result.at[:, out.columns]
                leaving.append(Leaving(home, target, sem.at[number]))
                made.append(leaving[-1])
                number += 1
            else:
                made.append(result)
        body(*given, *made, *extra)
        for value in queue:
            value.ready()
        for value in leaving:
            value.send()
        for value in leaving:
            value.copy.wait()

    results = [out.shape if isinstance(out, Store) else out for out in outs]
    moved = sum(value.size * value.dtype.itemsize for value in arrays + results)
    return pl.pallas_call(
        kernel,
        in_specs=in_specs,
        out_specs=out_specs,
        out_shape=out_shape,
        scratch_shapes=own_scratch + sems + list(scratch),
        input_output_aliases={count + i: i for i in range(len(aliases))},
        compiler_params=pltpu.CompilerParams(vmem_limit_bytes=vmem << 20),
        cost_estimate=pl.CostEstimate(flops=SHORT if near else LONG, bytes_accessed=moved, transcendentals=0),
        name=name,
    )(*arrays)


def joined_halves(pair, columns=slice(None)):
    half = pair[0].shape[0]
    pieces = []
    for array, mine in zip(pair, (True, False)):

        def into(core_ref, mine=mine):
            start = (core_ref[0] if mine else 1 - core_ref[0]) * half
            return (pl.ds(pl.multiple_of(start, half), half), slice(None))

        pieces.append((array, lambda core_ref: (slice(None), columns), into))
    start, stop, _ = columns.indices(pair[0].shape[1])
    return Load(pieces, (2 * half, stop - start), arrived=(1,))


def shape(dims, dtype):
    return jax.ShapeDtypeStruct(dims, dtype)


def rms_scale(values):
    return lax.rsqrt(jnp.mean(values * values, axis=-1, keepdims=True) + EPSILON)


def stack(core, own, other):
    return jnp.concatenate(
        [jnp.where(core == 0, own, other), jnp.where(core == 0, other, own)], axis=0
    )


def gain_row(core, own, other, index):
    own = own[index : index + 1, :].astype(F32)
    other = other[index : index + 1, :].astype(F32)
    return jnp.concatenate(
        [jnp.where(core == 0, own, other), jnp.where(core == 0, other, own)], axis=1
    )


def lanes(step, size):
    return pl.ds(pl.multiple_of(step * size, size), size)


def project_kernel(count, core_ref, gain_own, gain_other, x_ref, *refs):
    weights, outs = refs[:count], refs[count:]
    gain = gain_row(core_ref[0], gain_own[...], gain_other[...], 0)
    x = x_ref[...].astype(F32)
    outs[0][...] = (x * rms_scale(x) * gain).astype(BF)
    outs[0].send()
    normed = outs[0][...]
    for i in range(count):
        outs[1 + i][...] = mm(normed, weights[i][...], NN).astype(BF)
        outs[1 + i].send()


def project(core, x, gains, weights):
    count = len(weights)
    return call(
        functools.partial(project_kernel, count),
        [core, *gains, Load(x)] + [joined_halves(pair) for pair in weights],
        [Store(x.shape, BF) for _ in range(1 + count)],
        14 if x.shape[0] <= 512 else 48,
        "project",
    )


def split3(value):
    high = value.astype(BF).astype(F32)
    rest = value - high
    mid = rest.astype(BF).astype(F32)
    return high, mid, rest - mid


def key_extra(limit, rows):
    lane = lax.broadcasted_iota(jnp.int32, (rows, PAIR), 1) % HEAD_DIM
    row = lax.broadcasted_iota(jnp.int32, (rows, PAIR), 0)
    bias = jnp.where(row < limit, 0.0, DEAD)
    return jnp.where(lane < 3, 1.0, jnp.where(lane == 3, bias, 0.0)).astype(BF)


def block_of(step, rows):
    return pl.ds(pl.multiple_of(step * rows, rows), rows)


def place3(lane, base, parts, into):
    for i in (2, 1, 0):
        into = jnp.where(lane == base + i, parts[i], into)
    return into


def attend_block(limit, queries, bias_lane, keys, values, lane, earlier):
    rows = queries.shape[0]
    extra = key_extra(limit, rows)
    ones = jnp.ones((rows, PAIR), BF)
    results = []
    for head in range(2):
        mine = lane // HEAD_DIM == head
        scores = mm(jnp.where(mine, queries, bias_lane), jnp.where(mine, keys, extra), NT)
        top = jnp.max(scores, axis=-1, keepdims=True)
        if earlier is not None:
            top = jnp.maximum(top, earlier[head][1])
        weights = jnp.exp(scores - top).astype(BF)
        total = mm(weights, jnp.where(mine, values, ones), NN)
        if earlier is not None:
            total = total + earlier[head][0] * jnp.exp(earlier[head][1] - top)
        results.append((total, top))
    return results


def scaled_queries(q_ref, here):
    queries = q_ref[:, here] * jnp.asarray(HEAD_DIM**-0.5, BF)
    lane = lax.broadcasted_iota(jnp.int32, queries.shape, 1)
    return queries, jnp.where(lane % HEAD_DIM == 3, 1.0, 0.0).astype(BF), lane


def attend_own_kernel(limits_ref, q_ref, k_ref, v_ref, first_ref, second_ref, top_ref):
    top_ref[...] = jnp.zeros_like(top_ref.ref)
    for ref in (q_ref, k_ref, v_ref):
        ref.ready()

    @pl.loop(0, D // PAIR, unroll=2)
    def _(pair):
        here = lanes(pair, PAIR)
        queries, bias_lane, lane = scaled_queries(q_ref, here)
        heads = attend_block(limits_ref[0], queries, bias_lane, k_ref[:, here], v_ref[:, here], lane, None)
        first_ref[:, here], second_ref[:, here] = heads[0][0], heads[1][0]
        first_ref.send_lanes(here)
        second_ref.send_lanes(here)
        tops = top_ref[...]
        for head in range(2):
            tops = jnp.where(lane == 2 * pair + head, heads[head][1], tops)
        top_ref[...] = tops


def attend_own(limits, queries, keys, values):
    rows = queries.shape[0]
    return call(
        attend_own_kernel,
        [limits, Load(queries), Load(keys), Load(values)],
        [Store((rows, D), F32), Store((rows, D), F32), Store((rows, PAIR), F32)],
        16,
        "attend_own",
    )


def own_rows_kernel(core_ref, limits_ref, gain_own, gain_other, x_ref, wq, wk, wv, h1, q, k, v, *partial):
    project_kernel(3, core_ref, gain_own, gain_other, x_ref, wq, wk, wv, h1, q, k, v)
    attend_own_kernel(limits_ref, q, k, v, *partial)


def own_rows(core, limits, x, gains, weights):
    rows = x.shape[0]
    results = call(
        own_rows_kernel,
        [core, limits, *gains, Load(x)] + [joined_halves(pair) for pair in weights],
        [Store((rows, D), BF) for _ in range(4)]
        + [Store((rows, D), F32), Store((rows, D), F32), Store((rows, PAIR), F32)],
        22,
        "own_rows",
    )
    return results[:4], results[4:]


def attend_rest_kernel(limits_ref, q_ref, k_ref, v_ref, first_ref, second_ref, top_ref, wide_ref, low_ref, extra_ref):
    for ref in (q_ref, k_ref, v_ref, first_ref, second_ref, top_ref):
        ref.ready()
    rows = q_ref.shape[0]
    blocks = k_ref.shape[0] // rows

    @pl.loop(0, D // PAIR, unroll=2)
    def _(pair):
        here = lanes(pair, PAIR)
        queries, bias_lane, lane = scaled_queries(q_ref, here)
        tops = top_ref[...]
        heads = [
            (ref[:, here], jnp.sum(jnp.where(lane == 2 * pair + i, tops, 0.0), axis=-1, keepdims=True))
            for i, ref in enumerate((first_ref, second_ref))
        ]

        def more(block, heads):
            place = block_of(block, rows)
            return attend_block(
                limits_ref[1 + block], queries, bias_lane, k_ref[place, here], v_ref[place, here], lane, heads
            )

        heads = more(0, heads) if blocks == 1 else lax.fori_loop(0, blocks, more, heads)
        log_lanes = jnp.where(lane % HEAD_DIM == 3, 1.0, 0.0)
        outs = []
        for head, (total, top) in enumerate(heads):
            outs.append(total / pltpu.roll(total, HEAD_DIM, 1))
            log_lanes = place3(
                lane, HEAD_DIM * (1 - head), split3(-(top + jnp.log(total))), log_lanes
            )
        attended = jnp.where(lane < HEAD_DIM, outs[0], outs[1])
        wide_ref[:, here] = attended
        low_ref[:, here] = attended.astype(BF)
        extra_ref[:, here] = log_lanes.astype(BF)
        for ref in (wide_ref, low_ref, extra_ref):
            ref.send_lanes(here)


def attend_rest(limits, queries, keys, values, partial):
    rows = queries.shape[0]
    return call(
        attend_rest_kernel,
        [limits, Load(queries), Load(keys), Load(values)] + [Load(value) for value in partial],
        [Store((rows, D), F32), Store((rows, D), BF), Store((rows, D), BF)],
        18 if keys.shape[0] == rows else 40,
        "attend_rest",
    )


def attend_back_kernel(count, limits_ref, q_ref, dmb_ref, wo_ref, low_ref, wide_ref, extra_ref, *refs):
    inputs, outs = refs[:4], refs[4:]
    dq_ref, grad_refs, out_ref = outs[0], outs[1:5], outs[5]
    rows = q_ref.shape[0]
    scale = jnp.asarray(HEAD_DIM**-0.5, BF)
    lane = lax.broadcasted_iota(jnp.int32, (rows, PAIR), 1)
    none = jnp.zeros((rows, PAIR), BF)
    for ref in (q_ref, dmb_ref, low_ref, wide_ref, extra_ref, *inputs):
        ref.ready()

    @pl.loop(0, count)
    def _(pair):
        here = lanes(pair, PAIR)
        queries = q_ref[:, here] * scale
        dmb = dmb_ref[...]
        grads = mm(dmb, wo_ref[here, :], NT).astype(BF)
        out_ref[here, :] = mm(low_ref[:, here].T, dmb, NN).astype(BF)
        log_lanes = extra_ref[:, here]
        product = grads.astype(F32) * wide_ref[:, here]
        delta_lanes = jnp.zeros((rows, PAIR), F32)
        for head in range(2):
            mine = lane // HEAD_DIM == head
            delta = -jnp.sum(jnp.where(mine, product, 0.0), axis=-1, keepdims=True)
            delta_lanes = place3(lane, HEAD_DIM * (1 - head), split3(delta), delta_lanes)
        delta_lanes = delta_lanes.astype(BF)

        def over(limit, k_ref, v_ref, dk_ref, dv_ref, place):
            keys, values = k_ref[place, here], v_ref[place, here]
            extra = key_extra(limit, rows)
            keys_turned = (keys * scale).T
            dk = dv = 0.0
            dqs = []
            for head in range(2):
                mine = lane // HEAD_DIM == head
                probs = jnp.exp(
                    mm(jnp.where(mine, keys, extra), jnp.where(mine, queries, log_lanes), NT)
                )
                shifted = mm(
                    jnp.where(mine, values, extra), jnp.where(mine, grads, delta_lanes), NT
                )
                dscores = (probs * shifted).astype(BF)
                dv = dv + mm(probs.astype(BF), jnp.where(mine, grads, none), NN)
                dk = dk + mm(dscores, jnp.where(mine, queries, none), NN)
                dqs.append(mm(keys_turned[head * HEAD_DIM : (head + 1) * HEAD_DIM], dscores, NN))
            dk_ref[place, here] = dk.astype(BF)
            dv_ref[place, here] = dv.astype(BF)
            return jnp.concatenate(dqs, axis=0)

        k_own, k_rest, v_own, v_rest = inputs
        dk_own, dk_rest, dv_own, dv_rest = grad_refs
        dq = over(limits_ref[0], k_own, v_own, dk_own, dv_own, slice(None))
        blocks = k_rest.shape[0] // rows

        def more(block, dq):
            return dq + over(limits_ref[1 + block], k_rest, v_rest, dk_rest, dv_rest, block_of(block, rows))

        dq = more(0, dq) if blocks == 1 else lax.fori_loop(0, blocks, more, dq)
        dq_ref[:, here] = dq.T.astype(BF)
        for ref in (dq_ref, *grad_refs):
            ref.send_lanes(here)


def attend_back_inputs(queries, keys, values, dmb, wide, low, extra, out_weight, first, count):
    columns = slice(first * PAIR, (first + count) * PAIR)
    half = D // PAIR // 2

    def part(value):
        dims = (value.shape[0], columns.stop - columns.start)
        return Load([(value, lambda core_ref: (slice(None), columns), None)], dims)

    rows_of = [
        Choice(out_weight, pair // half, slice(pair % half * PAIR, (pair % half + 1) * PAIR))
        for pair in range(first, first + count)
    ]
    loads = [part(queries), Load(dmb)] + rows_of + [part(low), part(wide), part(extra)]
    return loads + [part(value) for value in (keys[0], values[0], keys[1], values[1])], columns


def attend_back_body(count, core_ref, limits_ref, refs, turned_wo):
    q_ref, dmb_ref, wo_refs, rest = refs[0], refs[1], refs[2 : 2 + count], refs[2 + count :]
    for i, ref in enumerate(wo_refs):
        turned_wo[i * PAIR : (i + 1) * PAIR, :] = ref[...]
    low_ref, wide_ref, extra_ref, k_own, v_own, k_rest, v_rest = rest[:7]
    attend_back_kernel(
        count, limits_ref, q_ref, dmb_ref, turned_wo, low_ref, wide_ref, extra_ref, k_own, k_rest, v_own, v_rest, *rest[7:]
    )


def attend_back(core, limits, queries, keys, values, dmb, wide, low, extra, out_weight, first, count, earlier):
    rows, rest = queries.shape[0], keys[1].shape[0]
    loads, columns = attend_back_inputs(queries, keys, values, dmb, wide, low, extra, out_weight, first, count)

    def body(core_ref, limits_ref, *refs):
        attend_back_body(count, core_ref, limits_ref, refs[:-1], refs[-1])

    return call(
        body,
        [core, limits] + loads,
        [Store((size, D), BF, columns) for size in (rows, rows, rest, rows, rest)]
        + [Store((columns.stop - columns.start, D), BF)],
        20 if rest == rows else 48,
        "attend_back",
        [pltpu.VMEM((count * PAIR, D), BF)],
        aliases=earlier,
    )


CURVE = 0.7978845608028654
CUBIC = 0.044715


def ffn_part(part, core, step, h2_ref, turned, dyb, dyb_turned, weights, own_ref, other_ref, acc_out, acc_back):
    wide, half = own_ref.shape[1] // 2, D // 2
    here, there = lanes(step, wide), lanes(part + 2 * step, wide)
    gate_ref, up_ref, down_ref = weights
    rows = block_of(part + 2 * step, wide)
    gate = mm(h2_ref[...], gate_ref[:, there], NN)
    up = mm(h2_ref[...], up_ref[:, there], NN)
    dn = mm(dyb[...], down_ref[rows, :], NT)
    square = gate * gate
    bent = jnp.tanh(CURVE * gate * (1.0 + CUBIC * square))
    rise = 0.5 * (1.0 + bent)
    bulge = gate * rise
    slope = rise + 0.5 * gate * (1.0 - bent * bent) * (CURVE * (1.0 + 3.0 * CUBIC * square))
    hidden = (bulge * up).astype(BF)
    dgate = (dn * up * slope).astype(BF)
    dup = (dn * bulge).astype(BF)
    ddown = mm(dyb_turned[...], hidden, NN).astype(BF)

    @pl.when(step == core)
    def _():
        own_ref[2 * half :, :wide] = ddown[:half]
        own_ref[2 * half :, wide:] = ddown[half:]

    @pl.when(step != core)
    def _():
        other_ref[2 * half :, :wide] = ddown[:half]
        other_ref[2 * half :, wide:] = ddown[half:]

    dgate_term = mm(turned[...], dgate, NN).astype(BF)
    dup_term = mm(turned[...], dup, NN).astype(BF)
    for i, term in ((0, dgate_term), (1, dup_term)):
        place = slice(i * half, (i + 1) * half)
        own_ref[place, here] = jnp.where(core == 0, term[:half], term[half:])
        other_ref[place, here] = jnp.where(core == 0, term[half:], term[:half])
    acc_back[...] += mm(dgate, gate_ref[:, there], NT) + mm(dup, up_ref[:, there], NT)
    acc_out[...] += mm(hidden, down_ref[rows, :], NN)


def live_grad(limits_ref, grad_ref):
    rows = grad_ref.shape[0]
    live = lax.broadcasted_iota(jnp.int32, (rows, D), 0) < limits_ref[0]
    return jnp.where(live, grad_ref[...].astype(F32), 0.0)


def ffn_body(core_ref, limits_ref, gain_own, gain_other, a_ref, wo_ref, x_ref, grad_ref, weights, outs, scratch, m_ref, acc_out):
    core = core_ref[0]
    output_ref, dm_ref, dmb_ref, *grads = outs
    h2_ref, turned, dyb, dyb_turned = scratch
    acc_back = dm_ref.ref
    m = mm(a_ref[...], wo_ref[...], NN) + x_ref[...].astype(F32)
    gain = gain_row(core, gain_own[...], gain_other[...], 1)
    m_ref[...] = m
    h2 = (m * rms_scale(m) * gain).astype(BF)
    h2_ref[...] = h2
    turned[...] = h2.T
    low = live_grad(limits_ref, grad_ref).astype(BF)
    dyb[...] = low
    dyb_turned[...] = low.T
    acc_out[...] = jnp.zeros_like(acc_out)
    acc_back[...] = jnp.zeros_like(acc_back)
    for ref in weights:
        ref.ready()
    for part in range(2):

        @pl.loop(0, 2)
        def _(step):
            ffn_part(
                part, core, step, h2_ref, turned, dyb, dyb_turned, weights, *grads[2 * part : 2 * part + 2], acc_out, acc_back
            )

        grads[2 * part + 1].send()
        grads[2 * part].send()
    m = m_ref[...]
    scale = rms_scale(m)
    scaled = acc_back[...] * gain
    dm = dyb[...].astype(F32) + scale * scaled - m * (scale * scale * scale) * jnp.mean(
        scaled * m, axis=-1, keepdims=True
    )
    dmb_ref[...] = dm.astype(BF)
    dmb_ref.send()
    dm_ref[...] = dm
    dm_ref.send()
    output_ref[...] = (m + acc_out[...]).astype(BF)


def ffn_results(rows, hidden):
    outs = [Store((rows, D), BF), Store((rows, D), F32), Store((rows, D), BF)]
    scratch = [pltpu.VMEM((rows, D), BF), pltpu.VMEM((D, rows), BF), pltpu.VMEM((rows, D), BF), pltpu.VMEM((D, rows), BF)]
    return outs + [Store((3 * D // 2, hidden // 2), BF) for _ in range(4)], scratch


def feed_forward(core, limits, x, attended, out_weight, gains, grad, weights):
    rows, hidden = x.shape[0], weights[0][0].shape[1]
    outs, scratch = ffn_results(rows, hidden)

    def body(core_ref, limits_ref, gain_own, gain_other, a, wo, x, grad, *refs):
        ffn_body(core_ref, limits_ref, gain_own, gain_other, a, wo, x, grad, refs[:3], refs[3:10], refs[10:14], *refs[14:])

    return call(
        body,
        [core, limits, *gains, Load(attended), joined_halves(out_weight), Load(x), Load(grad)]
        + [joined_halves(pair) for pair in weights],
        outs,
        52,
        "feed_forward",
        scratch + [pltpu.VMEM((rows, D), F32)] * 2,
    )


def middle_kernel(core_ref, limits_ref, gain_own, gain_other, x_rest, wk, wv, q, first, second, top, wo, x, grad, *refs):
    weights, outs = refs[:3], refs[3:]
    h1_rest, k_rest, v_rest, wide, low, extra = outs[:6]
    project_kernel(2, core_ref, gain_own, gain_other, x_rest, wk, wv, h1_rest, k_rest, v_rest)
    for ref in (q, first, second, top, wo, x, grad, *weights):
        ref.begin()
    attend_rest_kernel(limits_ref, q, k_rest, v_rest, first, second, top, wide, low, extra)
    ffn_body(
        core_ref, limits_ref, gain_own, gain_other, low, wo, x, grad, weights, outs[6:13], outs[13:], first.ref, second.ref
    )


def middle(core, limits, gains, x, x_rest, key_value, queries, partial, out_weight, grad, weights):
    rows, hidden = x.shape[0], weights[0][0].shape[1]
    low, full = ((rows, D), BF), ((rows, D), F32)
    ffn_outs, scratch = ffn_results(rows, hidden)
    results = call(
        middle_kernel,
        [core, limits, *gains, x_rest]
        + [joined_halves(pair) for pair in key_value]
        + [Load(queries)]
        + [Load(value) for value in partial]
        + [joined_halves(out_weight), Load(x), Load(grad)]
        + [joined_halves(pair) for pair in weights],
        [Store(*dims) for dims in (low, low, low, full, low, low)] + ffn_outs,
        49,
        "middle",
        scratch,
    )
    return results[:3], results[3:6], results[6:]


def project_grads_kernel(core_ref, own_normed, dq_ref, rest_normed, dk_own, dk_rest, dv_own, dv_rest, *refs):
    core = core_ref[0]
    out_terms, (own_ref, other_ref) = refs[:-2], refs[-2:]
    half = D // 2

    def put(i, term):
        own_ref[i * half : (i + 1) * half, :] = jnp.where(core == 0, term[:half], term[half:])
        other_ref[i * half : (i + 1) * half, :] = jnp.where(core == 0, term[half:], term[:half])

    turned = own_normed[...].T
    put(0, mm(turned, dq_ref[...], NN).astype(BF))
    turned_rest = rest_normed[...].T
    put(1, (mm(turned, dk_own[...], NN) + mm(turned_rest, dk_rest[...], NN)).astype(BF))
    put(2, (mm(turned, dv_own[...], NN) + mm(turned_rest, dv_rest[...], NN)).astype(BF))
    put(3, jnp.concatenate([term[...] for term in out_terms], axis=0))


def project_grads(core, normed, dq, dks, dvs, out_terms):
    total = dks[0].shape[0] + dks[1].shape[0]
    arrays = (normed[0], dq, normed[1], *dks, *dvs, *out_terms)
    return call(
        project_grads_kernel,
        [core] + [Load(value) for value in arrays],
        [Store((2 * D, D), BF) for _ in range(2)],
        18 if total <= 1024 else 54,
        "project_grads",
    )


def last_piece(core, limits, queries, keys, values, dmb, wide, low, extra, out_weight, first, count, earlier, out_terms, normed):
    rows, rest = queries.shape[0], keys[1].shape[0]
    loads, columns = attend_back_inputs(queries, keys, values, dmb, wide, low, extra, out_weight, first, count)
    done = slice(0, columns.start)
    inputs = len(loads)

    def before(value):
        return Load([(value, lambda core_ref: (slice(None), done), None)], (value.shape[0], done.stop))

    more = [Load(normed[0]), before(earlier[0]), Load(normed[1])]
    more += [before(value) for value in earlier[1:]] + [Load(term) for term in out_terms]

    def body(core_ref, limits_ref, *refs):
        ins, given, outs, wo, out_term = refs[:inputs], refs[inputs : inputs + len(more)], refs[-9:-4], refs[-2], refs[-1]
        own_ref, other_ref = refs[-4:-2]
        attend_back_body(count, core_ref, limits_ref, (*ins, *outs, out_term), wo)

        def both_parts(left, right):
            return jnp.concatenate([left[...], right[...]], axis=1)

        merged = [both_parts(left, right) for left, right in zip((given[1], *given[3:7]), outs)]
        project_grads_kernel(
            core_ref, given[0], merged[0], given[2], *merged[1:], *given[7:], out_term, own_ref, other_ref
        )

    width = columns.stop - columns.start
    return call(
        body,
        [core, limits] + loads + more,
        [Store((size, width), BF) for size in (rows, rows, rest, rows, rest)] + [Store((2 * D, D), BF) for _ in range(2)],
        36,
        "last_piece",
        [pltpu.VMEM((count * PAIR, D), BF)] * 2,
    )


def project_back_kernel(core_ref, dk_rest, key, dv_rest, value, dq_ref, query, dk_own, dv_own, rest_ref, own_ref):
    rows = dq_ref.shape[0]
    for ref in (dk_rest, key, dv_rest, value):
        ref.ready()

    def rest(block, _):
        place = block_of(block, rows)
        back = mm(dk_rest[place, :], key[...], NT) + mm(dv_rest[place, :], value[...], NT)
        rest_ref[place, :] = back.astype(BF)
        return _

    blocks = dk_rest.shape[0] // rows
    rest(0, 0) if blocks == 1 else lax.fori_loop(0, blocks, rest, 0)
    rest_ref.send()
    own_ref[...] = (
        mm(dq_ref[...], query[...], NT) + mm(dk_own[...], key[...], NT) + mm(dv_own[...], value[...], NT)
    )


def project_back(core, dq, dks, dvs, weights):
    query, key, value = (joined_halves(pair) for pair in weights)
    total = dks[0][0].shape[0] + dks[1][0].shape[0]

    def side_by_side(parts):
        pieces, start = [], 0
        for i, part in enumerate(parts):
            width = D - start if i == len(parts) - 1 else D - parts[-1].shape[1]
            columns = slice(start, start + width)
            take = None if part.shape[1] == width else (lambda core_ref, columns=columns: (slice(None), columns))
            pieces.append((part, take, lambda core_ref, columns=columns: (slice(None), columns)))
            start += width
        return Load(pieces, (parts[0].shape[0], D))

    dq_load, (dk_own, dk_rest), (dv_own, dv_rest) = side_by_side(dq), map(side_by_side, dks), map(side_by_side, dvs)
    return call(
        project_back_kernel,
        [core, dk_rest, key, dv_rest, value, dq_load, query, dk_own, dv_own],
        [Store((total - dq[0].shape[0], D), BF), Store((dq[0].shape[0], D), F32)],
        20 if total <= 1024 else 40,
        "project_back",
    )


def input_grad_kernel(core_ref, gain_own, gain_other, x_ref, dm_ref, own_ref, *refs):
    x = x_ref[...].astype(F32)
    scale = rms_scale(x)
    back = own_ref[...]
    for ref in refs[:-1]:
        back = back + ref[...].astype(F32)
    scaled = back * gain_row(core_ref[0], gain_own[...], gain_other[...], 0)
    refs[-1][...] = (
        dm_ref[...]
        + scale * scaled
        - x * (scale * scale * scale) * jnp.mean(scaled * x, axis=-1, keepdims=True)
    ).astype(BF)


def input_grad_of(core, gains, x, dm, own, received):
    return call(
        input_grad_kernel,
        [core, *gains] + [Load(value) for value in (x, dm, own)] + [Load(value, arrived=(0,)) for value in received],
        [Store(x.shape, BF)],
        14 if len(received) == 1 else 24,
        "input_grad",
    )[0]


def swap(value, axis, mask):
    count = lax.axis_size(axis)
    return lax.ppermute(value, axis, [(i, i ^ mask) for i in range(count)])


def tie(values, *earlier):
    return lax.optimization_barrier((values, earlier))[0]


def fold_kernel(count, bits_ref, *refs):
    outs = refs[2 * count :]
    for i in range(count):
        own, got = refs[2 * i], refs[2 * i + 1]
        half = own.shape[0] // 2
        for j, bit in ((0, bits_ref[i]), (1, 1 - bits_ref[i])):
            here = pl.ds(pl.multiple_of(bit * half, 16), half)
            outs[2 * i + j][...] = (own[here, :].astype(F32) + got[here, :].astype(F32)).astype(BF)


def paired(owns, gots):
    return [part for pair in zip(owns, gots) for part in pair]


def fold(bits, owns, gots):
    outs = [shape((own.shape[0] // 2, own.shape[1]), BF) for own in owns for _ in range(2)]
    results = call(
        functools.partial(fold_kernel, len(owns)),
        [bits] + paired(owns, gots),
        outs,
        3,
        "fold",
        near=True,
    )
    return results[0::2], results[1::2]


def fold_far(bits, own, got):
    rows, cols = own.shape
    half, parts = rows // 2, 3
    size = half // parts
    inputs = []
    for i in range(2 * parts):
        for value in (own, got):

            def here(bits_ref, i=i):
                bit = bits_ref[0] if i < parts else 1 - bits_ref[0]
                return (pl.ds(pl.multiple_of(bit * half + i % parts * size, 16), size), slice(None))

            inputs.append(Load([(value, here, None)], (size, cols), arrived=(0,) if value is got else ()))

    def body(bits_ref, *refs):
        ins, (sent, kept) = refs[:-2], refs[-2:]
        for i in range(2 * parts):
            out = kept if i < parts else sent
            place = slice(i % parts * size, (i % parts + 1) * size)
            out[place, :] = (ins[2 * i][...].astype(F32) + ins[2 * i + 1][...].astype(F32)).astype(BF)

    sent, kept = call(
        body, [bits] + inputs, [shape((half, cols), BF)] * 2, 14, "fold_far"
    )
    return [kept], [sent]


def add_kernel(count, *refs):
    for i in range(count):
        refs[2 * count + i][...] = (
            refs[2 * i][...].astype(F32) + refs[2 * i + 1][...].astype(F32)
        ).astype(BF)


def add(owns, gots):
    return call(
        functools.partial(add_kernel, len(owns)),
        paired(owns, gots),
        [shape(own.shape, BF) for own in owns],
        3,
        "add",
        near=True,
    )


def merge_kernel(count, bits_ref, *refs):
    for i in range(count):
        refs[2 * count + i][...] = stack(bits_ref[i], refs[2 * i][...], refs[2 * i + 1][...])


def merge(bits, owns, gots):
    return call(
        functools.partial(merge_kernel, len(owns)),
        [bits] + paired(owns, gots),
        [shape((2 * own.shape[0], own.shape[1]), BF) for own in owns],
        3,
        "merge",
        near=True,
    )


class Chain:
    def __init__(self, orders, owns, others):
        sizes = [lax.axis_size(axis) for axis in ("grp", "ctx", "wsh")]
        total = sizes[0] * sizes[1] * sizes[2]
        near = [2, 2 * sizes[1], 4 * sizes[1]]
        self.far, mask = [], 2
        while mask < total:
            if mask not in near:
                self.far.append(mask)
            mask *= 2
        here = (lax.axis_index("grp") * sizes[1] + lax.axis_index("ctx")) * 2 + lax.axis_index("wsh")
        self.total, self.near, self.orders = total, near, orders
        self.bits = []
        for stage in range(3):
            row = []
            for order in orders:
                one, two = near[order[0][stage]], near[order[1][stage]]
                mask = jnp.where(lax.axis_index("wsh") == 0, one, two)
                row.append((here // mask) % 2)
            self.bits.append(jnp.stack(row).astype(jnp.int32))
        self.count = 0
        self.kept = list(owns)
        self.got = [self.send(value, (1, 1)) for value in others]

    def send(self, value, masks):
        pairs = [(i, i ^ masks[i % 2]) for i in range(self.total)]
        return lax.ppermute(value, ("grp", "ctx", "wsh"), pairs)

    def send_near(self, values, stage):
        return [
            self.send(value, (self.near[order[0][stage]], self.near[order[1][stage]]))
            for value, order in zip(values, self.orders)
        ]

    def stages(self):
        return 3 + 1 + len(self.far) + 2

    def step(self, *earlier):
        stage, far = self.count, len(self.far)
        self.count += 1
        kept, got = tie((self.kept, self.got), *earlier)
        if stage < 3:
            far_away = stage == 0 and len(kept) == 1 and kept[0].shape[0] % 96 == 0
            self.kept, sent = fold_far(self.bits[0], kept[0], got[0]) if far_away else fold(self.bits[stage], kept, got)
            self.got = self.send_near(sent, stage)
            return sent
        if stage <= 3 + far:
            self.kept = add(kept, got)
            if stage < 3 + far:
                mask = self.far[stage - 3]
                self.got = [self.send(value, (mask, mask)) for value in self.kept]
            else:
                self.got = self.send_near(self.kept, 2)
            return self.kept
        back = 2 - (stage - 4 - far)
        self.kept = merge(self.bits[back], kept, got)
        self.got = self.send_near(self.kept, back - 1)
        return self.kept


def over_gain(total, gain):
    column = jnp.broadcast_to(jnp.sum(total, axis=1, keepdims=True), (total.shape[0], PAIR))
    return column.T[:1, :] / gain.astype(F32)


def ffn_finish(bits, gain, gate, up, part, chain, earlier, before):
    half, hidden = gate.shape
    wide = hidden // 4
    columns = [slice((part + 2 * j) * wide, (part + 2 * j + 1) * wide) for j in range(2)]

    def of(value):
        pieces = [
            (value, lambda bits_ref, c=c: (slice(None), c), lambda bits_ref, j=j: (slice(None), slice(j * wide, (j + 1) * wide)))
            for j, c in enumerate(columns)
        ]
        return Load(pieces, (half, 2 * wide))

    def body(bits_ref, gain_ref, kept, got, gate_ref, up_ref, *refs):
        dgate, dup, (ddown,), gain_out = refs[-4:]
        value = stack(bits_ref[0], kept[...], got[...])
        total = refs[0][...] if before else jnp.zeros((half, PAIR), F32)
        for i, (weight, outs) in enumerate(((gate_ref, dgate), (up_ref, dup))):
            term = value[i * half : (i + 1) * half].astype(F32)
            for j in range(2):
                outs[j][...] = term[:, j * wide : (j + 1) * wide]
                outs[j].send()
            product = term * weight[...].astype(F32)
            total = total + sum(product[:, k : k + PAIR] for k in range(0, 2 * wide, PAIR))
        for j in range(2):
            piece = value[2 * half :, j * wide : (j + 1) * wide]
            ddown[:, j * half : (j + 1) * half] = piece.T.astype(F32)
        gain_out[...] = over_gain(total, gain_ref[...]) if before else total

    kept, got = tie((chain.kept[0], chain.got[0]), earlier)
    wide_parts = [((half, wide), (slice(None), c)) for c in columns]
    down_part = [((wide, D), (slice(part * wide, (part + 1) * wide), slice(None)))]
    return call(
        body,
        [bits, gain, Load(kept, arrived=(0,)), Load(got, arrived=(0,)), of(gate), of(up)] + list(before[3:]),
        [Spread((half, hidden), F32, wide_parts) for _ in range(2)]
        + [Spread((2 * wide, D), F32, down_part), shape((1, half) if before else (half, PAIR), F32)],
        24,
        "ffn_finish",
        aliases=before[:3],
    )


def attention_finish_kernel(bits_ref, gain_ref, *refs):
    streams = len(refs) // 2 - 4
    weights, outs = refs[:3], refs[3 + 2 * streams :]
    value = jnp.concatenate(
        [stack(bits_ref[i], refs[3 + 2 * i][...], refs[4 + 2 * i][...]) for i in range(streams)], axis=0
    )
    half = D // 2
    total = jnp.zeros((half, PAIR), F32)
    for i in range(4):
        piece = value[i * half : (i + 1) * half].astype(F32)
        outs[i][...] = piece
        outs[i].send()
        if i < 3:
            product = piece * weights[i][...].astype(F32)
            total = total + sum(product[:, k : k + PAIR] for k in range(0, D, PAIR))
    outs[4][...] = over_gain(total, gain_ref[...])


def attention_finish(bits, gain, weights, chain):
    half = D // 2
    return call(
        attention_finish_kernel,
        [bits, gain]
        + [Load(value) for value in weights]
        + [Load(value, arrived=(0,)) for value in paired(chain.kept, chain.got)],
        [Store((half, D), F32)] * 4 + [shape((1, half), F32)],
        20,
        "attention_finish",
    )


ORDER = (1, 2, 3, "back", 1, 2, 1, 3, 2, "send", 1, 3, 2, 1, 3, 2, 1, 3, 2, 3, "input", "early", 3, "late")
AXES = (((0, 1, 2), (1, 0, 2)), ((2, 1, 0), (0, 2, 1)), ((0, 1, 2), (1, 2, 0)))
EARLY = ((1, (1, 2)),)


def on_device(
    tokens,
    lengths,
    query_weight,
    key_weight,
    value_weight,
    output_weight,
    gate_weight,
    up_weight,
    down_weight,
    attn_gain,
    ffn_gain,
    out_grad,
):
    blocks = lax.axis_size("ctx")
    x, grad = tokens[0], out_grad[0]
    rows = x.shape[0]
    place = lax.axis_index("ctx")
    core = lax.axis_index("wsh").astype(jnp.int32)[None]
    limits = jnp.clip(
        lengths[0] - rows * jnp.stack([place ^ r for r in range(blocks)]).astype(jnp.int32), 0, rows
    )

    def both(own):
        return (own, swap(own, "wsh", 1))

    wq, wk, wv = both(query_weight), both(key_weight), both(value_weight)
    gains = both(jnp.stack([attn_gain, ffn_gain]))
    others = [swap(x, "ctx", r) for r in range(1, blocks)]
    x_rest = others[0] if blocks == 2 else jnp.concatenate(others, axis=0)
    if blocks == 2:
        (h1, queries, key, value), partial = own_rows(core, limits, x, gains, [wq, wk, wv])
    else:
        h1, queries, key, value = project(core, x, gains, [wq, wk, wv])
        partial = attend_own(limits, queries, key, value)
    wo, wg, wu, wd = (
        both(tie(weight, wv[1])) for weight in (output_weight, gate_weight, up_weight, down_weight)
    )
    ffn_weights = (wg, wu, wd)
    if blocks == 2:
        rest, (wide, low, extra), results = middle(
            core, limits, gains, x, x_rest, [wk, wv], queries, partial, wo, grad, ffn_weights
        )
    else:
        rest = project(core, x_rest, gains, [wk, wv])
        wide, low, extra = attend_rest(limits, queries, *rest[1:], partial)
        results = feed_forward(core, limits, x, low, wo, gains, grad, ffn_weights)
    output, dm, dmb, *sums = results
    normed, keys, values = (h1, rest[0]), (key, rest[1]), (value, rest[2])
    first = Chain([AXES[0]], sums[:1], sums[1:2])
    second = Chain([AXES[1]], sums[2:3], sums[3:4])
    arrays = (core, limits, queries, keys, values)
    most, out_terms, token, first_pair = (), [], None, 0
    for count, steps in EARLY:
        ready = dmb if token is None else tie(dmb, token)
        *most, out_term = attend_back(*arrays, ready, wide, low, extra, wo, first_pair, count, most)
        out_terms.append(out_term)
        first_pair, token = first_pair + count, out_term
        for name in steps:
            token = (first, second)[name - 1].step(token)
    arrays += (tie(dmb, token), wide, low, extra, wo, first_pair, D // PAIR - first_pair)
    if blocks == 2:
        *final, own, other = last_piece(*arrays, most, out_terms, normed)
        grads = list(zip(most, final))
    else:
        *most, last_term = attend_back(*arrays, most)
        own, other = project_grads(core, normed, most[0], most[1:3], most[3:5], [*out_terms, last_term])
        grads = [(value,) for value in most]
    dq, dks, dvs = grads[0], grads[1:3], grads[3:5]
    third = Chain([AXES[2]], [own], [other])
    token = own
    received, chains, hidden = [], (first, second, third), ()
    for name in ORDER:
        if name == "back":
            back_rest, back_own = project_back(core, tie(dq, token), dks, dvs, [wq, wk, wv])
            token = back_own
        elif name == "send":
            sent = tie(back_rest, token)
            received = [
                swap(sent[(r - 1) * rows : r * rows] if blocks > 2 else sent, "ctx", r)
                for r in range(1, blocks)
            ]
        elif name == "input":
            token = input_grad = input_grad_of(core, gains, x, dm, tie(back_own, token), received)
        elif name in ("early", "late"):
            part = int(name == "late")
            chain = (first, second)[part]
            hidden = ffn_finish(
                chain.bits[0], ffn_gain[None], gate_weight, up_weight, part, chain, token, hidden
            )
            token = hidden[3]
        else:
            chain = chains[name - 1]
            for _ in range(1 + (len(chain.far) - 1) * (chain.count == 4)):
                token = chain.step(token)
    dquery, dkey, dvalue, dout, dgain_attn = attention_finish(
        third.bits[0], attn_gain[None], [query_weight, key_weight, value_weight], third
    )
    return (
        output[None],
        input_grad[None],
        dquery,
        dkey,
        dvalue,
        dout,
        *hidden[:3],
        dgain_attn.reshape(D // 2),
        hidden[3].reshape(D // 2),
    )


def solution(mesh):
    rows, weights, vector = P(("grp", "wsh"), "ctx", None), P("wsh", None), P("wsh")
    in_specs = (rows, P(("grp", "wsh"))) + (weights,) * 7 + (vector,) * 2 + (rows,)
    out_specs = (rows,) * 2 + (weights,) * 7 + (vector,) * 2
    return jax.shard_map(
        on_device, mesh=mesh, in_specs=in_specs, out_specs=out_specs, check_vma=False
    )
```
